32 devices in a mesh: inline: 2 (over x), xline: 8 (over z, core), particle: 2 (over y).
Axes of the slice: x: 2, y: 2, z: 4, core: 2. Of those that a mesh axis runs over, the one named last changes fastest.
Arguments:
- velocity: float32 [2, 16, 192, 128], P('particle', 'inline', 'xline'), may hold values from 0.04 to 0.18, as said below
- state_now: float32 [2, 16, 192, 128], P('particle', 'inline', 'xline'), may hold values from -6 to 6
- state_prev: float32 [2, 16, 192, 128], P('particle', 'inline', 'xline'), may hold values from -6 to 6
- observed: float32 [1024, 32], P(('inline', 'xline')), may hold values from -6 to 6
- rec_cell: int32 [1024], P(('inline', 'xline')), may hold values from 0 to 24575
- rec_gather: int32 [1024, 1], P(('inline', 'xline')), may hold values from 0 to 7; in each aligned block of 64 rows (0 to 63, 64 to 127, ...) at most 16 rows name the same one
Outputs:
- update: float32 [2, 16, 192, 128], P('particle', 'inline', 'xline')
The draws below stay inside these ranges and needn't reach their ends.
Inputs may be any that keep to these rules, and one draw needn't show every extreme that they name: `velocity`: values lie between the ends of the range everywhere. `rec_cell`: a flat cell number within the block of 8 x 24 x 128 cells of the device that holds the receiver. `rec_gather`: among the rows of one device no gather is named more than 16 times, and some device names some gather exactly 16 times.
All inputs are finite; a program needn't handle non-finite values.
Results may differ from the reference program's by a relative error of at most 0.0003.
Values sent between devices are 32-bit elements; how exact they have to be, the bound alone decides.
A program may use at most 64 MiB of HBM per device.

```python
import math
import jax
import jax.numpy as jnp
import numpy as np
from jax import lax

CX = 8
CY = 24
NZ = 128
NT = 32
REC_DEV = 64
CAP = 16
TAPS = 8
PARTICLES = 2
NX = 16
NY = 192
NRECV = 1024
N_INLINE = 2
N_XLINE = 8


def draw_velocity(key, part):
    along_x = jnp.arange(NX, dtype=jnp.float32)[:, None, None] / NX
    along_y = jnp.arange(NY, dtype=jnp.float32)[None, :, None] / NY
    spread = (1.0 + along_x + along_y) / 3.0
    sample = jax.random.uniform(key, (PARTICLES, NX, NY, NZ), jnp.float32)
    return 0.11 + 0.07 * spread[None] * (2.0 * sample - 1.0)


def set_ends(entries, rng, smallest, top_value):
    longest = entries.shape.index(max(entries.shape))
    spots = []
    for shift in (0, 1):
        where = [jax.random.randint(jax.random.fold_in(rng, axis), (), 0, length) for axis, length in enumerate(entries.shape)]
        where[longest] = (where[longest] + shift) % entries.shape[longest]
        spots.append(tuple(where))
    return entries.at[spots[0]].set(smallest).at[spots[1]].set(top_value)


def shard_levels(stream_key, dims, cuts, low, largest):
    def one(position, blocks):
        heights = jax.random.uniform(jax.random.fold_in(jax.random.fold_in(stream_key, 6), position), (blocks,), jnp.float32, low / len(cuts), largest / len(cuts))
        return jnp.repeat(jnp.exp(heights), dims[position] // blocks).reshape((-1,) + (1,) * (len(dims) - position - 1))

    loudness = one(*cuts[0])
    for cut in cuts[1:]:
        loudness = loudness * one(*cut)
    return loudness


def assign_block(key, own, number, rows, count, top, limit, skew):
    ranking = jax.random.permutation(key, count)
    heavy_load, ordinary = portions_of(count, rows * top, limit, skew, True), portions_of(count, rows * top, limit, skew, False)
    places = jnp.arange(count)

    def named(sizes, rotation):
        used = int((sizes > 0).sum())
        fixed = max(1, used // 4)
        moved = fixed + (places - fixed + rotation * (used - fixed)) % max(1, count - fixed)
        return jnp.zeros((count,), jnp.int32).at[ranking[jnp.where(places < fixed, places, moved)]].set(jnp.asarray(sizes, jnp.int32))

    sizes = jnp.where(number % 4 == 0, named(heavy_load, number // 4), named(ordinary, number - number // 4 - 1))
    mixed = jax.random.permutation(jax.random.fold_in(own, 3), count)
    donor, receiver = mixed[0:count // 2 * 2:2], mixed[1:count // 2 * 2:2]
    margin = jnp.minimum(sizes[donor] - 1, limit - sizes[receiver]) // 2
    margin = jnp.where((donor == ranking[0]) | (receiver == ranking[0]) | (sizes[receiver] == 0), 0, jnp.maximum(margin, 0))
    moved = jax.random.randint(jax.random.fold_in(own, 4), (count // 2,), 0, 1 << 20) % (margin + 1)
    sizes = sizes.at[donor].add(-moved).at[receiver].add(moved)
    members = jnp.searchsorted(jnp.cumsum(sizes), jnp.arange(rows * top), side="right").astype(jnp.int32)
    table = members.reshape(top, rows).T
    table = table[jax.random.permutation(jax.random.fold_in(own, 1), rows)]
    rotation = jax.random.randint(jax.random.fold_in(own, 2), (rows, 1), 0, top)
    return jnp.take_along_axis(table, (jnp.arange(top)[None, :] + rotation) % top, axis=1)


def portions_of(number_of, total, reach, slope, full):
    loads = [(1 << 20) // math.isqrt(standing ** slope) + 1 for standing in range(1, number_of + 1)]
    largest = reach if full else min(reach, max(-(-total // number_of), total * loads[0] // sum(loads)))
    least = 1 if total - largest >= number_of - 1 else 0
    given, spare = [largest] + [least] * (number_of - 1), total - largest - least * (number_of - 1)
    while spare > 0:
        candidates = [i for i in range(1, number_of) if given[i] < largest] or [i for i in range(1, number_of) if given[i] < reach]
        pool, left = sum([loads[i] for i in candidates]), spare
        for i in candidates:
            extra = min(reach - given[i], max(1, left * loads[i] // pool), spare)
            given[i] = given[i] + extra
            spare = spare - extra
    return np.array(given)


def normal_values(rng, dims, scale, most, pieces=(), kind=jnp.bfloat16):
    drawn = scale * jax.random.normal(rng, dims, jnp.float32)
    if pieces:
        drawn = drawn * shard_levels(rng, dims, pieces, -0.22, 0.18)
    return jnp.clip(drawn, -most, most).astype(kind)


def setup_inputs(seed: int = 0) -> dict:
    key_of = jax.random.split(jax.random.key(seed), 7)
    velocity = draw_velocity(jax.random.fold_in(key_of[6], 71), 0)
    state_now = normal_values(key_of[1], (PARTICLES, NX, NY, NZ), 1.0, 6.0, ((0, 2), (1, 2), (2, 8)), jnp.float32)
    state_prev = normal_values(key_of[2], (PARTICLES, NX, NY, NZ), 1.0, 6.0, ((0, 2), (1, 2), (2, 8)), jnp.float32)
    observed = normal_values(key_of[3], (NRECV, NT), 1.0, 6.0, ((0, 16),), jnp.float32)
    rec_cell = set_ends(jax.random.randint(key_of[4], (NRECV,), 0, CX * CY * NZ), jax.random.fold_in(key_of[4], 1), 0, (CX * CY * NZ) - 1).astype(jnp.int32)
    rec_gather_keys = jax.random.split(jax.random.fold_in(key_of[5], 1), NRECV // REC_DEV)
    rec_gather_turns = jax.random.permutation(jax.random.fold_in(key_of[5], 3), NRECV // REC_DEV)
    rec_gather = jax.vmap(lambda own, number: assign_block(jax.random.fold_in(key_of[5], 2), own, number, REC_DEV, N_XLINE, 1, CAP, 2))(rec_gather_keys, rec_gather_turns).reshape((NRECV, 1))
    return dict(velocity=velocity, state_now=state_now, state_prev=state_prev, observed=observed, rec_cell=rec_cell, rec_gather=rec_gather)


COEFFS = (8.0 / 5.0, -1.0 / 5.0, 8.0 / 315.0, -1.0 / 560.0)
CENTER = -205.0 / 72.0
KERNEL_WIDTH = 0.004
NOISE_VARIANCE = 0.0005
STEP_SIZE = 0.01
RIDGE_BASE = 1.0
RIDGE_SHARE = 0.1
HIGHEST = lax.Precision.HIGHEST

def laplace_inner(block):
    size_x, size_y, size_z = block.shape
    inner_x = size_x - 8
    inner_y = size_y - 8
    padded = jnp.pad(block, ((0, 0), (0, 0), (4, 4)))
    total = 3.0 * CENTER * block[4:4 + inner_x, 4:4 + inner_y, :]
    for shift in range(1, 5):
        weight = COEFFS[shift - 1]
        beside = padded[4 + shift:4 + shift + inner_x, 4:4 + inner_y, 4:4 + size_z]
        beside = beside + padded[4 - shift:4 - shift + inner_x, 4:4 + inner_y, 4:4 + size_z]
        beside = beside + padded[4:4 + inner_x, 4 + shift:4 + shift + inner_y, 4:4 + size_z]
        beside = beside + padded[4:4 + inner_x, 4 - shift:4 - shift + inner_y, 4:4 + size_z]
        beside = beside + padded[4:4 + inner_x, 4:4 + inner_y, 4 + shift:4 + shift + size_z]
        beside = beside + padded[4:4 + inner_x, 4:4 + inner_y, 4 - shift:4 - shift + size_z]
        total = total + weight * beside
    return total

def laplace(field):
    return laplace_inner(jnp.pad(field, ((4, 4), (4, 4), (0, 0))))

def lagged_traces(traces):
    steps = traces.shape[1]
    padded = jnp.pad(traces, ((0, 0), (TAPS - 1, 0)))
    return jnp.stack([padded[:, TAPS - 1 - shift:TAPS - 1 - shift + steps] for shift in range(TAPS)], axis=1)

def filter_stats(lagged, observed):
    count = lagged.shape[0]
    gram = jnp.einsum('mkt,mlt->mkl', lagged, lagged, precision=HIGHEST).reshape(count, TAPS * TAPS)
    cross = jnp.einsum('mkt,mt->mk', lagged, observed, precision=HIGHEST)
    return (gram, cross)

def solve_filter(gram, cross):
    matrix = gram.reshape(-1, TAPS, TAPS)
    trace_sum = jnp.trace(matrix, axis1=1, axis2=2)
    ridge = RIDGE_BASE + RIDGE_SHARE * trace_sum / TAPS
    matrix = matrix + ridge[:, None, None] * jnp.eye(TAPS, dtype=jnp.float32)[None]
    factor = jnp.linalg.cholesky(matrix)
    return jax.scipy.linalg.cho_solve((factor, True), cross[:, :, None])[:, :, 0]

def adjoint_sources(lagged, observed, filters):
    steps = observed.shape[1]
    fitted = jnp.einsum('mk,mkt->mt', filters, lagged, precision=HIGHEST)
    misfit = fitted - observed
    padded = jnp.pad(misfit, ((0, 0), (0, TAPS - 1)))
    ahead = jnp.stack([padded[:, shift:shift + steps] for shift in range(TAPS)], axis=1)
    return jnp.einsum('mk,mkt->mt', filters, ahead, precision=HIGHEST)

def reference(velocity, state_now, state_prev, observed, rec_cell, rec_gather):
    receivers = rec_cell.shape[0]
    device_block = jnp.arange(receivers, dtype=jnp.int32) // REC_DEV
    inline_row = device_block // N_XLINE
    xline_col = device_block % N_XLINE
    local_x = rec_cell // (CY * NZ)
    local_y = rec_cell // NZ % CY
    local_z = rec_cell % NZ
    flat_cell = ((inline_row * CX + local_x) * NY + xline_col * CY + local_y) * NZ + local_z
    gather_key = inline_row * N_XLINE + rec_gather[:, 0]
    gathers = N_INLINE * N_XLINE
    onehot = (gather_key[:, None] == jnp.arange(gathers, dtype=jnp.int32)[None, :]).astype(jnp.float32)
    gradients = []
    for particle in range(PARTICLES):
        courant = velocity[particle]

        def advance(carry, unused):
            current, previous = carry
            laplacian = laplace(current)
            following = 2.0 * current - previous + courant * laplacian
            return ((following, current), (laplacian, following.reshape(-1)[flat_cell]))
        unused, (laplacians, traces) = lax.scan(advance, (state_now[particle], state_prev[particle]), None, length=NT)
        synthetic = traces.T
        lagged = lagged_traces(synthetic)
        gram, cross = filter_stats(lagged, observed)
        gram_all = jnp.dot(onehot.T, gram, precision=HIGHEST)
        cross_all = jnp.dot(onehot.T, cross, precision=HIGHEST)
        filters_all = solve_filter(gram_all, cross_all)
        filters = jnp.dot(onehot, filters_all, precision=HIGHEST)
        adjoint_source = adjoint_sources(lagged, observed, filters)

        def backward(carry, inputs):
            wave, wave_old, gradient = carry
            laplacian, source = inputs
            wave_new = 2.0 * wave - wave_old + courant * laplace(wave)
            wave_new = wave_new.reshape(-1).at[flat_cell].add(source).reshape(wave.shape)
            return ((wave_new, wave, gradient + wave_new * laplacian), None)
        zeros_field = jnp.zeros(courant.shape, jnp.float32)
        (wave, wave_old, gradient), unused = lax.scan(backward, (zeros_field, zeros_field, zeros_field), (laplacians, adjoint_source.T), reverse=True)
        gradients.append(gradient / NT)
    cells = NX * NY * NZ
    updates = []
    for particle in range(PARTICLES):
        total = jnp.zeros(velocity.shape[1:], jnp.float32)
        for other in range(PARTICLES):
            distance = jnp.sum(jnp.square(velocity[particle] - velocity[other])) / cells
            kernel = jnp.exp(-distance / KERNEL_WIDTH)
            total = total + kernel * (-gradients[other] / NOISE_VARIANCE + 2.0 * (velocity[particle] - velocity[other]) / KERNEL_WIDTH)
        updates.append(STEP_SIZE / PARTICLES * total)
    return jnp.stack(updates)
```

```python
import jax
import jax.numpy as jnp
from jax import lax
from jax.experimental import pallas as pl
from jax.experimental.pallas import tpu as pltpu
from jax.sharding import PartitionSpec as P

NT = 32
CAP = 16
TAPS = 8


COEFFS = (8.0 / 5.0, -1.0 / 5.0, 8.0 / 315.0, -1.0 / 560.0)
CENTER = -205.0 / 72.0
KERNEL_WIDTH = 0.004
NOISE_VARIANCE = 0.0005
STEP_SIZE = 0.01
RIDGE_BASE = 1.0
RIDGE_SHARE = 0.1
HIGHEST = lax.Precision.HIGHEST


def extended(block, sides, width):
    for axis, dim in sides:
        count = lax.axis_size(axis)
        forward = [(i, i + 1) for i in range(count - 1)]
        backward = [(target, source) for source, target in forward]
        low = lax.ppermute(
            lax.slice_in_dim(block, block.shape[dim] - width, None, axis=dim), axis, forward
        )
        high = lax.ppermute(lax.slice_in_dim(block, 0, width, axis=dim), axis, backward)
        block = jnp.concatenate([low, block, high], axis=dim)
    return block


def laplace_inner(block):
    size_x, size_y, size_z = block.shape
    inner_x = size_x - 8
    inner_y = size_y - 8
    padded = jnp.pad(block, ((0, 0), (0, 0), (4, 4)))
    total = 3.0 * CENTER * block[4 : 4 + inner_x, 4 : 4 + inner_y, :]
    for shift in range(1, 5):
        weight = COEFFS[shift - 1]
        beside = padded[4 + shift : 4 + shift + inner_x, 4 : 4 + inner_y, 4 : 4 + size_z]
        beside = beside + padded[4 - shift : 4 - shift + inner_x, 4 : 4 + inner_y, 4 : 4 + size_z]
        beside = beside + padded[4 : 4 + inner_x, 4 + shift : 4 + shift + inner_y, 4 : 4 + size_z]
        beside = beside + padded[4 : 4 + inner_x, 4 - shift : 4 - shift + inner_y, 4 : 4 + size_z]
        beside = beside + padded[4 : 4 + inner_x, 4 : 4 + inner_y, 4 + shift : 4 + shift + size_z]
        beside = beside + padded[4 : 4 + inner_x, 4 : 4 + inner_y, 4 - shift : 4 - shift + size_z]
        total = total + weight * beside
    return total


def lagged_traces(traces):
    steps = traces.shape[1]
    padded = jnp.pad(traces, ((0, 0), (TAPS - 1, 0)))
    return jnp.stack(
        [padded[:, TAPS - 1 - shift : TAPS - 1 - shift + steps] for shift in range(TAPS)], axis=1
    )


def filter_stats(lagged, observed):
    count = lagged.shape[0]
    gram = jnp.einsum("mkt,mlt->mkl", lagged, lagged, precision=HIGHEST).reshape(count, TAPS * TAPS)
    cross = jnp.einsum("mkt,mt->mk", lagged, observed, precision=HIGHEST)
    return (gram, cross)


def solve_filter(gram, cross):
    matrix = gram.reshape(-1, TAPS, TAPS)
    sums = [matrix[:, k, l] for k in range(TAPS) for l in range(k + 1)]
    sums = jnp.stack(sums + [cross[:, k] for k in range(TAPS)])
    return jnp.concatenate(solve_rows(sums), axis=0).T


def adjoint_sources(lagged, observed, filters):
    steps = observed.shape[1]
    fitted = jnp.einsum("mk,mkt->mt", filters, lagged, precision=HIGHEST)
    misfit = fitted - observed
    padded = jnp.pad(misfit, ((0, 0), (0, TAPS - 1)))
    ahead = jnp.stack([padded[:, shift : shift + steps] for shift in range(TAPS)], axis=1)
    return jnp.einsum("mk,mkt->mt", filters, ahead, precision=HIGHEST)


def per_device(velocity, state_now, state_prev, observed, rec_cell, rec_gather):
    courant = velocity[0]
    particles = lax.axis_size("particle")
    models = lax.all_gather(velocity, "particle", axis=0, tiled=True)
    partial_sums = jnp.sum(jnp.square(models - velocity), axis=(1, 2, 3))
    cells_all = courant.size * lax.axis_size("inline") * lax.axis_size("xline")
    distance = lax.psum(partial_sums, ("inline", "xline")) / cells_all
    kernel = jnp.exp(-distance / KERNEL_WIDTH)

    def advance(carry, unused):
        current, previous = carry
        padded = extended(current[None], (("inline", 1), ("xline", 2)), 4)[0]
        laplacian = laplace_inner(padded)
        following = 2.0 * current - previous + courant * laplacian
        return ((following, current), (laplacian, following.reshape(-1)[rec_cell]))

    unused, (laplacians, traces) = lax.scan(advance, (state_now[0], state_prev[0]), None, length=NT)
    synthetic = traces.T
    steps = observed.shape[1]
    xline_count = lax.axis_size("xline")
    target = rec_gather[:, 0]
    choose = (target[:, None] == jnp.arange(xline_count, dtype=jnp.int32)[None, :]).astype(
        jnp.int32
    )
    order = jnp.arange(target.shape[0], dtype=jnp.int32)
    earlier = (order[None, :] < order[:, None]).astype(jnp.float32)
    before = jnp.dot(earlier, choose.astype(jnp.float32), precision=HIGHEST).astype(jnp.int32)
    position = target * CAP + jnp.sum(before * choose, axis=1)
    outgoing = jnp.zeros((xline_count * CAP, 2 * steps), jnp.float32)
    outgoing = outgoing.at[position].set(jnp.concatenate([synthetic, observed], axis=1))
    arrived = lax.all_to_all(
        outgoing.reshape(xline_count, CAP, 2 * steps),
        "xline",
        split_axis=0,
        concat_axis=0,
        tiled=True,
    )
    slots = arrived.reshape(xline_count * CAP, 2 * steps)
    slot_lagged = lagged_traces(slots[:, :steps])
    slot_observed = slots[:, steps:]
    gram, cross = filter_stats(slot_lagged, slot_observed)
    filters_one = solve_filter(
        jnp.sum(gram, axis=0, keepdims=True), jnp.sum(cross, axis=0, keepdims=True)
    )
    filters = jnp.broadcast_to(filters_one, (slots.shape[0], TAPS))
    slot_adjoint = adjoint_sources(slot_lagged, slot_observed, filters)
    returned = lax.all_to_all(
        slot_adjoint.reshape(xline_count, CAP, steps),
        "xline",
        split_axis=0,
        concat_axis=0,
        tiled=True,
    )
    adjoint_source = returned.reshape(xline_count * CAP, steps)[position]

    def backward(carry, inputs):
        wave, wave_old, gradient = carry
        laplacian, source = inputs
        padded = extended(wave[None], (("inline", 1), ("xline", 2)), 4)[0]
        wave_new = 2.0 * wave - wave_old + courant * laplace_inner(padded)
        wave_new = wave_new.reshape(-1).at[rec_cell].add(source).reshape(wave.shape)
        return ((wave_new, wave, gradient + wave_new * laplacian), None)

    zeros_field = jnp.zeros(courant.shape, jnp.float32)
    (wave, wave_old, gradient), unused = lax.scan(
        backward,
        (zeros_field, zeros_field, zeros_field),
        (laplacians, adjoint_source.T),
        reverse=True,
    )
    gradient = gradient / NT
    gradients = lax.all_gather(gradient[None], "particle", axis=0, tiled=True)
    terms = -gradients / NOISE_VARIANCE + 2.0 * (velocity - models) / KERNEL_WIDTH
    update = (
        STEP_SIZE / particles * jnp.sum(kernel[:, None, None, None] * terms, axis=0, keepdims=True)
    )
    return update


STEPS = 4
HALO = 4 * STEPS
OWN_X = 8
INTEGER_COEFFS = (8064.0, -1008.0, 128.0, -9.0)
INTEGER_SCALE = 1.0 / 5040.0


def tiles_of(step, rows):
    first = 4 * (step + 1)
    return [first + 8 * i for i in range((rows - 2 * first) // 8)]


def split_two(value):
    high = value.astype(jnp.bfloat16)
    rest = (value - high.astype(jnp.float32)).astype(jnp.bfloat16)
    return high, rest


def band_matrix():
    row = lax.broadcasted_iota(jnp.int32, (256, 128), 0) % 128
    col = lax.broadcasted_iota(jnp.int32, (256, 128), 1)
    away = jnp.abs(row - col)
    band = jnp.zeros((256, 128), jnp.float32)
    for shift in range(1, 5):
        band = jnp.where(away == shift, INTEGER_COEFFS[shift - 1], band)
    return band.astype(jnp.bfloat16)


def laplace_tile(wave, first, band):
    center = wave[:, pl.ds(first, 8), :]
    layers = center.shape[0]
    high, rest = split_two(center.reshape(layers * 8, 128))
    depth = jnp.dot(
        jnp.concatenate([high, rest], axis=1), band, preferred_element_type=jnp.float32
    ).reshape(layers, 8, 128)
    total = 3.0 * CENTER * center + INTEGER_SCALE * depth
    for shift in range(1, 5):
        beside = wave[:, pl.ds(first + shift, 8), :] + wave[:, pl.ds(first - shift, 8), :]
        blank = jnp.zeros((shift, 8, 128), jnp.float32)
        beside = beside + jnp.concatenate([center[shift:], blank], axis=0)
        beside = beside + jnp.concatenate([blank, center[:-shift]], axis=0)
        total = total + COEFFS[shift - 1] * beside
    return center, total


def own_half(value, inline):
    return jnp.where(inline == 0, value[:OWN_X], value[OWN_X:])


def exchange(number, wave, staged, near, far, send_sems, recv_sems, own_y, where):
    inline, xline, particle, count = where
    slot = lax.rem(number, 2)
    has = (xline > 0, xline < count - 1)
    near_row = (HALO, own_y + 8)
    far_row = (HALO + 8, own_y)
    old_row = (HALO + 4, own_y + 4)

    def copies(side):
        target = (inline, xline + (2 * side - 1), particle)
        near_copy = pltpu.make_async_remote_copy(
            src_ref=wave.at[0, :, pl.ds(near_row[side], 8), :],
            dst_ref=near.at[slot, 1 - side],
            send_sem=send_sems.at[slot, side, 0],
            recv_sem=recv_sems.at[slot, 1 - side, 0],
            device_id=target,
            device_id_type=pl.DeviceIdType.MESH,
        )
        far_copy = pltpu.make_async_remote_copy(
            src_ref=staged.at[side],
            dst_ref=far.at[slot, 1 - side],
            send_sem=send_sems.at[slot, side, 1],
            recv_sem=recv_sems.at[slot, 1 - side, 1],
            device_id=target,
            device_id_type=pl.DeviceIdType.MESH,
        )
        return near_copy, far_copy

    def start():
        for side in range(2):

            @pl.when(has[side])
            def _():
                near_copy, far_copy = copies(side)
                near_copy.start()
                staged[side, 0] = wave[0, :, pl.ds(far_row[side], 8), :]
                staged[side, 1] = wave[1, :, pl.ds(old_row[side], 8), :]
                far_copy.start()

    def take_near():
        for side in range(2):

            @pl.when(has[side])
            def _():
                copies(side)[0].wait_send()
                pltpu.make_async_remote_copy(
                    src_ref=wave.at[0, :, pl.ds(near_row[1 - side], 8), :],
                    dst_ref=near.at[slot, side],
                    send_sem=send_sems.at[slot, 1 - side, 0],
                    recv_sem=recv_sems.at[slot, side, 0],
                    device_id=(inline, xline + (2 * side - 1), particle),
                    device_id_type=pl.DeviceIdType.MESH,
                ).wait_recv()
                row = (HALO - 8, HALO + own_y)[side]
                wave[0, :, pl.ds(row, 8), :] = near[slot, side]

    def take_far():
        for side in range(2):

            @pl.when(has[side])
            def _():
                copies(side)[1].wait_send()
                pltpu.make_async_remote_copy(
                    src_ref=staged.at[1 - side],
                    dst_ref=far.at[slot, side],
                    send_sem=send_sems.at[slot, 1 - side, 1],
                    recv_sem=recv_sems.at[slot, side, 1],
                    device_id=(inline, xline + (2 * side - 1), particle),
                    device_id_type=pl.DeviceIdType.MESH,
                ).wait_recv()
                row = (HALO - 16, HALO + own_y + 8)[side]
                wave[0, :, pl.ds(row, 8), :] = far[slot, side, 0]
                row = (HALO - 12, HALO + own_y + 4)[side]
                wave[1, :, pl.ds(row, 8), :] = far[slot, side, 1]

    return start, take_near, take_far


LEVELS = ((0, 1, 2), (2, 0, 3), (3, 2, 1), (1, 3, 0))


def phases(rows):
    alone, with_near, with_all = [], [], []
    for step in range(STEPS):
        for first in tiles_of(step, rows):
            reach = 4 * (step + 1)
            low, high = first - reach, first + 8 + reach
            if low >= HALO and high <= rows - HALO and step < 2:
                alone.append((step, first))
            elif low >= HALO - 8 and high <= rows - HALO + 8 and step < 3:
                with_near.append((step, first))
            else:
                with_all.append((step, first))
    return alone, with_near, with_all


def run_round(number, hidden, tile, rows, transfer):
    start, take_near, take_far = transfer
    alone, with_near, with_all = phases(rows)

    @pl.when(number > 0)
    def _():
        start()
        hidden()

    for step, first in alone:
        tile(step, first)
    pl.when(number > 0)(take_near)
    for step, first in with_near:
        tile(step, first)
    pl.when(number > 0)(take_far)
    for step, first in with_all:
        tile(step, first)


def broadcast_copy(step, source, table, send_sems, recv_sems, me, particle, size, xlines):
    peer = lax.rem(me + step, size)
    return pltpu.make_async_remote_copy(
        src_ref=source,
        dst_ref=table.at[me],
        send_sem=send_sems.at[step],
        recv_sem=recv_sems.at[step],
        device_id=(peer // xlines, lax.rem(peer, xlines), particle),
        device_id_type=pl.DeviceIdType.MESH,
    )


def arrived_copy(step, source, table, send_sems, recv_sems, me, particle, size, xlines):
    peer = lax.rem(me + size - step, size)
    return pltpu.make_async_remote_copy(
        src_ref=source,
        dst_ref=table.at[peer],
        send_sem=send_sems.at[step],
        recv_sem=recv_sems.at[step],
        device_id=(peer // xlines, lax.rem(peer, xlines), particle),
        device_id_type=pl.DeviceIdType.MESH,
    )


def solve_rows(sums):
    entry = {}
    index = 0
    for k in range(TAPS):
        for l in range(k + 1):
            entry[k, l] = sums[index : index + 1]
            index += 1
    right = [sums[index + k : index + k + 1] for k in range(TAPS)]
    trace_sum = sum(entry[k, k] for k in range(TAPS))
    ridge = RIDGE_BASE + RIDGE_SHARE * trace_sum / TAPS
    for k in range(TAPS):
        entry[k, k] = entry[k, k] + ridge
    inverse = []
    for k in range(TAPS):
        inverse.append(1.0 / entry[k, k])
        factor = {i: entry[i, k] * inverse[k] for i in range(k + 1, TAPS)}
        for i in range(k + 1, TAPS):
            for l in range(k + 1, i + 1):
                entry[i, l] = entry[i, l] - factor[i] * entry[l, k]
            right[i] = right[i] - factor[i] * right[k]
        for i in range(k + 1, TAPS):
            entry[i, k] = factor[i]
    right = [right[k] * inverse[k] for k in range(TAPS)]
    for k in reversed(range(TAPS)):
        for i in range(k):
            right[i] = right[i] - entry[k, i] * right[k]
    return right


def whole_kernel(
    rec_layer, rec_row, velocity, state_now, state_prev, notes, depth_mask, update,
    courant, wave, staged, near, far, laplacians, picked, notes_all, traces, traces_all, model,
    synthetic, products, filters, misfit, strengths, hits, places, gradient, gradient_own,
    gradient_other, start_send, start_recv, send_sems, recv_sems, note_send, note_recv,
    trace_send, trace_recv, pair_send, pair_recv,
):
    inline, xline, particle = (lax.axis_index(a) for a in ("inline", "xline", "particle"))
    count = lax.axis_size("xline")
    size = 2 * count
    me = inline * count + xline
    own_y = velocity.shape[2]
    rows = own_y + 2 * HALO
    receivers = rec_row.shape[0]
    has_low, has_high = xline > 0, xline < count - 1
    other = 1 - inline
    always = xline >= 0
    partners = [
        (always, (other, xline, particle), 0, own_y, HALO),
        (has_low, (inline, xline - 1, particle), 0, HALO, own_y + HALO),
        (has_high, (inline, xline + 1, particle), own_y - HALO, HALO, 0),
        (has_low, (other, xline - 1, particle), 0, HALO, own_y + HALO),
        (has_high, (other, xline + 1, particle), own_y - HALO, HALO, 0),
    ]
    mirror = [0, 2, 1, 4, 3]
    sources = (state_now, state_prev, velocity)
    frames = (wave.at[0], wave.at[1], courant)

    barrier = pltpu.get_barrier_semaphore()

    def greet(step, carry):
        peer = lax.rem(me + step, size)
        pl.semaphore_signal(
            barrier, inc=1, device_id=(peer // count, lax.rem(peer, count), particle),
            device_id_type=pl.DeviceIdType.MESH,
        )
        return carry

    lax.fori_loop(1, size, greet, 0)
    pl.semaphore_signal(
        barrier, inc=1, device_id=(inline, xline, 1 - particle),
        device_id_type=pl.DeviceIdType.MESH,
    )

    layers = pl.ds(inline * OWN_X, OWN_X)
    for frame in frames:
        for edge in (0, own_y + HALO):

            @pl.when(jnp.logical_not(has_low if edge == 0 else has_high))
            def _():
                frame[:, pl.ds(edge, HALO), :] = jnp.zeros((2 * OWN_X, HALO, 128), jnp.float32)

    for kind in range(3):
        frames[kind][layers, pl.ds(HALO, own_y), :] = sources[kind][0]
    notes_all[me] = notes[...]
    picked[:, pl.ds(other * receivers, receivers), :] = jnp.zeros(
        (NT, receivers, 128), jnp.float32
    )
    pl.semaphore_wait(barrier, size)

    def start_copy(index, kind):
        valid, target, first, extent, landing_row = partners[index]
        return pltpu.make_async_remote_copy(
            src_ref=sources[kind].at[0, :, pl.ds(first, extent), :],
            dst_ref=frames[kind].at[layers, pl.ds(landing_row, extent), :],
            send_sem=start_send.at[index, kind],
            recv_sem=start_recv.at[index, kind],
            device_id=target,
            device_id_type=pl.DeviceIdType.MESH,
        )

    def arrival(index, kind):
        valid, target, first, extent, landing_row = partners[mirror[index]]
        partner_inline = partners[index][1][0]
        back = (HALO, 0, own_y + HALO, 0, own_y + HALO)[index]
        return pltpu.make_async_remote_copy(
            src_ref=sources[kind].at[0, :, pl.ds(first, extent), :],
            dst_ref=frames[kind].at[pl.ds(partner_inline * OWN_X, OWN_X), pl.ds(back, extent), :],
            send_sem=start_send.at[index, kind],
            recv_sem=start_recv.at[mirror[index], kind],
            device_id=partners[index][1],
            device_id_type=pl.DeviceIdType.MESH,
        )

    for kind in range(3):
        for index in range(5):

            @pl.when(partners[index][0])
            def _():
                start_copy(index, kind).start()

    def pair_copy(source, target, index):
        return pltpu.make_async_remote_copy(
            src_ref=source,
            dst_ref=target,
            send_sem=pair_send.at[index],
            recv_sem=pair_recv.at[index],
            device_id=(inline, xline, 1 - particle),
            device_id_type=pl.DeviceIdType.MESH,
        )

    pair_copy(velocity.at[0], model, 0).start()
    plane = (me, particle, size, count)

    def send_note(step, carry):
        broadcast_copy(step, notes, notes_all, note_send, note_recv, *plane).start()
        return carry

    lax.fori_loop(1, size, send_note, 0)

    for kind in range(3):
        for index in range(5):

            @pl.when(partners[index][0])
            def _():
                start_copy(index, kind).wait_send()
                arrival(index, kind).wait_recv()

    band = band_matrix()
    where = (inline, xline, particle, count)
    ones = jnp.ones((8, 256), jnp.bfloat16)

    def read_traces(first_time):
        for step in range(STEPS):
            time = first_time + step
            high, rest = split_two(picked[time] * depth_mask[...])
            row = lax.dot_general(
                ones, jnp.concatenate([high, rest], axis=1), (((1,), (1,)), ((), ())),
                preferred_element_type=jnp.float32,
            )
            traces[pl.ds(time, 1), :] = row[0:1]

    def pick_traces(number):
        for step in range(STEPS):
            new = wave.at[LEVELS[step][2]]
            for group in range(0, receivers, 16):
                lines = [
                    new[inline * OWN_X + rec_layer[r], pl.ds(rec_row[r], 1), :]
                    for r in range(group, group + 16)
                ]
                for offset, line in enumerate(lines):
                    picked[
                        number * STEPS + step,
                        pl.ds(inline * receivers + group + offset, 1),
                        :,
                    ] = line

    def hidden_traces(number):
        pick_traces(number)
        read_traces(number * STEPS)

    def forward_round(number, carry):
        transfer = exchange(
            number, wave, staged, near, far, send_sems, recv_sems, own_y, where
        )

        def tile(step, first):
            now, old, new = (wave.at[level] for level in LEVELS[step])
            time = number * STEPS + step
            center, laplacian = laplace_tile(now, first, band)
            here = pl.ds(first, 8)
            new[:, here, :] = 2.0 * center - old[:, here, :] + courant[:, here, :] * laplacian
            if HALO - 8 < first < HALO + own_y:
                laplacians[time, :, pl.ds(first - HALO + 8, 8), :] = own_half(laplacian, inline)

        run_round(number, lambda: hidden_traces(number - 1), tile, rows, transfer)
        return carry

    lax.fori_loop(0, NT // STEPS, forward_round, 0)
    hidden_traces(NT // STEPS - 1)

    pair_copy(velocity.at[0], model, 0).wait()
    apart = jnp.square(velocity[0] - model[...])
    traces[pl.ds(NT, 8), :] = jnp.zeros((8, 128), jnp.float32)
    traces[pl.ds(NT, 1), :] = jnp.sum(jnp.sum(apart, axis=0), axis=0, keepdims=True)
    traces_all[me] = traces[...]

    def send_traces(step, carry):
        broadcast_copy(step, traces, traces_all, trace_send, trace_recv, *plane).start()
        return carry

    lax.fori_loop(1, size, send_traces, 0)

    def take_notes(step, carry):
        arrived_copy(step, notes, notes_all, note_send, note_recv, *plane).wait()
        return carry

    lax.fori_loop(1, size, take_notes, 0)

    for column in range(3):
        from_column = xline + (column - 1)
        inside = (from_column >= 0) & (from_column < count)
        safe = jnp.clip(from_column, 0, count - 1)
        pair = notes_all[safe] + notes_all[count + safe]
        base = pair[NT : NT + 1].astype(jnp.int32)
        local_row = pair[NT + 1 : NT + 2].astype(jnp.int32)
        depth = pair[NT + 2 : NT + 3].astype(jnp.int32)
        moved = (column - 1) * own_y + HALO
        frame_row = local_row + moved
        fits = (frame_row >= 0) & (frame_row < rows) & inside
        row_id = jnp.where(fits, base + moved, -1)
        place = (lax.broadcasted_iota(jnp.int32, (128, 128), 0) == depth).astype(jnp.float32)
        place = place.astype(jnp.bfloat16)
        places[:, pl.ds(256 * column, 128)] = place
        places[:, pl.ds(256 * column + 128, 128)] = place
        line = lax.broadcasted_iota(jnp.int32, (128, 128), 0)
        for (first, found), slot in hit_slots(rows, own_y).items():
            if found == column:
                wanted = (line // 8) * rows + first + lax.rem(line, 8)
                hit = (wanted == row_id).astype(jnp.float32).astype(jnp.bfloat16)
                hits[slot, :, pl.ds(0, 128)] = hit
                hits[slot, :, pl.ds(128, 128)] = hit
    wave[...] = jnp.zeros(wave.shape, jnp.float32)
    gradient[...] = jnp.zeros(gradient.shape, jnp.float32)
    products[...] = jnp.zeros(products.shape, jnp.float32)
    misfit[...] = jnp.zeros(misfit.shape, jnp.float32)
    synthetic[...] = jnp.zeros(synthetic.shape, jnp.float32)

    def take_traces(step, carry):
        arrived_copy(step, traces, traces_all, trace_send, trace_recv, *plane).wait()
        return carry

    lax.fori_loop(1, size, take_traces, 0)

    keys = lax.broadcasted_iota(jnp.int32, (128, 128), 0)

    def members_of(column):
        pair = notes_all[column] + notes_all[count + column]
        return pair[:NT], (keys == pair[NT + 3 : NT + 4].astype(jnp.int32)).astype(jnp.float32)

    def add_column(column, sums):
        both = traces_all[column] + traces_all[count + column]
        synthetic[column, pl.ds(8, NT), :] = both[:NT]
        recorded, members = members_of(column)
        lagged = [synthetic[column, pl.ds(8 - k, NT), :] for k in range(TAPS)]
        index = 0
        for k in range(TAPS):
            for l in range(k + 1):
                products[pl.ds(index, 1), :] = jnp.sum(lagged[k] * lagged[l], axis=0, keepdims=True)
                index += 1
        for k in range(TAPS):
            products[pl.ds(index + k, 1), :] = jnp.sum(lagged[k] * recorded, axis=0, keepdims=True)
        return sums + lax.dot_general(
            products[...], members, (((1,), (1,)), ((), ())),
            preferred_element_type=jnp.float32, precision=HIGHEST,
        )

    sums = lax.fori_loop(0, count, add_column, jnp.zeros((48, 128), jnp.float32))
    for k, row in enumerate(solve_rows(sums)):
        filters[pl.ds(k, 1), :] = row

    for column in range(3):
        safe = jnp.clip(xline + (column - 1), 0, count - 1)
        recorded, members = members_of(safe)
        own = jnp.dot(
            filters[...], members, preferred_element_type=jnp.float32, precision=HIGHEST
        )
        fitted = sum(own[k : k + 1] * synthetic[safe, pl.ds(8 - k, NT), :] for k in range(TAPS))
        misfit[column, pl.ds(0, NT), :] = fitted - recorded
        source = sum(own[k : k + 1] * misfit[column, pl.ds(k, NT), :] for k in range(TAPS))
        high, rest = split_two(source)
        strengths[:, pl.ds(256 * column, 128)] = high.astype(jnp.float32)
        strengths[:, pl.ds(256 * column + 128, 128)] = rest.astype(jnp.float32)

    slots = hit_slots(rows, own_y)

    def backward_round(number, carry):
        transfer = exchange(
            number, wave, staged, near, far, send_sems, recv_sems, own_y, where
        )

        def tile(step, first):
            now, old, new = (wave.at[level] for level in LEVELS[step])
            time = NT - 1 - (number * STEPS + step)
            strength = strengths[pl.ds(time, 1), :].astype(jnp.bfloat16)
            center, laplacian = laplace_tile(now, first, band)
            here = pl.ds(first, 8)
            added = 0.0
            for column in columns_of(first, rows, own_y):
                part = slice(256 * column, 256 * (column + 1))
                added = added + lax.dot_general(
                    hits[slots[first, column]] * strength[:, part],
                    places[:, part],
                    (((1,), (1,)), ((), ())),
                    preferred_element_type=jnp.float32,
                )
            following = 2.0 * center - old[:, here, :] + courant[:, here, :] * laplacian
            following = following + added.reshape(2 * OWN_X, 8, 128)
            new[:, here, :] = following
            if HALO - 8 < first < HALO + own_y:
                kept = pl.ds(first - HALO + 8, 8)
                gradient[:, kept, :] = (
                    gradient[:, kept, :]
                    + own_half(following, inline) * laplacians[time, :, kept, :]
                )

        run_round(number, lambda: None, tile, rows, transfer)
        return carry

    lax.fori_loop(0, NT // STEPS, backward_round, 0)
    gradient_own[...] = gradient[:, pl.ds(8, own_y), :] * (1.0 / NT)
    pair_copy(gradient_own, gradient_other, 1).start()
    apart = jnp.zeros((1, 128), jnp.float32)
    for block in range(size):
        apart = apart + traces_all[block, pl.ds(NT, 1), :]
    cells = size * OWN_X * own_y * 128
    distance = jnp.sum(apart, axis=1, keepdims=True) / cells
    weight = jnp.exp(jnp.broadcast_to(-distance / KERNEL_WIDTH, (8, 128)))[0:1]
    between = 2.0 * (velocity[0] - model[...]) / KERNEL_WIDTH
    pair_copy(gradient_own, gradient_other, 1).wait()
    own_term = gradient_own[...] * (-1.0 / NOISE_VARIANCE)
    other_term = gradient_other[...] * (-1.0 / NOISE_VARIANCE) + between
    update[0] = (STEP_SIZE / 2) * (own_term + weight[None] * other_term)


def columns_of(first, rows, own_y):
    spans = ((0, HALO), (HALO, HALO + own_y), (HALO + own_y, rows))
    return [c for c, (start, stop) in enumerate(spans) if first < stop and first + 8 > start]


def hit_slots(rows, own_y):
    slots = {}
    for step in range(STEPS):
        for first in tiles_of(step, rows):
            for column in columns_of(first, rows, own_y):
                slots.setdefault((first, column), len(slots))
    return slots


def per_device_pair(velocity, state_now, state_prev, observed, rec_cell, rec_gather):
    inline, xlines = lax.axis_index("inline"), lax.axis_size("xline")
    own_y = velocity.shape[2]
    rows = own_y + 2 * HALO
    count = rec_cell.shape[0]
    size = 2 * xlines
    line = rec_cell // 128
    layer, local_row = line // own_y, line % own_y
    facts = jnp.stack(
        [
            (inline * OWN_X + layer) * rows + local_row,
            local_row,
            rec_cell % 128,
            inline * xlines + rec_gather[:, 0],
        ]
    ).astype(jnp.float32)
    notes = jnp.concatenate([observed.T, facts, jnp.zeros((4, count), jnp.float32)], axis=0)
    blank = jnp.zeros_like(notes)
    first = inline == 0
    notes = jnp.concatenate([jnp.where(first, notes, blank), jnp.where(first, blank, notes)], axis=1)
    lanes = jnp.arange(128, dtype=jnp.int32)[None, :]
    depth_mask = ((rec_cell % 128)[:, None] == lanes).astype(jnp.float32)
    depth_mask = jnp.concatenate([depth_mask, depth_mask], axis=0)
    vmem = pl.BlockSpec(memory_space=pltpu.VMEM)
    smem = pl.BlockSpec(memory_space=pltpu.SMEM)
    f32, bf16 = jnp.float32, jnp.bfloat16
    dma = pltpu.SemaphoreType.DMA
    return pl.pallas_call(
        whole_kernel,
        out_shape=jax.ShapeDtypeStruct(velocity.shape, f32),
        in_specs=[smem, smem] + [vmem] * 5,
        out_specs=vmem,
        scratch_shapes=[
            pltpu.VMEM((2 * OWN_X, rows, 128), f32),
            pltpu.VMEM((4, 2 * OWN_X, rows, 128), f32),
            pltpu.VMEM((2, 2, 2 * OWN_X, 8, 128), f32),
            pltpu.VMEM((2, 2, 2 * OWN_X, 8, 128), f32),
            pltpu.VMEM((2, 2, 2, 2 * OWN_X, 8, 128), f32),
            pltpu.VMEM((NT, OWN_X, own_y + 16, 128), f32),
            pltpu.VMEM((NT, 2 * count, 128), f32),
            pltpu.VMEM((size, NT + 8, 128), f32),
            pltpu.VMEM((NT + 8, 128), f32),
            pltpu.VMEM((size, NT + 8, 128), f32),
            pltpu.VMEM((OWN_X, own_y, 128), f32),
            pltpu.VMEM((xlines, NT + 8, 128), f32),
            pltpu.VMEM((48, 128), f32),
            pltpu.VMEM((8, 128), f32),
            pltpu.VMEM((3, NT + 8, 128), f32),
            pltpu.VMEM((NT, 768), f32),
            pltpu.VMEM((len(hit_slots(rows, own_y)), 128, 256), bf16),
            pltpu.VMEM((128, 768), bf16),
            pltpu.VMEM((OWN_X, own_y + 16, 128), f32),
            pltpu.VMEM((OWN_X, own_y, 128), f32),
            pltpu.VMEM((OWN_X, own_y, 128), f32),
            dma((5, 3)),
            dma((5, 3)),
            dma((2, 2, 2)),
            dma((2, 2, 2)),
            dma((size,)),
            dma((size,)),
            dma((size,)),
            dma((size,)),
            dma((2,)),
            dma((2,)),
        ],
        compiler_params=pltpu.CompilerParams(
            collective_id=0, has_side_effects=True, vmem_limit_bytes=48 * 1024 * 1024
        ),
        name="inversion_window",
    )(layer, local_row + HALO, velocity, state_now, state_prev, notes, depth_mask)


def solution(mesh):
    body = per_device_pair if (mesh.shape["inline"], mesh.shape["particle"]) == (2, 2) else per_device
    return jax.shard_map(
        body,
        mesh=mesh,
        in_specs=(
            P("particle", "inline", "xline", None),
            P("particle", "inline", "xline", None),
            P("particle", "inline", "xline", None),
            P(("inline", "xline"), None),
            P(("inline", "xline")),
            P(("inline", "xline"), None),
        ),
        out_specs=P("particle", "inline", "xline", None),
        check_vma=False,
    )
```

```python
import jax
import jax.numpy as jnp
from jax import lax
from jax.experimental import pallas as pl
from jax.experimental.pallas import tpu as pltpu
from jax.sharding import PartitionSpec as P

NT = 32
CAP = 16
TAPS = 8


COEFFS = (8.0 / 5.0, -1.0 / 5.0, 8.0 / 315.0, -1.0 / 560.0)
CENTER = -205.0 / 72.0
KERNEL_WIDTH = 0.004
NOISE_VARIANCE = 0.0005
STEP_SIZE = 0.01
RIDGE_BASE = 1.0
RIDGE_SHARE = 0.1
HIGHEST = lax.Precision.HIGHEST


def extended(block, sides, width):
    for axis, dim in sides:
        count = lax.axis_size(axis)
        forward = [(i, i + 1) for i in range(count - 1)]
        backward = [(target, source) for source, target in forward]
        low = lax.ppermute(
            lax.slice_in_dim(block, block.shape[dim] - width, None, axis=dim), axis, forward
        )
        high = lax.ppermute(lax.slice_in_dim(block, 0, width, axis=dim), axis, backward)
        block = jnp.concatenate([low, block, high], axis=dim)
    return block


def laplace_inner(block):
    size_x, size_y, size_z = block.shape
    inner_x = size_x - 8
    inner_y = size_y - 8
    padded = jnp.pad(block, ((0, 0), (0, 0), (4, 4)))
    total = 3.0 * CENTER * block[4 : 4 + inner_x, 4 : 4 + inner_y, :]
    for shift in range(1, 5):
        weight = COEFFS[shift - 1]
        beside = padded[4 + shift : 4 + shift + inner_x, 4 : 4 + inner_y, 4 : 4 + size_z]
        beside = beside + padded[4 - shift : 4 - shift + inner_x, 4 : 4 + inner_y, 4 : 4 + size_z]
        beside = beside + padded[4 : 4 + inner_x, 4 + shift : 4 + shift + inner_y, 4 : 4 + size_z]
        beside = beside + padded[4 : 4 + inner_x, 4 - shift : 4 - shift + inner_y, 4 : 4 + size_z]
        beside = beside + padded[4 : 4 + inner_x, 4 : 4 + inner_y, 4 + shift : 4 + shift + size_z]
        beside = beside + padded[4 : 4 + inner_x, 4 : 4 + inner_y, 4 - shift : 4 - shift + size_z]
        total = total + weight * beside
    return total


def lagged_traces(traces):
    steps = traces.shape[1]
    padded = jnp.pad(traces, ((0, 0), (TAPS - 1, 0)))
    return jnp.stack(
        [padded[:, TAPS - 1 - shift : TAPS - 1 - shift + steps] for shift in range(TAPS)], axis=1
    )


def filter_stats(lagged, observed):
    count = lagged.shape[0]
    gram = jnp.einsum("mkt,mlt->mkl", lagged, lagged, precision=HIGHEST).reshape(count, TAPS * TAPS)
    cross = jnp.einsum("mkt,mt->mk", lagged, observed, precision=HIGHEST)
    return (gram, cross)


def solve_filter(gram, cross):
    matrix = gram.reshape(-1, TAPS, TAPS)
    sums = [matrix[:, k, l] for k in range(TAPS) for l in range(k + 1)]
    sums = jnp.stack(sums + [cross[:, k] for k in range(TAPS)])
    return jnp.concatenate(solve_rows(sums), axis=0).T


def adjoint_sources(lagged, observed, filters):
    steps = observed.shape[1]
    fitted = jnp.einsum("mk,mkt->mt", filters, lagged, precision=HIGHEST)
    misfit = fitted - observed
    padded = jnp.pad(misfit, ((0, 0), (0, TAPS - 1)))
    ahead = jnp.stack([padded[:, shift : shift + steps] for shift in range(TAPS)], axis=1)
    return jnp.einsum("mk,mkt->mt", filters, ahead, precision=HIGHEST)


def per_device(velocity, state_now, state_prev, observed, rec_cell, rec_gather):
    courant = velocity[0]
    particles = lax.axis_size("particle")
    models = lax.all_gather(velocity, "particle", axis=0, tiled=True)
    partial_sums = jnp.sum(jnp.square(models - velocity), axis=(1, 2, 3))
    cells_all = courant.size * lax.axis_size("inline") * lax.axis_size("xline")
    distance = lax.psum(partial_sums, ("inline", "xline")) / cells_all
    kernel = jnp.exp(-distance / KERNEL_WIDTH)

    def advance(carry, unused):
        current, previous = carry
        padded = extended(current[None], (("inline", 1), ("xline", 2)), 4)[0]
        laplacian = laplace_inner(padded)
        following = 2.0 * current - previous + courant * laplacian
        return ((following, current), (laplacian, following.reshape(-1)[rec_cell]))

    unused, (laplacians, traces) = lax.scan(advance, (state_now[0], state_prev[0]), None, length=NT)
    synthetic = traces.T
    steps = observed.shape[1]
    xline_count = lax.axis_size("xline")
    target = rec_gather[:, 0]
    choose = (target[:, None] == jnp.arange(xline_count, dtype=jnp.int32)[None, :]).astype(
        jnp.int32
    )
    order = jnp.arange(target.shape[0], dtype=jnp.int32)
    earlier = (order[None, :] < order[:, None]).astype(jnp.float32)
    before = jnp.dot(earlier, choose.astype(jnp.float32), precision=HIGHEST).astype(jnp.int32)
    position = target * CAP + jnp.sum(before * choose, axis=1)
    outgoing = jnp.zeros((xline_count * CAP, 2 * steps), jnp.float32)
    outgoing = outgoing.at[position].set(jnp.concatenate([synthetic, observed], axis=1))
    arrived = lax.all_to_all(
        outgoing.reshape(xline_count, CAP, 2 * steps),
        "xline",
        split_axis=0,
        concat_axis=0,
        tiled=True,
    )
    slots = arrived.reshape(xline_count * CAP, 2 * steps)
    slot_lagged = lagged_traces(slots[:, :steps])
    slot_observed = slots[:, steps:]
    gram, cross = filter_stats(slot_lagged, slot_observed)
    filters_one = solve_filter(
        jnp.sum(gram, axis=0, keepdims=True), jnp.sum(cross, axis=0, keepdims=True)
    )
    filters = jnp.broadcast_to(filters_one, (slots.shape[0], TAPS))
    slot_adjoint = adjoint_sources(slot_lagged, slot_observed, filters)
    returned = lax.all_to_all(
        slot_adjoint.reshape(xline_count, CAP, steps),
        "xline",
        split_axis=0,
        concat_axis=0,
        tiled=True,
    )
    adjoint_source = returned.reshape(xline_count * CAP, steps)[position]

    def backward(carry, inputs):
        wave, wave_old, gradient = carry
        laplacian, source = inputs
        padded = extended(wave[None], (("inline", 1), ("xline", 2)), 4)[0]
        wave_new = 2.0 * wave - wave_old + courant * laplace_inner(padded)
        wave_new = wave_new.reshape(-1).at[rec_cell].add(source).reshape(wave.shape)
        return ((wave_new, wave, gradient + wave_new * laplacian), None)

    zeros_field = jnp.zeros(courant.shape, jnp.float32)
    (wave, wave_old, gradient), unused = lax.scan(
        backward,
        (zeros_field, zeros_field, zeros_field),
        (laplacians, adjoint_source.T),
        reverse=True,
    )
    gradient = gradient / NT
    gradients = lax.all_gather(gradient[None], "particle", axis=0, tiled=True)
    terms = -gradients / NOISE_VARIANCE + 2.0 * (velocity - models) / KERNEL_WIDTH
    update = (
        STEP_SIZE / particles * jnp.sum(kernel[:, None, None, None] * terms, axis=0, keepdims=True)
    )
    return update


STEPS = 8
HALF = 4
Z_HALO = 4 * STEPS
CORE_HALO = 4 * HALF
OWN_X = 8
OWN_Y = Z_HALO - 8
OWN_END = Z_HALO + OWN_Y
ROWS = OWN_END + CORE_HALO
KEYS = 8
INTEGER_COEFFS = (8064.0, -1008.0, 128.0, -9.0)
INTEGER_SCALE = 1.0 / 5040.0
LEVELS = ((0, 1, 2), (2, 0, 3), (3, 2, 1), (1, 3, 0))
MESH = pl.DeviceIdType.MESH
SECOND, NEAR, OWN, CORE = range(4)
SPANS = ((0, 8), (8, Z_HALO), (Z_HALO, OWN_END), (OWN_END, ROWS))


def split_two(value):
    high = value.astype(jnp.bfloat16)
    rest = (value - high.astype(jnp.float32)).astype(jnp.bfloat16)
    return high, rest


def band_matrix():
    row = lax.broadcasted_iota(jnp.int32, (256, 128), 0) % 128
    col = lax.broadcasted_iota(jnp.int32, (256, 128), 1)
    away = jnp.abs(row - col)
    band = jnp.zeros((256, 128), jnp.float32)
    for shift in range(1, 5):
        band = jnp.where(away == shift, INTEGER_COEFFS[shift - 1], band)
    return band.astype(jnp.bfloat16)


def laplace_tile(wave, first, band):
    center = wave[:, pl.ds(first, 8), :]
    layers = center.shape[0]
    high, rest = split_two(center.reshape(layers * 8, 128))
    depth = jnp.dot(
        jnp.concatenate([high, rest], axis=1), band, preferred_element_type=jnp.float32
    ).reshape(layers, 8, 128)
    total = 3.0 * CENTER * center + INTEGER_SCALE * depth
    for shift in range(1, 5):
        beside = wave[:, pl.ds(first + shift, 8), :] + wave[:, pl.ds(first - shift, 8), :]
        blank = jnp.zeros((shift, 8, 128), jnp.float32)
        beside = beside + jnp.concatenate([center[shift:], blank], axis=0)
        beside = beside + jnp.concatenate([blank, center[:-shift]], axis=0)
        total = total + COEFFS[shift - 1] * beside
    return center, total


def own_half(value, inline):
    return jnp.where(inline == 0, value[:OWN_X], value[OWN_X:])


def solve_rows(sums):
    entry = {}
    index = 0
    for k in range(TAPS):
        for l in range(k + 1):
            entry[k, l] = sums[index : index + 1]
            index += 1
    right = [sums[index + k : index + k + 1] for k in range(TAPS)]
    trace_sum = sum(entry[k, k] for k in range(TAPS))
    ridge = RIDGE_BASE + RIDGE_SHARE * trace_sum / TAPS
    for k in range(TAPS):
        entry[k, k] = entry[k, k] + ridge
    inverse = []
    for k in range(TAPS):
        inverse.append(1.0 / entry[k, k])
        factor = {i: entry[i, k] * inverse[k] for i in range(k + 1, TAPS)}
        for i in range(k + 1, TAPS):
            for l in range(k + 1, i + 1):
                entry[i, l] = entry[i, l] - factor[i] * entry[l, k]
            right[i] = right[i] - factor[i] * right[k]
        for i in range(k + 1, TAPS):
            entry[i, k] = factor[i]
    right = [right[k] * inverse[k] for k in range(TAPS)]
    for k in reversed(range(TAPS)):
        for i in range(k):
            right[i] = right[i] - entry[k, i] * right[k]
    return right


def tiles_of(step):
    first = 4 * (step + 1)
    return range(first, OWN_END + 4 * (HALF - 1 - step % HALF), 8)


def plan():
    first_half = [(s, f) for s in range(HALF) for f in tiles_of(s)]
    later = [(s, f) for s in range(HALF, STEPS) for f in tiles_of(s)]
    order, done = [], set()

    def ready(step, first, pieces, core, core_later):
        if Z_HALO - (first - 4 * (step + 1)) > 8 * pieces:
            return False
        reach = first + 8 + 4 * (step % HALF + 1)
        if reach > OWN_END and not (core if step < HALF else core_later):
            return False
        if step == 0:
            return True
        if step >= HALF and any(
            f + 8 > Z_HALO and f < OWN_END and (step - HALF, f) not in done
            for f in tiles_of(step - HALF)
        ):
            return False
        span = range(first - 4, first + 12)
        covered = {r for s, f in done if s == step - 1 for r in range(f, f + 8)}
        if step == HALF:
            return all(r in covered for r in span if r < OWN_END)
        return all(r in covered for r in span)

    def take(tiles, pieces, core, core_later):
        changed = True
        while changed:
            changed = False
            for step, first in tiles:
                if (step, first) not in done and ready(step, first, pieces, core, core_later):
                    done.add((step, first))
                    order.append(("tile", step, first))
                    changed = True

    both = first_half + later
    take(both, 0, False, False)
    order.append(("core", 0))
    take(both, 0, True, False)
    order.append(("piece", 0))
    take(first_half, 1, True, False)
    order.append(("middle",))
    take(both, 1, True, False)
    order.append(("core", 1))
    take(both, 1, True, True)
    for piece in range(1, 4):
        order.append(("piece", piece))
        take(both, piece + 1, True, True)
    assert len(done) == len(both)
    return order


def columns_of(first):
    return [c for c, (start, stop) in enumerate(SPANS) if first < stop and first + 8 > start]


def hit_slots():
    slots = {}
    for step in range(STEPS):
        for first in tiles_of(step):
            for column in columns_of(first):
                slots.setdefault((first, column), len(slots))
    return slots


def flip(block, index):
    return jnp.stack(
        [jnp.take_along_axis(block[i], index, axis=0) for i in range(block.shape[0])], axis=0
    )


def whole_kernel(
    rec_layer, rec_row, velocity, state_now, state_prev, notes, depth_mask, update,
    courant, wave, staged, staged_core, z_land, core_land, x_first, near_first, core_first,
    second_first, laplacians, picked, notes_all, traces, traces_all, sums_own, sums_all, turned,
    model, synthetic, products, filters, misfit, strengths, hits, places, gradient, gradient_own,
    gradient_other, start_send, start_recv, z_send, z_recv, core_send, core_recv, note_send,
    note_recv, trace_send, trace_recv, sum_send, sum_recv, pair_send, pair_recv,
):
    inline, xline, particle = (lax.axis_index(a) for a in ("inline", "xline", "particle"))
    count = lax.axis_size("xline")
    size = 2 * count
    me = inline * count + xline
    receivers = rec_row.shape[0]
    odd = lax.rem(xline, 2)
    toward = 1 - 2 * odd
    other = 1 - inline
    near, core = xline - toward, xline + toward
    second_in, second_out = xline - 2 * toward, xline + 2 * toward
    has_near = (near >= 0) & (near < count)
    has_in = (second_in >= 0) & (second_in < count)
    has_out = (second_out >= 0) & (second_out < count)
    always = xline >= 0
    sources = (state_now, state_prev, velocity)
    frames = (wave.at[0], wave.at[1], courant)
    sublane = lax.broadcasted_iota(jnp.int32, (8, 128), 0)
    backward_rows = 7 - sublane
    own_rows = jnp.where(odd == 1, 7 - sublane, sublane)

    barrier = pltpu.get_barrier_semaphore()

    def greet(step, carry):
        peer = lax.rem(me + step, size)
        pl.semaphore_signal(
            barrier, inc=1, device_id=(peer // count, lax.rem(peer, count), particle),
            device_id_type=MESH,
        )
        return carry

    lax.fori_loop(1, size, greet, 0)
    pl.semaphore_signal(
        barrier, inc=1, device_id=(inline, xline, 1 - particle), device_id_type=MESH
    )

    layers = pl.ds(inline * OWN_X, OWN_X)
    layers_other = pl.ds(other * OWN_X, OWN_X)

    def own_block(index):
        return pl.multiple_of(8 * (index + odd * (2 - 2 * index)), 8)

    for kind in range(3):
        for index in range(3):
            frames[kind][layers, pl.ds(Z_HALO + 8 * index, 8), :] = flip(
                sources[kind][0, :, pl.ds(own_block(index), 8), :], own_rows
            )

    @pl.when(jnp.logical_not(has_near))
    def _():
        for frame in frames:
            frame[:, pl.ds(8, Z_HALO - 8), :] = jnp.zeros((2 * OWN_X, Z_HALO - 8, 128), jnp.float32)
        notes_all[NEAR] = jnp.zeros(notes_all.shape[1:], jnp.float32)
        traces_all[NEAR] = jnp.zeros(traces_all.shape[1:], jnp.float32)

    @pl.when(jnp.logical_not(has_in))
    def _():
        for frame in frames:
            frame[:, pl.ds(0, 8), :] = jnp.zeros((2 * OWN_X, 8, 128), jnp.float32)
        notes_all[SECOND] = jnp.zeros(notes_all.shape[1:], jnp.float32)
        traces_all[SECOND] = jnp.zeros(traces_all.shape[1:], jnp.float32)

    notes_all[OWN, inline] = notes[...]
    picked[:, pl.ds(other * receivers, receivers), :] = jnp.zeros(
        (NT, receivers, 128), jnp.float32
    )
    pl.semaphore_wait(barrier, size)

    routes = [
        (always, always, (other, xline, particle), OWN),
        (always, always, (inline, core, particle), CORE),
        (always, always, (other, core, particle), CORE),
        (has_near, has_near, (inline, near, particle), NEAR),
        (has_near, has_near, (other, near, particle), NEAR),
        (has_out, has_in, (inline, second_out, particle), SECOND),
        (has_out, has_in, (other, second_out, particle), SECOND),
    ]
    origins = (other, inline, other, inline, other, inline, other)

    def remote(source, target, send, recv, device):
        return pltpu.make_async_remote_copy(
            src_ref=source, dst_ref=target, send_sem=send, recv_sem=recv, device_id=device,
            device_id_type=MESH,
        )

    def start_copy(index, kind, origin):
        column = routes[index][3]
        if column == OWN:
            first, extent, landing = 0, OWN_Y, x_first.at[kind]
        elif column == NEAR:
            first, extent, landing = 0, OWN_Y, near_first.at[kind, origin]
        elif column == CORE:
            first, extent, landing = 8 * (1 - odd), CORE_HALO, core_first.at[kind, origin]
        else:
            first, extent, landing = 16 * (1 - odd), 8, second_first.at[kind, origin]
        first = first if isinstance(first, int) else pl.multiple_of(first, 8)
        return remote(
            sources[kind].at[0, :, pl.ds(first, extent), :], landing, start_send.at[index, kind],
            start_recv.at[index, kind], routes[index][2],
        )

    for index in range(7):
        for kind in range(3):

            @pl.when(routes[index][0])
            def _():
                start_copy(index, kind, inline).start()

    def pair_copy(source, target, index):
        return remote(
            source, target, pair_send.at[index], pair_recv.at[index], (inline, xline, 1 - particle)
        )

    pair_copy(velocity.at[0], model, 0).start()

    def share(source, table, send, recv, origin, index):
        return remote(
            source, table.at[routes[index][3], origin], send.at[index], recv.at[index],
            routes[index][2],
        )

    def share_start(source, table, send, recv):
        for index in range(7):

            @pl.when(routes[index][0])
            def _():
                share(source, table, send, recv, inline, index).start()

    def share_wait(source, table, send, recv):
        for index in range(7):

            @pl.when(routes[index][0])
            def _():
                share(source, table, send, recv, inline, index).wait_send()

            @pl.when(routes[index][1])
            def _():
                share(source, table, send, recv, origins[index], index).wait_recv()

    share_start(notes, notes_all, note_send, note_recv)

    for index in range(7):
        column = routes[index][3]
        origin = origins[index]
        there = pl.ds(origin * OWN_X, OWN_X)
        for kind in range(3):

            @pl.when(routes[index][0])
            def _():
                start_copy(index, kind, inline).wait_send()

            @pl.when(routes[index][1])
            def _():
                start_copy(index, kind, origin).wait_recv()
                if column == OWN:
                    for block in range(3):
                        frames[kind][there, pl.ds(Z_HALO + 8 * block, 8), :] = flip(
                            x_first[kind, :, pl.ds(own_block(block), 8), :], own_rows
                        )
                elif column == NEAR:
                    for block in range(3):
                        frames[kind][there, pl.ds(8 + 8 * block, 8), :] = flip(
                            near_first[kind, origin, :, pl.ds(own_block(block), 8), :], own_rows
                        )
                elif column == CORE:
                    for block in range(2):
                        at = pl.multiple_of(8 * (block + odd * (1 - 2 * block)), 8)
                        frames[kind][there, pl.ds(OWN_END + 8 * block, 8), :] = flip(
                            core_first[kind, origin, :, pl.ds(at, 8), :], own_rows
                        )
                else:
                    frames[kind][there, pl.ds(0, 8), :] = flip(
                        second_first[kind, origin], own_rows
                    )

    band = band_matrix()
    ones = jnp.ones((8, 256), jnp.bfloat16)
    ordered = plan()

    def z_copies(slot):
        to_near, to_second = (inline, near, particle), (inline, second_out, particle)
        blocks = [
            (wave.at[0, :, pl.ds(Z_HALO, 8), :], 0, to_near),
            (staged.at[0], 1, to_near),
            (staged.at[2], 2, to_near),
            (staged.at[1], 3, to_near),
            (staged.at[3], 4, to_near),
            (staged.at[1], 5, to_second),
            (staged.at[4], 6, to_near),
        ]
        return [
            remote(source, z_land.at[slot, i], z_send.at[slot, i], z_recv.at[slot, i], target)
            for source, i, target in blocks
        ]

    def core_copies(slot, blocks):
        return [
            remote(
                block, core_land.at[slot, i], core_send.at[slot, i], core_recv.at[slot, i],
                (inline, core, particle),
            )
            for i, block in enumerate(blocks)
        ]

    z_valid = [has_near] * 5 + [has_out, has_near]
    z_arrives = [has_near] * 5 + [has_in, has_near]
    z_place = [(0, 24), (0, 16), (1, 20), (0, 8), (1, 12), (0, 0), (1, 4)]
    pieces = ((0,), (1, 2), (3, 4), (5, 6))
    core_place = [(0, OWN_END), (0, OWN_END + 8), (1, OWN_END + 4)]

    def send_round(slot):
        copies = z_copies(slot)
        staged[0] = wave[0, :, pl.ds(40, 8), :]
        staged[1] = wave[0, :, pl.ds(48, 8), :]
        staged[2] = wave[1, :, pl.ds(36, 8), :]
        staged[3] = wave[1, :, pl.ds(44, 8), :]
        staged[4] = wave[1, :, pl.ds(52, 8), :]
        for i in range(7):
            pl.when(z_valid[i])(copies[i].start)
        for copy in core_copies(slot, round_blocks):
            copy.start()

    round_blocks = [staged.at[1], staged.at[0], staged.at[3]]
    middle_blocks = [staged_core.at[i] for i in range(3)]

    def send_middle(slot):
        staged_core[0] = wave[0, :, pl.ds(48, 8), :]
        staged_core[1] = wave[0, :, pl.ds(40, 8), :]
        staged_core[2] = wave[1, :, pl.ds(44, 8), :]
        for copy in core_copies(slot, middle_blocks):
            copy.start()

    def take_core(slot, blocks):
        for i, copy in enumerate(core_copies(slot, blocks)):
            copy.wait()
            level, row = core_place[i]
            wave[level, :, pl.ds(row, 8), :] = flip(core_land[slot, i], backward_rows)

    def take_piece(slot, piece):
        copies = z_copies(slot)
        for i in pieces[piece]:
            pl.when(z_valid[i])(copies[i].wait_send)

            @pl.when(z_arrives[i])
            def _():
                copies[i].wait_recv()
                level, row = z_place[i]
                block = z_land[slot, i]
                if i != 5:
                    block = flip(block, backward_rows)
                wave[level, :, pl.ds(row, 8), :] = block

    rounds = NT // STEPS

    def run_round(number, sweep, tile):
        taken = sweep * (rounds - 1) + number - 1
        middle = 2 * (rounds - 1) + sweep * rounds + number
        for entry in ordered:
            if entry[0] == "tile":
                tile(entry[1], entry[2])
            elif entry[0] == "middle":
                send_middle(middle)
            elif entry[0] == "piece":

                @pl.when(number > 0)
                def _():
                    take_piece(taken, entry[1])
            elif entry[1] == 0:

                @pl.when(number > 0)
                def _():
                    take_core(taken, round_blocks)
            else:
                take_core(middle, middle_blocks)

        @pl.when(number < rounds - 1)
        def _():
            send_round(taken + 1)

    def keep_lines(time, level):
        new = wave.at[level]
        for group in range(0, receivers, 16):
            lines = [
                new[inline * OWN_X + rec_layer[r], pl.ds(rec_row[r], 1), :]
                for r in range(group, group + 16)
            ]
            for offset, line in enumerate(lines):
                picked[time, pl.ds(inline * receivers + group + offset, 1), :] = line

    def read_traces(first_time, steps):
        for step in range(steps):
            time = first_time + step
            high, rest = split_two(picked[time] * depth_mask[...])
            row = lax.dot_general(
                ones, jnp.concatenate([high, rest], axis=1), (((1,), (1,)), ((), ())),
                preferred_element_type=jnp.float32,
            )
            traces[pl.ds(time, 1), :] = row[0:1]

    own_tiles = {s: {f for f in tiles_of(s) if f + 8 > Z_HALO and f < OWN_END} for s in range(STEPS)}

    def forward_round(number, carry):
        left = [set(own_tiles[s]) for s in range(STEPS)]

        @pl.when(number > 0)
        def _():
            for step in range(HALF, STEPS):
                keep_lines((number - 1) * STEPS + step, LEVELS[step % 4][2])
            read_traces((number - 1) * STEPS + HALF, HALF)

        def tile(step, first):
            now, old, new = (wave.at[level] for level in LEVELS[step % 4])
            time = number * STEPS + step
            center, laplacian = laplace_tile(now, first, band)
            here = pl.ds(first, 8)
            new[:, here, :] = 2.0 * center - old[:, here, :] + courant[:, here, :] * laplacian
            if first in own_tiles[step]:
                laplacians[time, :, pl.ds(first - Z_HALO + 8, 8), :] = own_half(laplacian, inline)
                left[step].discard(first)
                if step < HALF and not left[step]:
                    keep_lines(time, LEVELS[step % 4][2])

        run_round(number, 0, tile)
        read_traces(number * STEPS, HALF)
        return carry

    lax.fori_loop(0, rounds, forward_round, 0)
    for step in range(HALF, STEPS):
        keep_lines(NT - STEPS + step, LEVELS[step % 4][2])
    read_traces(NT - HALF, HALF)
    traces_all[OWN, inline] = traces[...]
    share_start(traces, traces_all, trace_send, trace_recv)

    keys = lax.broadcasted_iota(jnp.int32, (128, 128), 0)
    synthetic[...] = jnp.zeros(synthetic.shape, jnp.float32)
    products[...] = jnp.zeros(products.shape, jnp.float32)
    synthetic[OWN, pl.ds(8, NT), :] = traces[pl.ds(0, NT), :]
    lagged = [synthetic[OWN, pl.ds(8 - k, NT), :] for k in range(TAPS)]
    recorded = notes[pl.ds(0, NT), :]
    index = 0
    for k in range(TAPS):
        for l in range(k + 1):
            products[pl.ds(index, 1), :] = jnp.sum(lagged[k] * lagged[l], axis=0, keepdims=True)
            index += 1
    for k in range(TAPS):
        products[pl.ds(index + k, 1), :] = jnp.sum(lagged[k] * recorded, axis=0, keepdims=True)
    own_key = notes[pl.ds(NT + 3, 1), :].astype(jnp.int32) - inline * KEYS
    local = (keys[:KEYS] == own_key).astype(jnp.float32)
    partial = lax.dot_general(
        local, products[...], (((1,), (1,)), ((), ())),
        preferred_element_type=jnp.float32, precision=HIGHEST,
    )
    pair_copy(velocity.at[0], model, 0).wait()
    apart = jnp.sum(jnp.square(velocity[0] - model[...]), axis=0)
    apart = apart[0:8] + apart[8:16] + apart[16:24]
    lane = lax.broadcasted_iota(jnp.int32, (8, 128), 1)
    partial = jnp.where(lane == 127, jnp.sum(apart, axis=1, keepdims=True), partial)
    sums_own[...] = partial
    sums_all[me] = partial

    def sum_copy(step, peer):
        sender = lax.rem(me + size - step, size)
        return remote(
            sums_own, sums_all.at[me if peer else sender], sum_send.at[step], sum_recv.at[step],
            (
                lax.rem(me + step, size) // count if peer else sender // count,
                lax.rem(me + step if peer else sender, count),
                particle,
            ),
        )

    def sum_start(step, carry):
        sum_copy(step, True).start()
        return carry

    lax.fori_loop(1, size, sum_start, 0)

    share_wait(notes, notes_all, note_send, note_recv)
    for column in range(4):
        pair = notes_all[column, 0] + notes_all[column, 1]
        place_row = pair[NT + 1 : NT + 2].astype(jnp.int32)
        frame_row = (place_row - 16, 31 - place_row, Z_HALO + place_row, OWN_END + 23 - place_row)[
            column
        ]
        depth = pair[NT + 2 : NT + 3].astype(jnp.int32)
        fits = (frame_row >= 0) & (frame_row < ROWS)
        row_id = jnp.where(fits, pair[NT : NT + 1].astype(jnp.int32) + frame_row, -1)
        place = (keys == depth).astype(jnp.float32).astype(jnp.bfloat16)
        places[:, pl.ds(256 * column, 128)] = place
        places[:, pl.ds(256 * column + 128, 128)] = place
        for (first, found), slot in hit_slots().items():
            if found == column:
                wanted = (keys // 8) * ROWS + first + lax.rem(keys, 8)
                hit = (wanted == row_id).astype(jnp.float32).astype(jnp.bfloat16)
                hits[slot, :, pl.ds(0, 128)] = hit
                hits[slot, :, pl.ds(128, 128)] = hit
    wave[...] = jnp.zeros(wave.shape, jnp.float32)
    gradient[...] = jnp.zeros(gradient.shape, jnp.float32)
    misfit[...] = jnp.zeros(misfit.shape, jnp.float32)
    turned[...] = jnp.zeros(turned.shape, jnp.float32)

    def sum_wait(step, carry):
        sum_copy(step, True).wait_send()
        sum_copy(step, False).wait_recv()
        return carry

    lax.fori_loop(1, size, sum_wait, 0)
    total = [jnp.zeros((8, 128), jnp.float32) for i in range(2)]
    for row in range(2):
        for column in range(count):
            total[row] = total[row] + sums_all[row * count + column]
        turned[pl.ds(KEYS * row, KEYS), :] = total[row]
    sums = jnp.transpose(turned[...])
    for k, row in enumerate(solve_rows(sums[:48])):
        filters[pl.ds(k, 1), :] = row

    share_wait(traces, traces_all, trace_send, trace_recv)
    for column in range(4):
        both = traces_all[column, 0] + traces_all[column, 1]
        synthetic[column, pl.ds(8, NT), :] = both[:NT]
        pair = notes_all[column, 0] + notes_all[column, 1]
        members = (keys == pair[NT + 3 : NT + 4].astype(jnp.int32)).astype(jnp.float32)
        own = jnp.dot(
            filters[...], members, preferred_element_type=jnp.float32, precision=HIGHEST
        )
        fitted = sum(own[k : k + 1] * synthetic[column, pl.ds(8 - k, NT), :] for k in range(TAPS))
        misfit[column, pl.ds(0, NT), :] = fitted - pair[:NT]
        source = sum(own[k : k + 1] * misfit[column, pl.ds(k, NT), :] for k in range(TAPS))
        high, rest = split_two(source)
        strengths[:, pl.ds(256 * column, 128)] = high.astype(jnp.float32)
        strengths[:, pl.ds(256 * column + 128, 128)] = rest.astype(jnp.float32)

    slots = hit_slots()

    def backward_round(number, carry):
        def tile(step, first):
            now, old, new = (wave.at[level] for level in LEVELS[step % 4])
            time = NT - 1 - (number * STEPS + step)
            strength = strengths[pl.ds(time, 1), :].astype(jnp.bfloat16)
            center, laplacian = laplace_tile(now, first, band)
            here = pl.ds(first, 8)
            added = 0.0
            for column in columns_of(first):
                part = slice(256 * column, 256 * (column + 1))
                added = added + lax.dot_general(
                    hits[slots[first, column]] * strength[:, part],
                    places[:, part],
                    (((1,), (1,)), ((), ())),
                    preferred_element_type=jnp.float32,
                )
            following = 2.0 * center - old[:, here, :] + courant[:, here, :] * laplacian
            following = following + added.reshape(2 * OWN_X, 8, 128)
            new[:, here, :] = following
            if first in own_tiles[step]:
                kept = pl.ds(first - Z_HALO + 8, 8)
                gradient[:, kept, :] = (
                    gradient[:, kept, :]
                    + own_half(following, inline) * laplacians[time, :, kept, :]
                )

        run_round(number, 1, tile)
        return carry

    lax.fori_loop(0, rounds, backward_round, 0)
    for index in range(3):
        gradient_own[:, pl.ds(own_block(index), 8), :] = flip(
            gradient[:, pl.ds(8 + 8 * index, 8), :] * (1.0 / NT), own_rows
        )
    pair_copy(gradient_own, gradient_other, 1).start()
    apart = jnp.where(lane == 127, total[0] + total[1], 0.0)
    apart = jnp.sum(jnp.sum(apart, axis=0, keepdims=True), axis=1, keepdims=True)
    distance = apart / (size * OWN_X * OWN_Y * 128)
    weight = jnp.exp(jnp.broadcast_to(-distance / KERNEL_WIDTH, (8, 128)))[0:1]
    between = 2.0 * (velocity[0] - model[...]) / KERNEL_WIDTH
    pair_copy(gradient_own, gradient_other, 1).wait()
    own_term = gradient_own[...] * (-1.0 / NOISE_VARIANCE)
    other_term = gradient_other[...] * (-1.0 / NOISE_VARIANCE) + between
    update[0] = (STEP_SIZE / 2) * (own_term + weight[None] * other_term)


def per_device_pair(velocity, state_now, state_prev, observed, rec_cell, rec_gather):
    inline, xline = lax.axis_index("inline"), lax.axis_index("xline")
    count = rec_cell.shape[0]
    size = 2 * lax.axis_size("xline")
    line = rec_cell // 128
    layer, local_row = line // OWN_Y, line % OWN_Y
    place = jnp.where(xline % 2 == 1, OWN_Y - 1 - local_row, local_row)
    facts = jnp.stack(
        [
            (inline * OWN_X + layer) * ROWS,
            place,
            rec_cell % 128,
            inline * KEYS + rec_gather[:, 0],
        ]
    ).astype(jnp.float32)
    notes = jnp.concatenate([observed.T, facts, jnp.zeros((4, count), jnp.float32)], axis=0)
    blank = jnp.zeros_like(notes)
    first = inline == 0
    notes = jnp.concatenate([jnp.where(first, notes, blank), jnp.where(first, blank, notes)], axis=1)
    lanes = jnp.arange(128, dtype=jnp.int32)[None, :]
    depth_mask = ((rec_cell % 128)[:, None] == lanes).astype(jnp.float32)
    depth_mask = jnp.concatenate([depth_mask, depth_mask], axis=0)
    vmem = pl.BlockSpec(memory_space=pltpu.VMEM)
    smem = pl.BlockSpec(memory_space=pltpu.SMEM)
    f32, bf16 = jnp.float32, jnp.bfloat16
    dma = pltpu.SemaphoreType.DMA
    exchanges = 2 * (NT // STEPS - 1)
    halves = exchanges + 2 * (NT // STEPS)
    return pl.pallas_call(
        whole_kernel,
        out_shape=jax.ShapeDtypeStruct(velocity.shape, f32),
        in_specs=[smem, smem] + [vmem] * 5,
        out_specs=vmem,
        scratch_shapes=[
            pltpu.VMEM((2 * OWN_X, ROWS, 128), f32),
            pltpu.VMEM((4, 2 * OWN_X, ROWS, 128), f32),
            pltpu.VMEM((5, 2 * OWN_X, 8, 128), f32),
            pltpu.VMEM((3, 2 * OWN_X, 8, 128), f32),
            pltpu.VMEM((exchanges, 7, 2 * OWN_X, 8, 128), f32),
            pltpu.VMEM((halves, 3, 2 * OWN_X, 8, 128), f32),
            pltpu.VMEM((3, OWN_X, OWN_Y, 128), f32),
            pltpu.VMEM((3, 2, OWN_X, OWN_Y, 128), f32),
            pltpu.VMEM((3, 2, OWN_X, CORE_HALO, 128), f32),
            pltpu.VMEM((3, 2, OWN_X, 8, 128), f32),
            pltpu.VMEM((NT, OWN_X, OWN_Y + 16, 128), f32),
            pltpu.VMEM((NT, 2 * count, 128), f32),
            pltpu.VMEM((4, 2, NT + 8, 128), f32),
            pltpu.VMEM((NT, 128), f32),
            pltpu.VMEM((4, 2, NT, 128), f32),
            pltpu.VMEM((8, 128), f32),
            pltpu.VMEM((size, 8, 128), f32),
            pltpu.VMEM((128, 128), f32),
            pltpu.VMEM((OWN_X, OWN_Y, 128), f32),
            pltpu.VMEM((4, NT + 8, 128), f32),
            pltpu.VMEM((128, 128), f32),
            pltpu.VMEM((8, 128), f32),
            pltpu.VMEM((4, NT + 8, 128), f32),
            pltpu.VMEM((NT, 1024), f32),
            pltpu.VMEM((len(hit_slots()), 128, 256), bf16),
            pltpu.VMEM((128, 1024), bf16),
            pltpu.VMEM((OWN_X, OWN_Y + 16, 128), f32),
            pltpu.VMEM((OWN_X, OWN_Y, 128), f32),
            pltpu.VMEM((OWN_X, OWN_Y, 128), f32),
            dma((7, 3)),
            dma((7, 3)),
            dma((exchanges, 7)),
            dma((exchanges, 7)),
            dma((halves, 3)),
            dma((halves, 3)),
            dma((7,)),
            dma((7,)),
            dma((7,)),
            dma((7,)),
            dma((size,)),
            dma((size,)),
            dma((2,)),
            dma((2,)),
        ],
        compiler_params=pltpu.CompilerParams(
            collective_id=0, has_side_effects=True, vmem_limit_bytes=48 * 1024 * 1024
        ),
        name="inversion_window",
    )(layer, place + Z_HALO, velocity, state_now, state_prev, notes, depth_mask)


def solution(mesh):
    shape = mesh.shape
    paired = (shape["inline"], shape["particle"]) == (2, 2) and shape["xline"] in (2, 4, 6, 8)
    return jax.shard_map(
        per_device_pair if paired else per_device,
        mesh=mesh,
        in_specs=(
            P("particle", "inline", "xline", None),
            P("particle", "inline", "xline", None),
            P("particle", "inline", "xline", None),
            P(("inline", "xline"), None),
            P(("inline", "xline")),
            P(("inline", "xline"), None),
        ),
        out_specs=P("particle", "inline", "xline", None),
        check_vma=False,
    )
```

```python
import jax
import jax.numpy as jnp
from jax import lax
from jax.experimental import pallas as pl
from jax.experimental.pallas import tpu as pltpu
from jax.sharding import PartitionSpec as P

NT = 32
CAP = 16
TAPS = 8


COEFFS = (8.0 / 5.0, -1.0 / 5.0, 8.0 / 315.0, -1.0 / 560.0)
CENTER = -205.0 / 72.0
KERNEL_WIDTH = 0.004
NOISE_VARIANCE = 0.0005
STEP_SIZE = 0.01
RIDGE_BASE = 1.0
RIDGE_SHARE = 0.1
HIGHEST = lax.Precision.HIGHEST


def extended(block, sides, width):
    for axis, dim in sides:
        count = lax.axis_size(axis)
        forward = [(i, i + 1) for i in range(count - 1)]
        backward = [(target, source) for source, target in forward]
        low = lax.ppermute(
            lax.slice_in_dim(block, block.shape[dim] - width, None, axis=dim), axis, forward
        )
        high = lax.ppermute(lax.slice_in_dim(block, 0, width, axis=dim), axis, backward)
        block = jnp.concatenate([low, block, high], axis=dim)
    return block


def laplace_inner(block):
    size_x, size_y, size_z = block.shape
    inner_x = size_x - 8
    inner_y = size_y - 8
    padded = jnp.pad(block, ((0, 0), (0, 0), (4, 4)))
    total = 3.0 * CENTER * block[4 : 4 + inner_x, 4 : 4 + inner_y, :]
    for shift in range(1, 5):
        weight = COEFFS[shift - 1]
        beside = padded[4 + shift : 4 + shift + inner_x, 4 : 4 + inner_y, 4 : 4 + size_z]
        beside = beside + padded[4 - shift : 4 - shift + inner_x, 4 : 4 + inner_y, 4 : 4 + size_z]
        beside = beside + padded[4 : 4 + inner_x, 4 + shift : 4 + shift + inner_y, 4 : 4 + size_z]
        beside = beside + padded[4 : 4 + inner_x, 4 - shift : 4 - shift + inner_y, 4 : 4 + size_z]
        beside = beside + padded[4 : 4 + inner_x, 4 : 4 + inner_y, 4 + shift : 4 + shift + size_z]
        beside = beside + padded[4 : 4 + inner_x, 4 : 4 + inner_y, 4 - shift : 4 - shift + size_z]
        total = total + weight * beside
    return total


def lagged_traces(traces):
    steps = traces.shape[1]
    padded = jnp.pad(traces, ((0, 0), (TAPS - 1, 0)))
    return jnp.stack(
        [padded[:, TAPS - 1 - shift : TAPS - 1 - shift + steps] for shift in range(TAPS)], axis=1
    )


def filter_stats(lagged, observed):
    count = lagged.shape[0]
    gram = jnp.einsum("mkt,mlt->mkl", lagged, lagged, precision=HIGHEST).reshape(count, TAPS * TAPS)
    cross = jnp.einsum("mkt,mt->mk", lagged, observed, precision=HIGHEST)
    return (gram, cross)


def solve_filter(gram, cross):
    matrix = gram.reshape(-1, TAPS, TAPS)
    sums = [matrix[:, k, l] for k in range(TAPS) for l in range(k + 1)]
    sums = jnp.stack(sums + [cross[:, k] for k in range(TAPS)])
    return jnp.concatenate(solve_rows(sums), axis=0).T


def adjoint_sources(lagged, observed, filters):
    steps = observed.shape[1]
    fitted = jnp.einsum("mk,mkt->mt", filters, lagged, precision=HIGHEST)
    misfit = fitted - observed
    padded = jnp.pad(misfit, ((0, 0), (0, TAPS - 1)))
    ahead = jnp.stack([padded[:, shift : shift + steps] for shift in range(TAPS)], axis=1)
    return jnp.einsum("mk,mkt->mt", filters, ahead, precision=HIGHEST)


def per_device(velocity, state_now, state_prev, observed, rec_cell, rec_gather):
    courant = velocity[0]
    particles = lax.axis_size("particle")
    models = lax.all_gather(velocity, "particle", axis=0, tiled=True)
    partial_sums = jnp.sum(jnp.square(models - velocity), axis=(1, 2, 3))
    cells_all = courant.size * lax.axis_size("inline") * lax.axis_size("xline")
    distance = lax.psum(partial_sums, ("inline", "xline")) / cells_all
    kernel = jnp.exp(-distance / KERNEL_WIDTH)

    def advance(carry, unused):
        current, previous = carry
        padded = extended(current[None], (("inline", 1), ("xline", 2)), 4)[0]
        laplacian = laplace_inner(padded)
        following = 2.0 * current - previous + courant * laplacian
        return ((following, current), (laplacian, following.reshape(-1)[rec_cell]))

    unused, (laplacians, traces) = lax.scan(advance, (state_now[0], state_prev[0]), None, length=NT)
    synthetic = traces.T
    steps = observed.shape[1]
    xline_count = lax.axis_size("xline")
    target = rec_gather[:, 0]
    choose = (target[:, None] == jnp.arange(xline_count, dtype=jnp.int32)[None, :]).astype(
        jnp.int32
    )
    order = jnp.arange(target.shape[0], dtype=jnp.int32)
    earlier = (order[None, :] < order[:, None]).astype(jnp.float32)
    before = jnp.dot(earlier, choose.astype(jnp.float32), precision=HIGHEST).astype(jnp.int32)
    position = target * CAP + jnp.sum(before * choose, axis=1)
    outgoing = jnp.zeros((xline_count * CAP, 2 * steps), jnp.float32)
    outgoing = outgoing.at[position].set(jnp.concatenate([synthetic, observed], axis=1))
    arrived = lax.all_to_all(
        outgoing.reshape(xline_count, CAP, 2 * steps),
        "xline",
        split_axis=0,
        concat_axis=0,
        tiled=True,
    )
    slots = arrived.reshape(xline_count * CAP, 2 * steps)
    slot_lagged = lagged_traces(slots[:, :steps])
    slot_observed = slots[:, steps:]
    gram, cross = filter_stats(slot_lagged, slot_observed)
    filters_one = solve_filter(
        jnp.sum(gram, axis=0, keepdims=True), jnp.sum(cross, axis=0, keepdims=True)
    )
    filters = jnp.broadcast_to(filters_one, (slots.shape[0], TAPS))
    slot_adjoint = adjoint_sources(slot_lagged, slot_observed, filters)
    returned = lax.all_to_all(
        slot_adjoint.reshape(xline_count, CAP, steps),
        "xline",
        split_axis=0,
        concat_axis=0,
        tiled=True,
    )
    adjoint_source = returned.reshape(xline_count * CAP, steps)[position]

    def backward(carry, inputs):
        wave, wave_old, gradient = carry
        laplacian, source = inputs
        padded = extended(wave[None], (("inline", 1), ("xline", 2)), 4)[0]
        wave_new = 2.0 * wave - wave_old + courant * laplace_inner(padded)
        wave_new = wave_new.reshape(-1).at[rec_cell].add(source).reshape(wave.shape)
        return ((wave_new, wave, gradient + wave_new * laplacian), None)

    zeros_field = jnp.zeros(courant.shape, jnp.float32)
    (wave, wave_old, gradient), unused = lax.scan(
        backward,
        (zeros_field, zeros_field, zeros_field),
        (laplacians, adjoint_source.T),
        reverse=True,
    )
    gradient = gradient / NT
    gradients = lax.all_gather(gradient[None], "particle", axis=0, tiled=True)
    terms = -gradients / NOISE_VARIANCE + 2.0 * (velocity - models) / KERNEL_WIDTH
    update = (
        STEP_SIZE / particles * jnp.sum(kernel[:, None, None, None] * terms, axis=0, keepdims=True)
    )
    return update


STEPS = 8
HALF = 4
Z_HALO = 4 * STEPS
CORE_HALO = 4 * HALF
OWN_X = 8
OWN_Y = Z_HALO - 8
OWN_END = Z_HALO + OWN_Y
ROWS = OWN_END + CORE_HALO
KEYS = 8
INTEGER_COEFFS = (8064.0, -1008.0, 128.0, -9.0)
INTEGER_SCALE = 1.0 / 5040.0
LEVELS = ((0, 1, 2), (2, 0, 3), (3, 2, 1), (1, 3, 0))
MESH = pl.DeviceIdType.MESH
SECOND, NEAR, OWN, CORE = range(4)
SPANS = ((0, 8), (8, Z_HALO), (Z_HALO, OWN_END), (OWN_END, ROWS))


def split_two(value):
    high = value.astype(jnp.bfloat16)
    rest = (value - high.astype(jnp.float32)).astype(jnp.bfloat16)
    return high, rest


def band_matrix():
    row = lax.broadcasted_iota(jnp.int32, (256, 128), 0) % 128
    col = lax.broadcasted_iota(jnp.int32, (256, 128), 1)
    away = jnp.abs(row - col)
    band = jnp.zeros((256, 128), jnp.float32)
    for shift in range(1, 5):
        band = jnp.where(away == shift, INTEGER_COEFFS[shift - 1], band)
    return band.astype(jnp.bfloat16)


def laplace_tile(wave, first, band):
    center = wave[:, pl.ds(first, 8), :]
    layers = center.shape[0]
    high, rest = split_two(center.reshape(layers * 8, 128))
    depth = jnp.dot(
        jnp.concatenate([high, rest], axis=1), band, preferred_element_type=jnp.float32
    ).reshape(layers, 8, 128)
    total = 3.0 * CENTER * center + INTEGER_SCALE * depth
    for shift in range(1, 5):
        beside = wave[:, pl.ds(first + shift, 8), :] + wave[:, pl.ds(first - shift, 8), :]
        blank = jnp.zeros((shift, 8, 128), jnp.float32)
        beside = beside + jnp.concatenate([center[shift:], blank], axis=0)
        beside = beside + jnp.concatenate([blank, center[:-shift]], axis=0)
        total = total + COEFFS[shift - 1] * beside
    return center, total


def own_half(value, inline):
    return jnp.where(inline == 0, value[:OWN_X], value[OWN_X:])


def solve_rows(sums):
    entry = {}
    index = 0
    for k in range(TAPS):
        for l in range(k + 1):
            entry[k, l] = sums[index : index + 1]
            index += 1
    right = [sums[index + k : index + k + 1] for k in range(TAPS)]
    trace_sum = sum(entry[k, k] for k in range(TAPS))
    ridge = RIDGE_BASE + RIDGE_SHARE * trace_sum / TAPS
    for k in range(TAPS):
        entry[k, k] = entry[k, k] + ridge
    inverse = []
    for k in range(TAPS):
        inverse.append(1.0 / entry[k, k])
        factor = {i: entry[i, k] * inverse[k] for i in range(k + 1, TAPS)}
        for i in range(k + 1, TAPS):
            for l in range(k + 1, i + 1):
                entry[i, l] = entry[i, l] - factor[i] * entry[l, k]
            right[i] = right[i] - factor[i] * right[k]
        for i in range(k + 1, TAPS):
            entry[i, k] = factor[i]
    right = [right[k] * inverse[k] for k in range(TAPS)]
    for k in reversed(range(TAPS)):
        for i in range(k):
            right[i] = right[i] - entry[k, i] * right[k]
    return right


def tiles_of(step):
    first = 4 * (step + 1)
    return range(first, OWN_END + 4 * (HALF - 1 - step % HALF), 8)


def plan():
    first_half = [(s, f) for s in range(HALF) for f in tiles_of(s)]
    later = [(s, f) for s in range(HALF, STEPS) for f in tiles_of(s)]
    order, done = [], set()

    def ready(step, first, pieces, core, core_later):
        if Z_HALO - (first - 4 * (step + 1)) > 8 * pieces:
            return False
        reach = first + 8 + 4 * (step % HALF + 1)
        if reach > OWN_END and not (core if step < HALF else core_later):
            return False
        if step == 0:
            return True
        if step >= HALF and any(
            f + 8 > Z_HALO and f < OWN_END and (step - HALF, f) not in done
            for f in tiles_of(step - HALF)
        ):
            return False
        span = range(first - 4, first + 12)
        covered = {r for s, f in done if s == step - 1 for r in range(f, f + 8)}
        if step == HALF:
            return all(r in covered for r in span if r < OWN_END)
        return all(r in covered for r in span)

    def take(tiles, pieces, core, core_later):
        changed = True
        while changed:
            changed = False
            for step, first in tiles:
                if (step, first) not in done and ready(step, first, pieces, core, core_later):
                    done.add((step, first))
                    order.append(("tile", step, first))
                    changed = True

    both = first_half + later
    take(both, 0, False, False)
    order.append(("core", 0))
    take(both, 0, True, False)
    order.append(("piece", 0))
    take(first_half, 1, True, False)
    order.append(("middle",))
    take(both, 1, True, False)
    order.append(("piece", 1))
    take(both, 2, True, False)
    order.append(("core", 1))
    take(both, 2, True, True)
    order.append(("piece", 2))
    take(both, 3, True, True)
    order.append(("early",))
    order.append(("piece", 3))
    take(both, 4, True, True)
    assert len(done) == len(both)
    return order


def columns_of(first):
    return [c for c, (start, stop) in enumerate(SPANS) if first < stop and first + 8 > start]


def hit_slots():
    slots = {}
    for step in range(STEPS):
        for first in tiles_of(step):
            for column in columns_of(first):
                slots.setdefault((first, column), len(slots))
    return slots


def flip(block, index):
    return jnp.stack(
        [jnp.take_along_axis(block[i], index, axis=0) for i in range(block.shape[0])], axis=0
    )


def whole_kernel(
    rec_layer, rec_row, velocity, state_now, state_prev, notes, depth_mask, update,
    courant, wave, staged, staged_core, z_land, core_land, x_first, near_first, core_first,
    second_first, laplacians, picked, notes_all, traces, traces_all, sums_own, sums_all, turned,
    model, synthetic, products, filters, misfit, strengths, hits, places, gradient, gradient_own,
    gradient_other, start_send, start_recv, z_send, z_recv, core_send, core_recv, note_send,
    note_recv, trace_send, trace_recv, sum_send, sum_recv, pair_send, pair_recv,
):
    inline, xline, particle = (lax.axis_index(a) for a in ("inline", "xline", "particle"))
    count = lax.axis_size("xline")
    size = 2 * count
    me = inline * count + xline
    receivers = rec_row.shape[0]
    odd = lax.rem(xline, 2)
    toward = 1 - 2 * odd
    other = 1 - inline
    near, core = xline - toward, xline + toward
    second_in, second_out = xline - 2 * toward, xline + 2 * toward
    has_near = (near >= 0) & (near < count)
    has_in = (second_in >= 0) & (second_in < count)
    has_out = (second_out >= 0) & (second_out < count)
    always = xline >= 0
    sources = (state_now, state_prev, velocity)
    frames = (wave.at[0], wave.at[1], courant)
    sublane = lax.broadcasted_iota(jnp.int32, (8, 128), 0)
    backward_rows = 7 - sublane
    own_rows = jnp.where(odd == 1, 7 - sublane, sublane)

    barrier = pltpu.get_barrier_semaphore()

    def greet(step, carry):
        peer = lax.rem(me + step, size)
        pl.semaphore_signal(
            barrier, inc=1, device_id=(peer // count, lax.rem(peer, count), particle),
            device_id_type=MESH,
        )
        return carry

    lax.fori_loop(1, size, greet, 0)
    pl.semaphore_signal(
        barrier, inc=1, device_id=(inline, xline, 1 - particle), device_id_type=MESH
    )

    layers = pl.ds(inline * OWN_X, OWN_X)
    layers_other = pl.ds(other * OWN_X, OWN_X)

    def own_block(index):
        return pl.multiple_of(8 * (index + odd * (2 - 2 * index)), 8)

    for kind in range(3):
        for index in range(3):
            frames[kind][layers, pl.ds(Z_HALO + 8 * index, 8), :] = flip(
                sources[kind][0, :, pl.ds(own_block(index), 8), :], own_rows
            )

    @pl.when(jnp.logical_not(has_near))
    def _():
        for frame in frames:
            frame[:, pl.ds(8, Z_HALO - 8), :] = jnp.zeros((2 * OWN_X, Z_HALO - 8, 128), jnp.float32)
        notes_all[NEAR] = jnp.zeros(notes_all.shape[1:], jnp.float32)
        traces_all[NEAR] = jnp.zeros(traces_all.shape[1:], jnp.float32)

    @pl.when(jnp.logical_not(has_in))
    def _():
        for frame in frames:
            frame[:, pl.ds(0, 8), :] = jnp.zeros((2 * OWN_X, 8, 128), jnp.float32)
        notes_all[SECOND] = jnp.zeros(notes_all.shape[1:], jnp.float32)
        traces_all[SECOND] = jnp.zeros(traces_all.shape[1:], jnp.float32)

    notes_all[OWN, inline] = notes[...]
    picked[:, pl.ds(other * receivers, receivers), :] = jnp.zeros(
        (NT, receivers, 128), jnp.float32
    )
    pl.semaphore_wait(barrier, size)

    routes = [
        (always, always, (other, xline, particle), OWN),
        (always, always, (inline, core, particle), CORE),
        (always, always, (other, core, particle), CORE),
        (has_near, has_near, (inline, near, particle), NEAR),
        (has_near, has_near, (other, near, particle), NEAR),
        (has_out, has_in, (inline, second_out, particle), SECOND),
        (has_out, has_in, (other, second_out, particle), SECOND),
    ]
    origins = (other, inline, other, inline, other, inline, other)

    def remote(source, target, send, recv, device):
        return pltpu.make_async_remote_copy(
            src_ref=source, dst_ref=target, send_sem=send, recv_sem=recv, device_id=device,
            device_id_type=MESH,
        )

    def start_copy(index, kind, arriving=False):
        column = routes[index][3]
        passed_on = index in (2, 4, 6)
        origin = other if passed_on or (arriving and index == 0) else inline
        if column == OWN:
            first, extent, landing = 0, OWN_Y, x_first.at[kind]
        elif column == NEAR:
            first, extent, landing = 0, OWN_Y, near_first.at[kind, origin]
        elif column == CORE:
            first, extent, landing = 8 * (1 - odd), CORE_HALO, core_first.at[kind, origin]
        else:
            first, extent, landing = 16 * (1 - odd), 8, second_first.at[kind, origin]
        rows = pl.ds(first if isinstance(first, int) else pl.multiple_of(first, 8), extent)
        source = x_first.at[kind, :, rows, :] if passed_on else sources[kind].at[0, :, rows, :]
        target = routes[index - 1 if passed_on else index][2]
        return remote(
            source, landing, start_send.at[index, kind], start_recv.at[index, kind], target
        )

    def start_all(index, kind):
        @pl.when(routes[index][0])
        def _():
            start_copy(index, kind).start()

    def finish_first(indices):
        for index in indices:
            for kind in range(3):

                @pl.when(routes[index][0])
                def _():
                    start_copy(index, kind).wait_send()

                @pl.when(routes[index][1])
                def _():
                    start_copy(index, kind, True).wait_recv()

    for index in (0, 3, 1, 5):
        for kind in range(3):
            start_all(index, kind)

    def pair_copy(source, target, index):
        return remote(
            source, target, pair_send.at[index], pair_recv.at[index], (inline, xline, 1 - particle)
        )

    pair_copy(velocity.at[0], model, 0).start()

    def share(source, table, send, recv, origin, index):
        return remote(
            source, table.at[routes[index][3], origin], send.at[index], recv.at[index],
            routes[index][2],
        )

    def share_start(source, table, send, recv):
        for index in range(7):

            @pl.when(routes[index][0])
            def _():
                share(source, table, send, recv, inline, index).start()

    def share_wait(source, table, send, recv):
        for index in range(7):

            @pl.when(routes[index][0])
            def _():
                share(source, table, send, recv, inline, index).wait_send()

            @pl.when(routes[index][1])
            def _():
                share(source, table, send, recv, origins[index], index).wait_recv()

    first_layers = (pl.ds(0, OWN_X), pl.ds(OWN_X, OWN_X))

    def first_core():
        finish_first((1, 2))
        for kind in range(3):
            for half in range(2):
                for block in range(2):
                    at = pl.multiple_of(8 * (block + odd * (1 - 2 * block)), 8)
                    frames[kind][first_layers[half], pl.ds(OWN_END + 8 * block, 8), :] = flip(
                        core_first[kind, half, :, pl.ds(at, 8), :], own_rows
                    )

    def first_piece(piece):
        if piece == 0:
            finish_first((3, 4))
        if piece == 3:
            finish_first((5, 6))

        @pl.when(has_in if piece == 3 else has_near)
        def _():
            for kind in range(3):
                for half in range(2):
                    if piece == 3:
                        block = second_first[kind, half]
                    else:
                        block = near_first[kind, half, :, pl.ds(own_block(2 - piece), 8), :]
                    frames[kind][first_layers[half], pl.ds(24 - 8 * piece, 8), :] = flip(
                        block, own_rows
                    )

    for kind in range(3):
        start_copy(0, kind).wait_send()
        start_copy(0, kind, True).wait_recv()
        for index in (4, 2, 6):
            start_all(index, kind)
    for kind in range(3):
        for block in range(3):
            frames[kind][layers_other, pl.ds(Z_HALO + 8 * block, 8), :] = flip(
                x_first[kind, :, pl.ds(own_block(block), 8), :], own_rows
            )
    share_start(notes, notes_all, note_send, note_recv)

    band = band_matrix()
    ones = jnp.ones((8, 256), jnp.bfloat16)
    ordered = plan()

    def z_copies(slot):
        to_near, to_second = (inline, near, particle), (inline, second_out, particle)
        blocks = [
            (wave.at[0, :, pl.ds(Z_HALO, 8), :], 0, to_near),
            (staged.at[0], 1, to_near),
            (staged.at[2], 2, to_near),
            (staged.at[1], 3, to_near),
            (staged.at[3], 4, to_near),
            (staged.at[1], 5, to_second),
            (staged.at[4], 6, to_near),
        ]
        return [
            remote(source, z_land.at[slot, i], z_send.at[slot, i], z_recv.at[slot, i], target)
            for source, i, target in blocks
        ]

    def core_copies(slot, blocks):
        return [
            remote(
                block, core_land.at[slot, i], core_send.at[slot, i], core_recv.at[slot, i],
                (inline, core, particle),
            )
            for i, block in enumerate(blocks)
        ]

    z_valid = [has_near] * 5 + [has_out, has_near]
    z_arrives = [has_near] * 5 + [has_in, has_near]
    z_place = [(0, 24), (0, 16), (1, 20), (0, 8), (1, 12), (0, 0), (1, 4)]
    pieces = ((0,), (1, 2), (3, 4), (5, 6))
    sent = ((0,), (1, 2), (3, 4, 5, 6), ())
    core_place = [(0, OWN_END), (0, OWN_END + 8), (1, OWN_END + 4)]

    def send_early(slot):
        copies = z_copies(slot)
        staged[0] = wave[0, :, pl.ds(40, 8), :]
        staged[1] = wave[0, :, pl.ds(48, 8), :]
        staged[2] = wave[1, :, pl.ds(36, 8), :]
        staged[3] = wave[1, :, pl.ds(44, 8), :]
        staged[4] = wave[1, :, pl.ds(52, 8), :]
        for i in (5, 6):
            pl.when(z_valid[i])(copies[i].start)
        for copy in core_copies(slot, round_blocks):
            copy.start()

    def send_round(slot):
        copies = z_copies(slot)
        for i in range(5):
            pl.when(z_valid[i])(copies[i].start)

    round_blocks = [staged.at[1], staged.at[0], staged.at[3]]
    middle_blocks = [staged_core.at[i] for i in range(3)]

    def send_middle(slot):
        staged_core[0] = wave[0, :, pl.ds(48, 8), :]
        staged_core[1] = wave[0, :, pl.ds(40, 8), :]
        staged_core[2] = wave[1, :, pl.ds(44, 8), :]
        for copy in core_copies(slot, middle_blocks):
            copy.start()

    def take_core(slot, blocks):
        for i, copy in enumerate(core_copies(slot, blocks)):
            copy.wait()
            level, row = core_place[i]
            wave[level, :, pl.ds(row, 8), :] = flip(core_land[slot, i], backward_rows)

    def take_piece(slot, piece):
        copies = z_copies(slot)
        for i in sent[piece]:
            pl.when(z_valid[i])(copies[i].wait_send)
        for i in pieces[piece]:

            @pl.when(z_arrives[i])
            def _():
                copies[i].wait_recv()
                level, row = z_place[i]
                block = z_land[slot, i]
                if i != 5:
                    block = flip(block, backward_rows)
                wave[level, :, pl.ds(row, 8), :] = block

    rounds = NT // STEPS

    def run_round(number, sweep, tile):
        taken = sweep * (rounds - 1) + number - 1
        middle = 2 * (rounds - 1) + sweep * rounds + number
        for entry in ordered:
            if entry[0] == "tile":
                tile(entry[1], entry[2])
            elif entry[0] == "middle":
                send_middle(middle)
            elif entry[0] == "early":

                @pl.when(number < rounds - 1)
                def _():
                    send_early(taken + 1)
            elif entry[0] == "piece":

                @pl.when(number > 0)
                def _():
                    take_piece(taken, entry[1])

                if sweep == 0:

                    @pl.when(number == 0)
                    def _():
                        first_piece(entry[1])
            elif entry[1] == 0:

                @pl.when(number > 0)
                def _():
                    take_core(taken, round_blocks)

                if sweep == 0:
                    pl.when(number == 0)(first_core)
            else:
                take_core(middle, middle_blocks)

        @pl.when(number < rounds - 1)
        def _():
            send_round(taken + 1)

    def keep_lines(time, level):
        new = wave.at[level]
        for group in range(0, receivers, 16):
            lines = [
                new[inline * OWN_X + rec_layer[r], pl.ds(rec_row[r], 1), :]
                for r in range(group, group + 16)
            ]
            for offset, line in enumerate(lines):
                picked[time, pl.ds(inline * receivers + group + offset, 1), :] = line

    def read_traces(first_time, steps):
        for step in range(steps):
            time = first_time + step
            high, rest = split_two(picked[time] * depth_mask[...])
            row = lax.dot_general(
                ones, jnp.concatenate([high, rest], axis=1), (((1,), (1,)), ((), ())),
                preferred_element_type=jnp.float32,
            )
            traces[pl.ds(time, 1), :] = row[0:1]

    own_tiles = {s: {f for f in tiles_of(s) if f + 8 > Z_HALO and f < OWN_END} for s in range(STEPS)}

    def forward_round(number, carry):
        left = [set(own_tiles[s]) for s in range(STEPS)]

        @pl.when(number > 0)
        def _():
            for step in range(HALF, STEPS):
                keep_lines((number - 1) * STEPS + step, LEVELS[step % 4][2])
            read_traces((number - 1) * STEPS + HALF, HALF)

        def tile(step, first):
            now, old, new = (wave.at[level] for level in LEVELS[step % 4])
            time = number * STEPS + step
            center, laplacian = laplace_tile(now, first, band)
            here = pl.ds(first, 8)
            new[:, here, :] = 2.0 * center - old[:, here, :] + courant[:, here, :] * laplacian
            if first in own_tiles[step]:
                laplacians[time, :, pl.ds(first - Z_HALO + 8, 8), :] = own_half(laplacian, inline)
                left[step].discard(first)
                if step < HALF and not left[step]:
                    keep_lines(time, LEVELS[step % 4][2])

        run_round(number, 0, tile)
        read_traces(number * STEPS, HALF)
        return carry

    lax.fori_loop(0, rounds, forward_round, 0)
    for step in range(HALF, STEPS):
        keep_lines(NT - STEPS + step, LEVELS[step % 4][2])
    read_traces(NT - HALF, HALF)
    traces_all[OWN, inline] = traces[...]
    share_start(traces, traces_all, trace_send, trace_recv)

    keys = lax.broadcasted_iota(jnp.int32, (128, 128), 0)
    synthetic[...] = jnp.zeros(synthetic.shape, jnp.float32)
    products[...] = jnp.zeros(products.shape, jnp.float32)
    synthetic[OWN, pl.ds(8, NT), :] = traces[pl.ds(0, NT), :]
    lagged = [synthetic[OWN, pl.ds(8 - k, NT), :] for k in range(TAPS)]
    recorded = notes[pl.ds(0, NT), :]
    index = 0
    for k in range(TAPS):
        for l in range(k + 1):
            products[pl.ds(index, 1), :] = jnp.sum(lagged[k] * lagged[l], axis=0, keepdims=True)
            index += 1
    for k in range(TAPS):
        products[pl.ds(index + k, 1), :] = jnp.sum(lagged[k] * recorded, axis=0, keepdims=True)
    own_key = notes[pl.ds(NT + 3, 1), :].astype(jnp.int32) - inline * KEYS
    local = (keys[:KEYS] == own_key).astype(jnp.float32)
    partial = lax.dot_general(
        local, products[...], (((1,), (1,)), ((), ())),
        preferred_element_type=jnp.float32, precision=HIGHEST,
    )
    pair_copy(velocity.at[0], model, 0).wait()
    apart = jnp.sum(jnp.square(velocity[0] - model[...]), axis=0)
    apart = apart[0:8] + apart[8:16] + apart[16:24]
    lane = lax.broadcasted_iota(jnp.int32, (8, 128), 1)
    partial = jnp.where(lane == 127, jnp.sum(apart, axis=1, keepdims=True), partial)
    sums_own[...] = partial
    sums_all[me] = partial

    def sum_copy(step, peer):
        sender = lax.rem(me + size - step, size)
        return remote(
            sums_own, sums_all.at[me if peer else sender], sum_send.at[step], sum_recv.at[step],
            (
                lax.rem(me + step, size) // count if peer else sender // count,
                lax.rem(me + step if peer else sender, count),
                particle,
            ),
        )

    def sum_start(step, carry):
        sum_copy(step, True).start()
        return carry

    lax.fori_loop(1, size, sum_start, 0)

    share_wait(notes, notes_all, note_send, note_recv)
    for column in range(4):
        pair = notes_all[column, 0] + notes_all[column, 1]
        place_row = pair[NT + 1 : NT + 2].astype(jnp.int32)
        frame_row = (place_row - 16, 31 - place_row, Z_HALO + place_row, OWN_END + 23 - place_row)[
            column
        ]
        depth = pair[NT + 2 : NT + 3].astype(jnp.int32)
        fits = (frame_row >= 0) & (frame_row < ROWS)
        row_id = jnp.where(fits, pair[NT : NT + 1].astype(jnp.int32) + frame_row, -1)
        place = (keys == depth).astype(jnp.float32).astype(jnp.bfloat16)
        places[:, pl.ds(256 * column, 128)] = place
        places[:, pl.ds(256 * column + 128, 128)] = place
        for (first, found), slot in hit_slots().items():
            if found == column:
                wanted = (keys // 8) * ROWS + first + lax.rem(keys, 8)
                hit = (wanted == row_id).astype(jnp.float32).astype(jnp.bfloat16)
                hits[slot, :, pl.ds(0, 128)] = hit
                hits[slot, :, pl.ds(128, 128)] = hit
    wave[...] = jnp.zeros(wave.shape, jnp.float32)
    gradient[...] = jnp.zeros(gradient.shape, jnp.float32)
    misfit[...] = jnp.zeros(misfit.shape, jnp.float32)
    turned[...] = jnp.zeros(turned.shape, jnp.float32)

    def sum_wait(step, carry):
        sum_copy(step, True).wait_send()
        sum_copy(step, False).wait_recv()
        return carry

    lax.fori_loop(1, size, sum_wait, 0)
    total = [jnp.zeros((8, 128), jnp.float32) for i in range(2)]
    for row in range(2):
        for column in range(count):
            total[row] = total[row] + sums_all[row * count + column]
        turned[pl.ds(KEYS * row, KEYS), :] = total[row]
    sums = jnp.transpose(turned[...])
    for k, row in enumerate(solve_rows(sums[:48])):
        filters[pl.ds(k, 1), :] = row

    share_wait(traces, traces_all, trace_send, trace_recv)
    for column in range(4):
        both = traces_all[column, 0] + traces_all[column, 1]
        synthetic[column, pl.ds(8, NT), :] = both[:NT]
        pair = notes_all[column, 0] + notes_all[column, 1]
        members = (keys == pair[NT + 3 : NT + 4].astype(jnp.int32)).astype(jnp.float32)
        own = jnp.dot(
            filters[...], members, preferred_element_type=jnp.float32, precision=HIGHEST
        )
        fitted = sum(own[k : k + 1] * synthetic[column, pl.ds(8 - k, NT), :] for k in range(TAPS))
        misfit[column, pl.ds(0, NT), :] = fitted - pair[:NT]
        source = sum(own[k : k + 1] * misfit[column, pl.ds(k, NT), :] for k in range(TAPS))
        high, rest = split_two(source)
        strengths[:, pl.ds(256 * column, 128)] = high.astype(jnp.float32)
        strengths[:, pl.ds(256 * column + 128, 128)] = rest.astype(jnp.float32)

    slots = hit_slots()

    def backward_round(number, carry):
        def tile(step, first):
            now, old, new = (wave.at[level] for level in LEVELS[step % 4])
            time = NT - 1 - (number * STEPS + step)
            strength = strengths[pl.ds(time, 1), :].astype(jnp.bfloat16)
            center, laplacian = laplace_tile(now, first, band)
            here = pl.ds(first, 8)
            added = 0.0
            for column in columns_of(first):
                part = slice(256 * column, 256 * (column + 1))
                added = added + lax.dot_general(
                    hits[slots[first, column]] * strength[:, part],
                    places[:, part],
                    (((1,), (1,)), ((), ())),
                    preferred_element_type=jnp.float32,
                )
            following = 2.0 * center - old[:, here, :] + courant[:, here, :] * laplacian
            following = following + added.reshape(2 * OWN_X, 8, 128)
            new[:, here, :] = following
            if first in own_tiles[step]:
                kept = pl.ds(first - Z_HALO + 8, 8)
                gradient[:, kept, :] = (
                    gradient[:, kept, :]
                    + own_half(following, inline) * laplacians[time, :, kept, :]
                )

        run_round(number, 1, tile)
        return carry

    lax.fori_loop(0, rounds, backward_round, 0)
    for index in range(3):
        gradient_own[:, pl.ds(own_block(index), 8), :] = flip(
            gradient[:, pl.ds(8 + 8 * index, 8), :] * (1.0 / NT), own_rows
        )
    pair_copy(gradient_own, gradient_other, 1).start()
    apart = jnp.where(lane == 127, total[0] + total[1], 0.0)
    apart = jnp.sum(jnp.sum(apart, axis=0, keepdims=True), axis=1, keepdims=True)
    distance = apart / (size * OWN_X * OWN_Y * 128)
    weight = jnp.exp(jnp.broadcast_to(-distance / KERNEL_WIDTH, (8, 128)))[0:1]
    between = 2.0 * (velocity[0] - model[...]) / KERNEL_WIDTH
    pair_copy(gradient_own, gradient_other, 1).wait()
    own_term = gradient_own[...] * (-1.0 / NOISE_VARIANCE)
    other_term = gradient_other[...] * (-1.0 / NOISE_VARIANCE) + between
    update[0] = (STEP_SIZE / 2) * (own_term + weight[None] * other_term)


def per_device_pair(velocity, state_now, state_prev, observed, rec_cell, rec_gather):
    inline, xline = lax.axis_index("inline"), lax.axis_index("xline")
    count = rec_cell.shape[0]
    size = 2 * lax.axis_size("xline")
    line = rec_cell // 128
    layer, local_row = line // OWN_Y, line % OWN_Y
    place = jnp.where(xline % 2 == 1, OWN_Y - 1 - local_row, local_row)
    facts = jnp.stack(
        [
            (inline * OWN_X + layer) * ROWS,
            place,
            rec_cell % 128,
            inline * KEYS + rec_gather[:, 0],
        ]
    ).astype(jnp.float32)
    notes = jnp.concatenate([observed.T, facts, jnp.zeros((4, count), jnp.float32)], axis=0)
    blank = jnp.zeros_like(notes)
    first = inline == 0
    notes = jnp.concatenate([jnp.where(first, notes, blank), jnp.where(first, blank, notes)], axis=1)
    lanes = jnp.arange(128, dtype=jnp.int32)[None, :]
    depth_mask = ((rec_cell % 128)[:, None] == lanes).astype(jnp.float32)
    depth_mask = jnp.concatenate([depth_mask, depth_mask], axis=0)
    vmem = pl.BlockSpec(memory_space=pltpu.VMEM)
    smem = pl.BlockSpec(memory_space=pltpu.SMEM)
    f32, bf16 = jnp.float32, jnp.bfloat16
    dma = pltpu.SemaphoreType.DMA
    exchanges = 2 * (NT // STEPS - 1)
    halves = exchanges + 2 * (NT // STEPS)
    return pl.pallas_call(
        whole_kernel,
        out_shape=jax.ShapeDtypeStruct(velocity.shape, f32),
        in_specs=[smem, smem] + [vmem] * 5,
        out_specs=vmem,
        scratch_shapes=[
            pltpu.VMEM((2 * OWN_X, ROWS, 128), f32),
            pltpu.VMEM((4, 2 * OWN_X, ROWS, 128), f32),
            pltpu.VMEM((5, 2 * OWN_X, 8, 128), f32),
            pltpu.VMEM((3, 2 * OWN_X, 8, 128), f32),
            pltpu.VMEM((exchanges, 7, 2 * OWN_X, 8, 128), f32),
            pltpu.VMEM((halves, 3, 2 * OWN_X, 8, 128), f32),
            pltpu.VMEM((3, OWN_X, OWN_Y, 128), f32),
            pltpu.VMEM((3, 2, OWN_X, OWN_Y, 128), f32),
            pltpu.VMEM((3, 2, OWN_X, CORE_HALO, 128), f32),
            pltpu.VMEM((3, 2, OWN_X, 8, 128), f32),
            pltpu.VMEM((NT, OWN_X, OWN_Y + 16, 128), f32),
            pltpu.VMEM((NT, 2 * count, 128), f32),
            pltpu.VMEM((4, 2, NT + 8, 128), f32),
            pltpu.VMEM((NT, 128), f32),
            pltpu.VMEM((4, 2, NT, 128), f32),
            pltpu.VMEM((8, 128), f32),
            pltpu.VMEM((size, 8, 128), f32),
            pltpu.VMEM((128, 128), f32),
            pltpu.VMEM((OWN_X, OWN_Y, 128), f32),
            pltpu.VMEM((4, NT + 8, 128), f32),
            pltpu.VMEM((128, 128), f32),
            pltpu.VMEM((8, 128), f32),
            pltpu.VMEM((4, NT + 8, 128), f32),
            pltpu.VMEM((NT, 1024), f32),
            pltpu.VMEM((len(hit_slots()), 128, 256), bf16),
            pltpu.VMEM((128, 1024), bf16),
            pltpu.VMEM((OWN_X, OWN_Y + 16, 128), f32),
            pltpu.VMEM((OWN_X, OWN_Y, 128), f32),
            pltpu.VMEM((OWN_X, OWN_Y, 128), f32),
            dma((7, 3)),
            dma((7, 3)),
            dma((exchanges, 7)),
            dma((exchanges, 7)),
            dma((halves, 3)),
            dma((halves, 3)),
            dma((7,)),
            dma((7,)),
            dma((7,)),
            dma((7,)),
            dma((size,)),
            dma((size,)),
            dma((2,)),
            dma((2,)),
        ],
        compiler_params=pltpu.CompilerParams(
            collective_id=0, has_side_effects=True, vmem_limit_bytes=48 * 1024 * 1024
        ),
        name="inversion_window",
    )(layer, place + Z_HALO, velocity, state_now, state_prev, notes, depth_mask)


def solution(mesh):
    shape = mesh.shape
    paired = (shape["inline"], shape["particle"]) == (2, 2) and shape["xline"] in (2, 4, 6, 8)
    return jax.shard_map(
        per_device_pair if paired else per_device,
        mesh=mesh,
        in_specs=(
            P("particle", "inline", "xline", None),
            P("particle", "inline", "xline", None),
            P("particle", "inline", "xline", None),
            P(("inline", "xline"), None),
            P(("inline", "xline")),
            P(("inline", "xline"), None),
        ),
        out_specs=P("particle", "inline", "xline", None),
        check_vma=False,
    )
```

```python
import jax
import jax.numpy as jnp
from jax import lax
from jax.experimental import pallas as pl
from jax.experimental.pallas import tpu as pltpu
from jax.sharding import PartitionSpec as P

NT = 32
CAP = 16
TAPS = 8


COEFFS = (8.0 / 5.0, -1.0 / 5.0, 8.0 / 315.0, -1.0 / 560.0)
CENTER = -205.0 / 72.0
KERNEL_WIDTH = 0.004
NOISE_VARIANCE = 0.0005
STEP_SIZE = 0.01
RIDGE_BASE = 1.0
RIDGE_SHARE = 0.1
HIGHEST = lax.Precision.HIGHEST


def extended(block, sides, width):
    for axis, dim in sides:
        count = lax.axis_size(axis)
        forward = [(i, i + 1) for i in range(count - 1)]
        backward = [(target, source) for source, target in forward]
        low = lax.ppermute(
            lax.slice_in_dim(block, block.shape[dim] - width, None, axis=dim), axis, forward
        )
        high = lax.ppermute(lax.slice_in_dim(block, 0, width, axis=dim), axis, backward)
        block = jnp.concatenate([low, block, high], axis=dim)
    return block


def laplace_inner(block):
    size_x, size_y, size_z = block.shape
    inner_x = size_x - 8
    inner_y = size_y - 8
    padded = jnp.pad(block, ((0, 0), (0, 0), (4, 4)))
    total = 3.0 * CENTER * block[4 : 4 + inner_x, 4 : 4 + inner_y, :]
    for shift in range(1, 5):
        weight = COEFFS[shift - 1]
        beside = padded[4 + shift : 4 + shift + inner_x, 4 : 4 + inner_y, 4 : 4 + size_z]
        beside = beside + padded[4 - shift : 4 - shift + inner_x, 4 : 4 + inner_y, 4 : 4 + size_z]
        beside = beside + padded[4 : 4 + inner_x, 4 + shift : 4 + shift + inner_y, 4 : 4 + size_z]
        beside = beside + padded[4 : 4 + inner_x, 4 - shift : 4 - shift + inner_y, 4 : 4 + size_z]
        beside = beside + padded[4 : 4 + inner_x, 4 : 4 + inner_y, 4 + shift : 4 + shift + size_z]
        beside = beside + padded[4 : 4 + inner_x, 4 : 4 + inner_y, 4 - shift : 4 - shift + size_z]
        total = total + weight * beside
    return total


def lagged_traces(traces):
    steps = traces.shape[1]
    padded = jnp.pad(traces, ((0, 0), (TAPS - 1, 0)))
    return jnp.stack(
        [padded[:, TAPS - 1 - shift : TAPS - 1 - shift + steps] for shift in range(TAPS)], axis=1
    )


def filter_stats(lagged, observed):
    count = lagged.shape[0]
    gram = jnp.einsum("mkt,mlt->mkl", lagged, lagged, precision=HIGHEST).reshape(count, TAPS * TAPS)
    cross = jnp.einsum("mkt,mt->mk", lagged, observed, precision=HIGHEST)
    return (gram, cross)


def solve_filter(gram, cross):
    matrix = gram.reshape(-1, TAPS, TAPS)
    sums = [matrix[:, k, l] for k in range(TAPS) for l in range(k + 1)]
    sums = jnp.stack(sums + [cross[:, k] for k in range(TAPS)])
    return jnp.concatenate(solve_rows(sums), axis=0).T


def adjoint_sources(lagged, observed, filters):
    steps = observed.shape[1]
    fitted = jnp.einsum("mk,mkt->mt", filters, lagged, precision=HIGHEST)
    misfit = fitted - observed
    padded = jnp.pad(misfit, ((0, 0), (0, TAPS - 1)))
    ahead = jnp.stack([padded[:, shift : shift + steps] for shift in range(TAPS)], axis=1)
    return jnp.einsum("mk,mkt->mt", filters, ahead, precision=HIGHEST)


def per_device(velocity, state_now, state_prev, observed, rec_cell, rec_gather):
    courant = velocity[0]
    particles = lax.axis_size("particle")
    models = lax.all_gather(velocity, "particle", axis=0, tiled=True)
    partial_sums = jnp.sum(jnp.square(models - velocity), axis=(1, 2, 3))
    cells_all = courant.size * lax.axis_size("inline") * lax.axis_size("xline")
    distance = lax.psum(partial_sums, ("inline", "xline")) / cells_all
    kernel = jnp.exp(-distance / KERNEL_WIDTH)

    def advance(carry, unused):
        current, previous = carry
        padded = extended(current[None], (("inline", 1), ("xline", 2)), 4)[0]
        laplacian = laplace_inner(padded)
        following = 2.0 * current - previous + courant * laplacian
        return ((following, current), (laplacian, following.reshape(-1)[rec_cell]))

    unused, (laplacians, traces) = lax.scan(advance, (state_now[0], state_prev[0]), None, length=NT)
    synthetic = traces.T
    steps = observed.shape[1]
    xline_count = lax.axis_size("xline")
    target = rec_gather[:, 0]
    choose = (target[:, None] == jnp.arange(xline_count, dtype=jnp.int32)[None, :]).astype(
        jnp.int32
    )
    order = jnp.arange(target.shape[0], dtype=jnp.int32)
    earlier = (order[None, :] < order[:, None]).astype(jnp.float32)
    before = jnp.dot(earlier, choose.astype(jnp.float32), precision=HIGHEST).astype(jnp.int32)
    position = target * CAP + jnp.sum(before * choose, axis=1)
    outgoing = jnp.zeros((xline_count * CAP, 2 * steps), jnp.float32)
    outgoing = outgoing.at[position].set(jnp.concatenate([synthetic, observed], axis=1))
    arrived = lax.all_to_all(
        outgoing.reshape(xline_count, CAP, 2 * steps),
        "xline",
        split_axis=0,
        concat_axis=0,
        tiled=True,
    )
    slots = arrived.reshape(xline_count * CAP, 2 * steps)
    slot_lagged = lagged_traces(slots[:, :steps])
    slot_observed = slots[:, steps:]
    gram, cross = filter_stats(slot_lagged, slot_observed)
    filters_one = solve_filter(
        jnp.sum(gram, axis=0, keepdims=True), jnp.sum(cross, axis=0, keepdims=True)
    )
    filters = jnp.broadcast_to(filters_one, (slots.shape[0], TAPS))
    slot_adjoint = adjoint_sources(slot_lagged, slot_observed, filters)
    returned = lax.all_to_all(
        slot_adjoint.reshape(xline_count, CAP, steps),
        "xline",
        split_axis=0,
        concat_axis=0,
        tiled=True,
    )
    adjoint_source = returned.reshape(xline_count * CAP, steps)[position]

    def backward(carry, inputs):
        wave, wave_old, gradient = carry
        laplacian, source = inputs
        padded = extended(wave[None], (("inline", 1), ("xline", 2)), 4)[0]
        wave_new = 2.0 * wave - wave_old + courant * laplace_inner(padded)
        wave_new = wave_new.reshape(-1).at[rec_cell].add(source).reshape(wave.shape)
        return ((wave_new, wave, gradient + wave_new * laplacian), None)

    zeros_field = jnp.zeros(courant.shape, jnp.float32)
    (wave, wave_old, gradient), unused = lax.scan(
        backward,
        (zeros_field, zeros_field, zeros_field),
        (laplacians, adjoint_source.T),
        reverse=True,
    )
    gradient = gradient / NT
    gradients = lax.all_gather(gradient[None], "particle", axis=0, tiled=True)
    terms = -gradients / NOISE_VARIANCE + 2.0 * (velocity - models) / KERNEL_WIDTH
    update = (
        STEP_SIZE / particles * jnp.sum(kernel[:, None, None, None] * terms, axis=0, keepdims=True)
    )
    return update


STEPS = 8
HALF = 4
Z_HALO = 4 * STEPS
CORE_HALO = 4 * HALF
OWN_X = 8
OWN_Y = Z_HALO - 8
OWN_END = Z_HALO + OWN_Y
ROWS = OWN_END + CORE_HALO
KEYS = 8
INTEGER_COEFFS = (8064.0, -1008.0, 128.0, -9.0)
INTEGER_SCALE = 1.0 / 5040.0
LEVELS = ((0, 1, 2), (2, 0, 3), (3, 2, 1), (1, 3, 0))
MESH = pl.DeviceIdType.MESH
SECOND, NEAR, OWN, CORE = range(4)
SPANS = ((0, 8), (8, Z_HALO), (Z_HALO, OWN_END), (OWN_END, ROWS))


def split_two(value):
    high = value.astype(jnp.bfloat16)
    rest = (value - high.astype(jnp.float32)).astype(jnp.bfloat16)
    return high, rest


def band_matrix():
    row = lax.broadcasted_iota(jnp.int32, (256, 128), 0) % 128
    col = lax.broadcasted_iota(jnp.int32, (256, 128), 1)
    away = jnp.abs(row - col)
    band = jnp.zeros((256, 128), jnp.float32)
    for shift in range(1, 5):
        band = jnp.where(away == shift, INTEGER_COEFFS[shift - 1], band)
    return band.astype(jnp.bfloat16)


def laplace_tile(wave, first, band):
    center = wave[:, pl.ds(first, 8), :]
    layers = center.shape[0]
    high, rest = split_two(center.reshape(layers * 8, 128))
    depth = jnp.dot(
        jnp.concatenate([high, rest], axis=1), band, preferred_element_type=jnp.float32
    ).reshape(layers, 8, 128)
    total = 3.0 * CENTER * center + INTEGER_SCALE * depth
    for shift in range(1, 5):
        beside = wave[:, pl.ds(first + shift, 8), :] + wave[:, pl.ds(first - shift, 8), :]
        blank = jnp.zeros((shift, 8, 128), jnp.float32)
        beside = beside + jnp.concatenate([center[shift:], blank], axis=0)
        beside = beside + jnp.concatenate([blank, center[:-shift]], axis=0)
        total = total + COEFFS[shift - 1] * beside
    return center, total


def own_half(value, inline):
    return jnp.where(inline == 0, value[:OWN_X], value[OWN_X:])


def solve_rows(sums):
    entry = {}
    index = 0
    for k in range(TAPS):
        for l in range(k + 1):
            entry[k, l] = sums[index : index + 1]
            index += 1
    right = [sums[index + k : index + k + 1] for k in range(TAPS)]
    trace_sum = sum(entry[k, k] for k in range(TAPS))
    ridge = RIDGE_BASE + RIDGE_SHARE * trace_sum / TAPS
    for k in range(TAPS):
        entry[k, k] = entry[k, k] + ridge
    inverse = []
    for k in range(TAPS):
        inverse.append(1.0 / entry[k, k])
        factor = {i: entry[i, k] * inverse[k] for i in range(k + 1, TAPS)}
        for i in range(k + 1, TAPS):
            for l in range(k + 1, i + 1):
                entry[i, l] = entry[i, l] - factor[i] * entry[l, k]
            right[i] = right[i] - factor[i] * right[k]
        for i in range(k + 1, TAPS):
            entry[i, k] = factor[i]
    right = [right[k] * inverse[k] for k in range(TAPS)]
    for k in reversed(range(TAPS)):
        for i in range(k):
            right[i] = right[i] - entry[k, i] * right[k]
    return right


def tiles_of(step):
    first = 4 * (step + 1)
    return range(first, OWN_END + 4 * (HALF - 1 - step % HALF), 8)


def plan():
    first_half = [(s, f) for s in range(HALF) for f in tiles_of(s)]
    later = [(s, f) for s in range(HALF, STEPS) for f in tiles_of(s)]
    order, done = [], set()

    def ready(step, first, pieces, core, core_later):
        if Z_HALO - (first - 4 * (step + 1)) > 8 * pieces:
            return False
        reach = first + 8 + 4 * (step % HALF + 1)
        if reach > OWN_END and not (core if step < HALF else core_later):
            return False
        if step == 0:
            return True
        if step >= HALF and any(
            f + 8 > Z_HALO and f < OWN_END and (step - HALF, f) not in done
            for f in tiles_of(step - HALF)
        ):
            return False
        span = range(first - 4, first + 12)
        covered = {r for s, f in done if s == step - 1 for r in range(f, f + 8)}
        if step == HALF:
            return all(r in covered for r in span if r < OWN_END)
        return all(r in covered for r in span)

    def take(tiles, pieces, core, core_later):
        changed = True
        while changed:
            changed = False
            for step, first in tiles:
                if (step, first) not in done and ready(step, first, pieces, core, core_later):
                    done.add((step, first))
                    order.append(("tile", step, first))
                    changed = True

    both = first_half + later
    take(both, 0, False, False)
    order.append(("core", 0))
    take(both, 0, True, False)
    order.append(("piece", 0))
    take(first_half, 1, True, False)
    order.append(("middle",))
    take(both, 1, True, False)
    order.append(("piece", 1))
    take(both, 2, True, False)
    order.append(("core", 1))
    take(both, 2, True, True)
    order.append(("early", 0))
    order.append(("piece", 2))
    take(both, 3, True, True)
    order.append(("early", 1))
    order.append(("piece", 3))
    take(both, 4, True, True)
    assert len(done) == len(both)
    return order


def columns_of(first):
    return [c for c, (start, stop) in enumerate(SPANS) if first < stop and first + 8 > start]


def hit_slots():
    slots = {}
    for step in range(STEPS):
        for first in tiles_of(step):
            for column in columns_of(first):
                slots.setdefault((first, column), len(slots))
    return slots


def flip(block, index):
    return jnp.stack(
        [jnp.take_along_axis(block[i], index, axis=0) for i in range(block.shape[0])], axis=0
    )


def whole_kernel(
    rec_cell, velocity, state_now, state_prev, observed, cells, gathers, update,
    rec_layer, rec_row, fields, seen, cell_row, gather_row, notes, depth_mask, local_sem, courant, wave, staged, staged_core, z_land, core_land, x_first, near_first, core_first,
    second_first, laplacians, picked, notes_all, traces, traces_all, sums_own, sums_all, turned,
    model, synthetic, products, filters, misfit, strengths, hits, places, gradient, gradient_own,
    gradient_other, start_send, start_recv, z_send, z_recv, core_send, core_recv, note_send,
    note_recv, trace_send, trace_recv, sum_send, sum_recv, pair_send, pair_recv,
):
    inline, xline, particle = (lax.axis_index(a) for a in ("inline", "xline", "particle"))
    count = lax.axis_size("xline")
    size = 2 * count
    me = inline * count + xline
    receivers = rec_cell.shape[0]
    odd = lax.rem(xline, 2)
    toward = 1 - 2 * odd
    other = 1 - inline
    near, core = xline - toward, xline + toward
    second_in, second_out = xline - 2 * toward, xline + 2 * toward
    has_near = (near >= 0) & (near < count)
    has_in = (second_in >= 0) & (second_in < count)
    has_out = (second_out >= 0) & (second_out < count)
    always = xline >= 0
    sources = [fields.at[pl.ds(kind, 1)] for kind in range(3)]
    frames = (wave.at[0], wave.at[1], courant)
    sublane = lax.broadcasted_iota(jnp.int32, (8, 128), 0)
    backward_rows = 7 - sublane
    own_rows = jnp.where(odd == 1, 7 - sublane, sublane)

    inputs = [
        pltpu.make_async_copy(source, target, local_sem.at[i])
        for i, (source, target) in enumerate(
            [
                (observed, seen),
                (cells, cell_row),
                (gathers, gather_row),
                (state_now.at[0], fields.at[0]),
                (state_prev.at[0], fields.at[1]),
                (velocity.at[0], fields.at[2]),
            ]
        )
    ]
    for copy in inputs:
        copy.start()
    barrier = pltpu.get_barrier_semaphore()

    def greet(step, carry):
        peer = lax.rem(me + step, size)
        pl.semaphore_signal(
            barrier, inc=1, device_id=(peer // count, lax.rem(peer, count), particle),
            device_id_type=MESH,
        )
        return carry

    lax.fori_loop(1, size, greet, 0)
    pl.semaphore_signal(
        barrier, inc=1, device_id=(inline, xline, 1 - particle), device_id_type=MESH
    )

    for r in range(receivers):
        line = rec_cell[r] >> 7
        layer = (line * 2731) >> 16
        row = line - layer * OWN_Y
        rec_layer[r] = layer
        rec_row[r] = Z_HALO + row + odd * (OWN_Y - 1 - 2 * row)
    for copy in inputs:
        copy.wait()
    pl.semaphore_wait(barrier, size)

    routes = [
        (always, always, (other, xline, particle), OWN),
        (always, always, (inline, core, particle), CORE),
        (always, always, (other, core, particle), CORE),
        (has_near, has_near, (inline, near, particle), NEAR),
        (has_near, has_near, (other, near, particle), NEAR),
        (has_out, has_in, (inline, second_out, particle), SECOND),
        (has_out, has_in, (other, second_out, particle), SECOND),
    ]
    origins = (other, inline, other, inline, other, inline, other)

    def remote(source, target, send, recv, device):
        return pltpu.make_async_remote_copy(
            src_ref=source, dst_ref=target, send_sem=send, recv_sem=recv, device_id=device,
            device_id_type=MESH,
        )

    def start_copy(index, kind, arriving=False):
        column = routes[index][3]
        passed_on = index in (2, 4, 6)
        origin = other if passed_on or (arriving and index == 0) else inline
        if column == OWN:
            first, extent, landing = 0, OWN_Y, x_first.at[kind]
        elif column == NEAR:
            first, extent, landing = 0, OWN_Y, near_first.at[kind, origin]
        elif column == CORE:
            first, extent, landing = 8 * (1 - odd), CORE_HALO, core_first.at[kind, origin]
        else:
            first, extent, landing = 16 * (1 - odd), 8, second_first.at[kind, origin]
        rows = pl.ds(first if isinstance(first, int) else pl.multiple_of(first, 8), extent)
        source = x_first.at[kind, :, rows, :] if passed_on else sources[kind].at[0, :, rows, :]
        target = routes[index - 1 if passed_on else index][2]
        return remote(
            source, landing, start_send.at[index, kind], start_recv.at[index, kind], target
        )

    def start_all(index, kind):
        @pl.when(routes[index][0])
        def _():
            start_copy(index, kind).start()

    def finish_first(indices):
        for index in indices:
            for kind in range(3):

                @pl.when(routes[index][0])
                def _():
                    start_copy(index, kind).wait_send()

                @pl.when(routes[index][1])
                def _():
                    start_copy(index, kind, True).wait_recv()

    for index in (0, 3, 1, 5):
        for kind in range(3):
            start_all(index, kind)

    def pair_copy(source, target, index):
        return remote(
            source, target, pair_send.at[index], pair_recv.at[index], (inline, xline, 1 - particle)
        )

    pair_copy(fields.at[2], model, 0).start()

    def share(source, table, send, recv, origin, index):
        return remote(
            source, table.at[routes[index][3], origin], send.at[index], recv.at[index],
            routes[index][2],
        )

    def share_start(source, table, send, recv):
        for index in range(7):

            @pl.when(routes[index][0])
            def _():
                share(source, table, send, recv, inline, index).start()

    def share_wait(source, table, send, recv):
        for index in range(7):

            @pl.when(routes[index][0])
            def _():
                share(source, table, send, recv, inline, index).wait_send()

            @pl.when(routes[index][1])
            def _():
                share(source, table, send, recv, origins[index], index).wait_recv()

    layers = pl.ds(inline * OWN_X, OWN_X)
    layers_other = pl.ds(other * OWN_X, OWN_X)

    def own_block(index):
        return pl.multiple_of(8 * (index + odd * (2 - 2 * index)), 8)

    for kind in range(3):
        for index in range(3):
            frames[kind][layers, pl.ds(Z_HALO + 8 * index, 8), :] = flip(
                fields[kind, :, pl.ds(own_block(index), 8), :], own_rows
            )

    @pl.when(jnp.logical_not(has_near))
    def _():
        for frame in frames:
            frame[:, pl.ds(8, Z_HALO - 8), :] = jnp.zeros((2 * OWN_X, Z_HALO - 8, 128), jnp.float32)
        notes_all[NEAR] = jnp.zeros(notes_all.shape[1:], jnp.float32)
        traces_all[NEAR] = jnp.zeros(traces_all.shape[1:], jnp.float32)

    @pl.when(jnp.logical_not(has_in))
    def _():
        for frame in frames:
            frame[:, pl.ds(0, 8), :] = jnp.zeros((2 * OWN_X, 8, 128), jnp.float32)
        notes_all[SECOND] = jnp.zeros(notes_all.shape[1:], jnp.float32)
        traces_all[SECOND] = jnp.zeros(traces_all.shape[1:], jnp.float32)

    lane = lax.broadcasted_iota(jnp.int32, (8, 128), 1)
    here = (lane // receivers) == inline
    cell = jnp.concatenate([cell_row[...], cell_row[...]], axis=1)
    gather = jnp.concatenate([gather_row[...], gather_row[...]], axis=1)
    line = cell >> 7
    layer = (line * 2731) >> 16
    row = line - layer * OWN_Y
    facts = [
        (inline * OWN_X + layer) * ROWS,
        row + odd * (OWN_Y - 1 - 2 * row),
        cell & 127,
        inline * KEYS + gather,
    ]
    for block in range(0, NT, 8):
        part = seen[pl.ds(block, 8), :]
        notes[pl.ds(block, 8), :] = jnp.where(here, jnp.concatenate([part, part], axis=1), 0.0)
    notes[pl.ds(NT, 8), :] = jnp.zeros((8, 128), jnp.float32)
    for i, fact in enumerate(facts):
        notes[pl.ds(NT + i, 1), :] = jnp.where(here[0:1], fact.astype(jnp.float32), 0.0)
    keys = lax.broadcasted_iota(jnp.int32, (128, 128), 0)
    depth_mask[...] = jnp.transpose((keys == (cell & 127)).astype(jnp.float32))
    notes_all[OWN, inline] = notes[...]
    picked[:, pl.ds(other * receivers, receivers), :] = jnp.zeros(
        (NT, receivers, 128), jnp.float32
    )
    first_layers = (pl.ds(0, OWN_X), pl.ds(OWN_X, OWN_X))

    def first_core():
        finish_first((1, 2))
        for kind in range(3):
            for half in range(2):
                for block in range(2):
                    at = pl.multiple_of(8 * (block + odd * (1 - 2 * block)), 8)
                    frames[kind][first_layers[half], pl.ds(OWN_END + 8 * block, 8), :] = flip(
                        core_first[kind, half, :, pl.ds(at, 8), :], own_rows
                    )

    def first_piece(piece):
        if piece == 0:
            finish_first((3, 4))
        if piece == 3:
            finish_first((5, 6))

        @pl.when(has_in if piece == 3 else has_near)
        def _():
            for kind in range(3):
                for half in range(2):
                    if piece == 3:
                        block = second_first[kind, half]
                    else:
                        block = near_first[kind, half, :, pl.ds(own_block(2 - piece), 8), :]
                    frames[kind][first_layers[half], pl.ds(24 - 8 * piece, 8), :] = flip(
                        block, own_rows
                    )

    for kind in range(3):
        start_copy(0, kind).wait_send()
        start_copy(0, kind, True).wait_recv()
        for index in (4, 2, 6):
            start_all(index, kind)
    for kind in range(3):
        for block in range(3):
            frames[kind][layers_other, pl.ds(Z_HALO + 8 * block, 8), :] = flip(
                x_first[kind, :, pl.ds(own_block(block), 8), :], own_rows
            )
    share_start(notes, notes_all, note_send, note_recv)

    band = band_matrix()
    ones = jnp.ones((8, 256), jnp.bfloat16)
    ordered = plan()

    def z_copies(slot):
        to_near, to_second = (inline, near, particle), (inline, second_out, particle)
        blocks = [
            (wave.at[0, :, pl.ds(Z_HALO, 8), :], 0, to_near),
            (staged.at[0], 1, to_near),
            (staged.at[2], 2, to_near),
            (staged.at[1], 3, to_near),
            (staged.at[3], 4, to_near),
            (staged.at[1], 5, to_second),
            (staged.at[4], 6, to_near),
        ]
        return [
            remote(source, z_land.at[slot, i], z_send.at[slot, i], z_recv.at[slot, i], target)
            for source, i, target in blocks
        ]

    def core_copies(slot, blocks):
        return [
            remote(
                block, core_land.at[slot, i], core_send.at[slot, i], core_recv.at[slot, i],
                (inline, core, particle),
            )
            for i, block in enumerate(blocks)
        ]

    z_valid = [has_near] * 5 + [has_out, has_near]
    z_arrives = [has_near] * 5 + [has_in, has_near]
    z_place = [(0, 24), (0, 16), (1, 20), (0, 8), (1, 12), (0, 0), (1, 4)]
    pieces = ((0,), (1, 2), (3, 4), (5, 6))
    sent = ((0,), (1, 2, 3, 4, 5, 6), (), ())
    core_place = [(0, OWN_END), (0, OWN_END + 8), (1, OWN_END + 4)]

    def start_blocks(slot, blocks):
        copies = z_copies(slot)
        for i in blocks:
            pl.when(z_valid[i])(copies[i].start)

    def send_early(slot, part):
        if part == 0:
            staged[1] = wave[0, :, pl.ds(48, 8), :]
            staged[3] = wave[1, :, pl.ds(44, 8), :]
            staged[4] = wave[1, :, pl.ds(52, 8), :]
            start_blocks(slot, (5, 6))
        else:
            staged[0] = wave[0, :, pl.ds(40, 8), :]
            staged[2] = wave[1, :, pl.ds(36, 8), :]
            start_blocks(slot, (1, 2))
            for copy in core_copies(slot, round_blocks):
                copy.start()

    def send_round(slot):
        start_blocks(slot, (0, 3, 4))

    round_blocks = [staged.at[1], staged.at[0], staged.at[3]]
    middle_blocks = [staged_core.at[i] for i in range(3)]

    def send_middle(slot):
        staged_core[0] = wave[0, :, pl.ds(48, 8), :]
        staged_core[1] = wave[0, :, pl.ds(40, 8), :]
        staged_core[2] = wave[1, :, pl.ds(44, 8), :]
        for copy in core_copies(slot, middle_blocks):
            copy.start()

    def take_core(slot, blocks):
        for i, copy in enumerate(core_copies(slot, blocks)):
            copy.wait()
            level, row = core_place[i]
            wave[level, :, pl.ds(row, 8), :] = flip(core_land[slot, i], backward_rows)

    def take_piece(slot, piece):
        copies = z_copies(slot)
        for i in sent[piece]:
            pl.when(z_valid[i])(copies[i].wait_send)
        for i in pieces[piece]:

            @pl.when(z_arrives[i])
            def _():
                copies[i].wait_recv()
                level, row = z_place[i]
                block = z_land[slot, i]
                if i != 5:
                    block = flip(block, backward_rows)
                wave[level, :, pl.ds(row, 8), :] = block

    rounds = NT // STEPS

    def run_round(number, sweep, tile):
        taken = sweep * (rounds - 1) + number - 1
        middle = 2 * (rounds - 1) + sweep * rounds + number
        for entry in ordered:
            if entry[0] == "tile":
                tile(entry[1], entry[2])
            elif entry[0] == "middle":
                send_middle(middle)
            elif entry[0] == "early":

                @pl.when(number < rounds - 1)
                def _():
                    send_early(taken + 1, entry[1])
            elif entry[0] == "piece":

                @pl.when(number > 0)
                def _():
                    take_piece(taken, entry[1])

                if sweep == 0:

                    @pl.when(number == 0)
                    def _():
                        first_piece(entry[1])
            elif entry[1] == 0:

                @pl.when(number > 0)
                def _():
                    take_core(taken, round_blocks)

                if sweep == 0:
                    pl.when(number == 0)(first_core)
            else:
                take_core(middle, middle_blocks)

        @pl.when(number < rounds - 1)
        def _():
            send_round(taken + 1)

    def keep_lines(time, level):
        new = wave.at[level]
        for group in range(0, receivers, 16):
            lines = [
                new[inline * OWN_X + rec_layer[r], pl.ds(rec_row[r], 1), :]
                for r in range(group, group + 16)
            ]
            for offset, line in enumerate(lines):
                picked[time, pl.ds(inline * receivers + group + offset, 1), :] = line

    def read_traces(first_time, steps):
        for step in range(steps):
            time = first_time + step
            high, rest = split_two(picked[time] * depth_mask[...])
            row = lax.dot_general(
                ones, jnp.concatenate([high, rest], axis=1), (((1,), (1,)), ((), ())),
                preferred_element_type=jnp.float32,
            )
            traces[pl.ds(time, 1), :] = row[0:1]

    own_tiles = {s: {f for f in tiles_of(s) if f + 8 > Z_HALO and f < OWN_END} for s in range(STEPS)}

    def forward_round(number, carry):
        left = [set(own_tiles[s]) for s in range(STEPS)]

        @pl.when(number > 0)
        def _():
            for step in range(HALF, STEPS):
                keep_lines((number - 1) * STEPS + step, LEVELS[step % 4][2])
            read_traces((number - 1) * STEPS + HALF, HALF)

        def tile(step, first):
            now, old, new = (wave.at[level] for level in LEVELS[step % 4])
            time = number * STEPS + step
            center, laplacian = laplace_tile(now, first, band)
            here = pl.ds(first, 8)
            new[:, here, :] = 2.0 * center - old[:, here, :] + courant[:, here, :] * laplacian
            if first in own_tiles[step]:
                laplacians[time, :, pl.ds(first - Z_HALO + 8, 8), :] = own_half(laplacian, inline)
                left[step].discard(first)
                if step < HALF and not left[step]:
                    keep_lines(time, LEVELS[step % 4][2])

        run_round(number, 0, tile)
        read_traces(number * STEPS, HALF)
        return carry

    lax.fori_loop(0, rounds, forward_round, 0)
    for step in range(HALF, STEPS):
        keep_lines(NT - STEPS + step, LEVELS[step % 4][2])
    read_traces(NT - HALF, HALF)
    traces_all[OWN, inline] = traces[...]
    share_start(traces, traces_all, trace_send, trace_recv)

    synthetic[...] = jnp.zeros(synthetic.shape, jnp.float32)
    products[...] = jnp.zeros(products.shape, jnp.float32)
    synthetic[OWN, pl.ds(8, NT), :] = traces[pl.ds(0, NT), :]
    lagged = [synthetic[OWN, pl.ds(8 - k, NT), :] for k in range(TAPS)]
    recorded = notes[pl.ds(0, NT), :]
    index = 0
    for k in range(TAPS):
        for l in range(k + 1):
            products[pl.ds(index, 1), :] = jnp.sum(lagged[k] * lagged[l], axis=0, keepdims=True)
            index += 1
    for k in range(TAPS):
        products[pl.ds(index + k, 1), :] = jnp.sum(lagged[k] * recorded, axis=0, keepdims=True)
    own_key = notes[pl.ds(NT + 3, 1), :].astype(jnp.int32) - inline * KEYS
    local = (keys[:KEYS] == own_key).astype(jnp.float32)
    partial = lax.dot_general(
        local, products[...], (((1,), (1,)), ((), ())),
        preferred_element_type=jnp.float32, precision=HIGHEST,
    )
    pair_copy(fields.at[2], model, 0).wait()
    apart = jnp.sum(jnp.square(fields[2] - model[...]), axis=0)
    apart = apart[0:8] + apart[8:16] + apart[16:24]
    partial = jnp.where(lane == 127, jnp.sum(apart, axis=1, keepdims=True), partial)
    sums_own[...] = partial
    sums_all[me] = partial

    def sum_copy(step, peer):
        sender = lax.rem(me + size - step, size)
        return remote(
            sums_own, sums_all.at[me if peer else sender], sum_send.at[step], sum_recv.at[step],
            (
                lax.rem(me + step, size) // count if peer else sender // count,
                lax.rem(me + step if peer else sender, count),
                particle,
            ),
        )

    def sum_start(step, carry):
        sum_copy(step, True).start()
        return carry

    lax.fori_loop(1, size, sum_start, 0)

    share_wait(notes, notes_all, note_send, note_recv)
    for column in range(4):
        pair = notes_all[column, 0] + notes_all[column, 1]
        place_row = pair[NT + 1 : NT + 2].astype(jnp.int32)
        frame_row = (place_row - 16, 31 - place_row, Z_HALO + place_row, OWN_END + 23 - place_row)[
            column
        ]
        depth = pair[NT + 2 : NT + 3].astype(jnp.int32)
        fits = (frame_row >= 0) & (frame_row < ROWS)
        row_id = jnp.where(fits, pair[NT : NT + 1].astype(jnp.int32) + frame_row, -1)
        place = (keys == depth).astype(jnp.float32).astype(jnp.bfloat16)
        places[:, pl.ds(256 * column, 128)] = place
        places[:, pl.ds(256 * column + 128, 128)] = place
        for (first, found), slot in hit_slots().items():
            if found == column:
                wanted = (keys // 8) * ROWS + first + lax.rem(keys, 8)
                hit = (wanted == row_id).astype(jnp.float32).astype(jnp.bfloat16)
                hits[slot, :, pl.ds(0, 128)] = hit
                hits[slot, :, pl.ds(128, 128)] = hit
    wave[...] = jnp.zeros(wave.shape, jnp.float32)
    gradient[...] = jnp.zeros(gradient.shape, jnp.float32)
    misfit[...] = jnp.zeros(misfit.shape, jnp.float32)
    turned[...] = jnp.zeros(turned.shape, jnp.float32)

    def sum_wait(step, carry):
        sum_copy(step, True).wait_send()
        sum_copy(step, False).wait_recv()
        return carry

    lax.fori_loop(1, size, sum_wait, 0)
    total = [jnp.zeros((8, 128), jnp.float32) for i in range(2)]
    for row in range(2):
        for column in range(count):
            total[row] = total[row] + sums_all[row * count + column]
        turned[pl.ds(KEYS * row, KEYS), :] = total[row]
    sums = jnp.transpose(turned[...])
    for k, row in enumerate(solve_rows(sums[:48])):
        filters[pl.ds(k, 1), :] = row

    share_wait(traces, traces_all, trace_send, trace_recv)
    for column in range(4):
        both = traces_all[column, 0] + traces_all[column, 1]
        synthetic[column, pl.ds(8, NT), :] = both[:NT]
        pair = notes_all[column, 0] + notes_all[column, 1]
        members = (keys == pair[NT + 3 : NT + 4].astype(jnp.int32)).astype(jnp.float32)
        own = jnp.dot(
            filters[...], members, preferred_element_type=jnp.float32, precision=HIGHEST
        )
        fitted = sum(own[k : k + 1] * synthetic[column, pl.ds(8 - k, NT), :] for k in range(TAPS))
        misfit[column, pl.ds(0, NT), :] = fitted - pair[:NT]
        source = sum(own[k : k + 1] * misfit[column, pl.ds(k, NT), :] for k in range(TAPS))
        high, rest = split_two(source)
        strengths[:, pl.ds(256 * column, 128)] = high.astype(jnp.float32)
        strengths[:, pl.ds(256 * column + 128, 128)] = rest.astype(jnp.float32)

    slots = hit_slots()

    def backward_round(number, carry):
        def tile(step, first):
            now, old, new = (wave.at[level] for level in LEVELS[step % 4])
            time = NT - 1 - (number * STEPS + step)
            strength = strengths[pl.ds(time, 1), :].astype(jnp.bfloat16)
            center, laplacian = laplace_tile(now, first, band)
            here = pl.ds(first, 8)
            added = 0.0
            for column in columns_of(first):
                part = slice(256 * column, 256 * (column + 1))
                added = added + lax.dot_general(
                    hits[slots[first, column]] * strength[:, part],
                    places[:, part],
                    (((1,), (1,)), ((), ())),
                    preferred_element_type=jnp.float32,
                )
            following = 2.0 * center - old[:, here, :] + courant[:, here, :] * laplacian
            following = following + added.reshape(2 * OWN_X, 8, 128)
            new[:, here, :] = following
            if first in own_tiles[step]:
                kept = pl.ds(first - Z_HALO + 8, 8)
                gradient[:, kept, :] = (
                    gradient[:, kept, :]
                    + own_half(following, inline) * laplacians[time, :, kept, :]
                )

        run_round(number, 1, tile)
        return carry

    lax.fori_loop(0, rounds, backward_round, 0)
    for index in range(3):
        gradient_own[:, pl.ds(own_block(index), 8), :] = flip(
            gradient[:, pl.ds(8 + 8 * index, 8), :] * (1.0 / NT), own_rows
        )
    pair_copy(gradient_own, gradient_other, 1).start()
    apart = jnp.where(lane == 127, total[0] + total[1], 0.0)
    apart = jnp.sum(jnp.sum(apart, axis=0, keepdims=True), axis=1, keepdims=True)
    distance = apart / (size * OWN_X * OWN_Y * 128)
    weight = jnp.exp(jnp.broadcast_to(-distance / KERNEL_WIDTH, (8, 128)))[0:1]
    between = 2.0 * (fields[2] - model[...]) / KERNEL_WIDTH
    pair_copy(gradient_own, gradient_other, 1).wait()
    own_term = gradient_own[...] * (-1.0 / NOISE_VARIANCE)
    other_term = gradient_other[...] * (-1.0 / NOISE_VARIANCE) + between
    update[0] = (STEP_SIZE / 2) * (own_term + weight[None] * other_term)


def per_device_pair(velocity, state_now, state_prev, observed, rec_cell, rec_gather):
    count = rec_cell.shape[0]
    size = 2 * lax.axis_size("xline")
    vmem = pl.BlockSpec(memory_space=pltpu.VMEM)
    smem = pl.BlockSpec(memory_space=pltpu.SMEM)
    f32, bf16 = jnp.float32, jnp.bfloat16
    dma = pltpu.SemaphoreType.DMA
    exchanges = 2 * (NT // STEPS - 1)
    halves = exchanges + 2 * (NT // STEPS)
    return pl.pallas_call(
        whole_kernel,
        out_shape=jax.ShapeDtypeStruct(velocity.shape, f32),
        in_specs=[smem] + [pl.BlockSpec(memory_space=pltpu.HBM)] * 6,
        out_specs=vmem,
        scratch_shapes=[
            pltpu.SMEM((count,), jnp.int32),
            pltpu.SMEM((count,), jnp.int32),
            pltpu.VMEM((3, OWN_X, OWN_Y, 128), f32),
            pltpu.VMEM((NT, count), f32),
            pltpu.VMEM((1, count), jnp.int32),
            pltpu.VMEM((1, count), jnp.int32),
            pltpu.VMEM((NT + 8, 128), f32),
            pltpu.VMEM((128, 128), f32),
            dma((6,)),
            pltpu.VMEM((2 * OWN_X, ROWS, 128), f32),
            pltpu.VMEM((4, 2 * OWN_X, ROWS, 128), f32),
            pltpu.VMEM((5, 2 * OWN_X, 8, 128), f32),
            pltpu.VMEM((3, 2 * OWN_X, 8, 128), f32),
            pltpu.VMEM((exchanges, 7, 2 * OWN_X, 8, 128), f32),
            pltpu.VMEM((halves, 3, 2 * OWN_X, 8, 128), f32),
            pltpu.VMEM((3, OWN_X, OWN_Y, 128), f32),
            pltpu.VMEM((3, 2, OWN_X, OWN_Y, 128), f32),
            pltpu.VMEM((3, 2, OWN_X, CORE_HALO, 128), f32),
            pltpu.VMEM((3, 2, OWN_X, 8, 128), f32),
            pltpu.VMEM((NT, OWN_X, OWN_Y + 16, 128), f32),
            pltpu.VMEM((NT, 2 * count, 128), f32),
            pltpu.VMEM((4, 2, NT + 8, 128), f32),
            pltpu.VMEM((NT, 128), f32),
            pltpu.VMEM((4, 2, NT, 128), f32),
            pltpu.VMEM((8, 128), f32),
            pltpu.VMEM((size, 8, 128), f32),
            pltpu.VMEM((128, 128), f32),
            pltpu.VMEM((OWN_X, OWN_Y, 128), f32),
            pltpu.VMEM((4, NT + 8, 128), f32),
            pltpu.VMEM((128, 128), f32),
            pltpu.VMEM((8, 128), f32),
            pltpu.VMEM((4, NT + 8, 128), f32),
            pltpu.VMEM((NT, 1024), f32),
            pltpu.VMEM((len(hit_slots()), 128, 256), bf16),
            pltpu.VMEM((128, 1024), bf16),
            pltpu.VMEM((OWN_X, OWN_Y + 16, 128), f32),
            pltpu.VMEM((OWN_X, OWN_Y, 128), f32),
            pltpu.VMEM((OWN_X, OWN_Y, 128), f32),
            dma((7, 3)),
            dma((7, 3)),
            dma((exchanges, 7)),
            dma((exchanges, 7)),
            dma((halves, 3)),
            dma((halves, 3)),
            dma((7,)),
            dma((7,)),
            dma((7,)),
            dma((7,)),
            dma((size,)),
            dma((size,)),
            dma((2,)),
            dma((2,)),
        ],
        compiler_params=pltpu.CompilerParams(
            collective_id=0, has_side_effects=True, vmem_limit_bytes=58 * 1024 * 1024
        ),
        name="inversion_window",
    )(
        rec_cell, velocity, state_now, state_prev, observed.T, rec_cell.reshape(1, count),
        rec_gather.reshape(1, count),
    )


def solution(mesh):
    shape = mesh.shape
    paired = (shape["inline"], shape["particle"]) == (2, 2) and shape["xline"] in (2, 4, 6, 8)
    return jax.shard_map(
        per_device_pair if paired else per_device,
        mesh=mesh,
        in_specs=(
            P("particle", "inline", "xline", None),
            P("particle", "inline", "xline", None),
            P("particle", "inline", "xline", None),
            P(("inline", "xline"), None),
            P(("inline", "xline")),
            P(("inline", "xline"), None),
        ),
        out_specs=P("particle", "inline", "xline", None),
        check_vma=False,
    )
```

```python
import jax
import jax.numpy as jnp
from jax import lax
from jax.experimental import pallas as pl
from jax.experimental.pallas import tpu as pltpu
from jax.sharding import PartitionSpec as P

NT = 32
CAP = 16
TAPS = 8


COEFFS = (8.0 / 5.0, -1.0 / 5.0, 8.0 / 315.0, -1.0 / 560.0)
CENTER = -205.0 / 72.0
KERNEL_WIDTH = 0.004
NOISE_VARIANCE = 0.0005
STEP_SIZE = 0.01
RIDGE_BASE = 1.0
RIDGE_SHARE = 0.1
HIGHEST = lax.Precision.HIGHEST


def extended(block, sides, width):
    for axis, dim in sides:
        count = lax.axis_size(axis)
        forward = [(i, i + 1) for i in range(count - 1)]
        backward = [(target, source) for source, target in forward]
        low = lax.ppermute(
            lax.slice_in_dim(block, block.shape[dim] - width, None, axis=dim), axis, forward
        )
        high = lax.ppermute(lax.slice_in_dim(block, 0, width, axis=dim), axis, backward)
        block = jnp.concatenate([low, block, high], axis=dim)
    return block


def laplace_inner(block):
    size_x, size_y, size_z = block.shape
    inner_x = size_x - 8
    inner_y = size_y - 8
    padded = jnp.pad(block, ((0, 0), (0, 0), (4, 4)))
    total = 3.0 * CENTER * block[4 : 4 + inner_x, 4 : 4 + inner_y, :]
    for shift in range(1, 5):
        weight = COEFFS[shift - 1]
        beside = padded[4 + shift : 4 + shift + inner_x, 4 : 4 + inner_y, 4 : 4 + size_z]
        beside = beside + padded[4 - shift : 4 - shift + inner_x, 4 : 4 + inner_y, 4 : 4 + size_z]
        beside = beside + padded[4 : 4 + inner_x, 4 + shift : 4 + shift + inner_y, 4 : 4 + size_z]
        beside = beside + padded[4 : 4 + inner_x, 4 - shift : 4 - shift + inner_y, 4 : 4 + size_z]
        beside = beside + padded[4 : 4 + inner_x, 4 : 4 + inner_y, 4 + shift : 4 + shift + size_z]
        beside = beside + padded[4 : 4 + inner_x, 4 : 4 + inner_y, 4 - shift : 4 - shift + size_z]
        total = total + weight * beside
    return total


def lagged_traces(traces):
    steps = traces.shape[1]
    padded = jnp.pad(traces, ((0, 0), (TAPS - 1, 0)))
    return jnp.stack(
        [padded[:, TAPS - 1 - shift : TAPS - 1 - shift + steps] for shift in range(TAPS)], axis=1
    )


def filter_stats(lagged, observed):
    count = lagged.shape[0]
    gram = jnp.einsum("mkt,mlt->mkl", lagged, lagged, precision=HIGHEST).reshape(count, TAPS * TAPS)
    cross = jnp.einsum("mkt,mt->mk", lagged, observed, precision=HIGHEST)
    return (gram, cross)


def solve_filter(gram, cross):
    matrix = gram.reshape(-1, TAPS, TAPS)
    sums = [matrix[:, k, l] for k in range(TAPS) for l in range(k + 1)]
    sums = jnp.stack(sums + [cross[:, k] for k in range(TAPS)])
    return jnp.concatenate(solve_rows(sums), axis=0).T


def adjoint_sources(lagged, observed, filters):
    steps = observed.shape[1]
    fitted = jnp.einsum("mk,mkt->mt", filters, lagged, precision=HIGHEST)
    misfit = fitted - observed
    padded = jnp.pad(misfit, ((0, 0), (0, TAPS - 1)))
    ahead = jnp.stack([padded[:, shift : shift + steps] for shift in range(TAPS)], axis=1)
    return jnp.einsum("mk,mkt->mt", filters, ahead, precision=HIGHEST)


def per_device(velocity, state_now, state_prev, observed, rec_cell, rec_gather):
    courant = velocity[0]
    particles = lax.axis_size("particle")
    models = lax.all_gather(velocity, "particle", axis=0, tiled=True)
    partial_sums = jnp.sum(jnp.square(models - velocity), axis=(1, 2, 3))
    cells_all = courant.size * lax.axis_size("inline") * lax.axis_size("xline")
    distance = lax.psum(partial_sums, ("inline", "xline")) / cells_all
    kernel = jnp.exp(-distance / KERNEL_WIDTH)

    def advance(carry, unused):
        current, previous = carry
        padded = extended(current[None], (("inline", 1), ("xline", 2)), 4)[0]
        laplacian = laplace_inner(padded)
        following = 2.0 * current - previous + courant * laplacian
        return ((following, current), (laplacian, following.reshape(-1)[rec_cell]))

    unused, (laplacians, traces) = lax.scan(advance, (state_now[0], state_prev[0]), None, length=NT)
    synthetic = traces.T
    steps = observed.shape[1]
    xline_count = lax.axis_size("xline")
    target = rec_gather[:, 0]
    choose = (target[:, None] == jnp.arange(xline_count, dtype=jnp.int32)[None, :]).astype(
        jnp.int32
    )
    order = jnp.arange(target.shape[0], dtype=jnp.int32)
    earlier = (order[None, :] < order[:, None]).astype(jnp.float32)
    before = jnp.dot(earlier, choose.astype(jnp.float32), precision=HIGHEST).astype(jnp.int32)
    position = target * CAP + jnp.sum(before * choose, axis=1)
    outgoing = jnp.zeros((xline_count * CAP, 2 * steps), jnp.float32)
    outgoing = outgoing.at[position].set(jnp.concatenate([synthetic, observed], axis=1))
    arrived = lax.all_to_all(
        outgoing.reshape(xline_count, CAP, 2 * steps),
        "xline",
        split_axis=0,
        concat_axis=0,
        tiled=True,
    )
    slots = arrived.reshape(xline_count * CAP, 2 * steps)
    slot_lagged = lagged_traces(slots[:, :steps])
    slot_observed = slots[:, steps:]
    gram, cross = filter_stats(slot_lagged, slot_observed)
    filters_one = solve_filter(
        jnp.sum(gram, axis=0, keepdims=True), jnp.sum(cross, axis=0, keepdims=True)
    )
    filters = jnp.broadcast_to(filters_one, (slots.shape[0], TAPS))
    slot_adjoint = adjoint_sources(slot_lagged, slot_observed, filters)
    returned = lax.all_to_all(
        slot_adjoint.reshape(xline_count, CAP, steps),
        "xline",
        split_axis=0,
        concat_axis=0,
        tiled=True,
    )
    adjoint_source = returned.reshape(xline_count * CAP, steps)[position]

    def backward(carry, inputs):
        wave, wave_old, gradient = carry
        laplacian, source = inputs
        padded = extended(wave[None], (("inline", 1), ("xline", 2)), 4)[0]
        wave_new = 2.0 * wave - wave_old + courant * laplace_inner(padded)
        wave_new = wave_new.reshape(-1).at[rec_cell].add(source).reshape(wave.shape)
        return ((wave_new, wave, gradient + wave_new * laplacian), None)

    zeros_field = jnp.zeros(courant.shape, jnp.float32)
    (wave, wave_old, gradient), unused = lax.scan(
        backward,
        (zeros_field, zeros_field, zeros_field),
        (laplacians, adjoint_source.T),
        reverse=True,
    )
    gradient = gradient / NT
    gradients = lax.all_gather(gradient[None], "particle", axis=0, tiled=True)
    terms = -gradients / NOISE_VARIANCE + 2.0 * (velocity - models) / KERNEL_WIDTH
    update = (
        STEP_SIZE / particles * jnp.sum(kernel[:, None, None, None] * terms, axis=0, keepdims=True)
    )
    return update


STEPS = 8
HALF = 4
Z_HALO = 4 * STEPS
CORE_HALO = 4 * HALF
OWN_X = 8
OWN_Y = Z_HALO - 8
OWN_END = Z_HALO + OWN_Y
ROWS = OWN_END + CORE_HALO
KEYS = 8
INTEGER_COEFFS = (8064.0, -1008.0, 128.0, -9.0)
INTEGER_SCALE = 1.0 / 5040.0
LEVELS = ((0, 1, 2), (2, 0, 3), (3, 2, 1), (1, 3, 0))
MESH = pl.DeviceIdType.MESH
SECOND, NEAR, OWN, CORE = range(4)
SPANS = ((0, 8), (8, Z_HALO), (Z_HALO, OWN_END), (OWN_END, ROWS))


def split_two(value):
    high = value.astype(jnp.bfloat16)
    rest = (value - high.astype(jnp.float32)).astype(jnp.bfloat16)
    return high, rest


def band_matrix():
    row = lax.broadcasted_iota(jnp.int32, (256, 128), 0) % 128
    col = lax.broadcasted_iota(jnp.int32, (256, 128), 1)
    away = jnp.abs(row - col)
    band = jnp.zeros((256, 128), jnp.float32)
    for shift in range(1, 5):
        band = jnp.where(away == shift, INTEGER_COEFFS[shift - 1], band)
    return band.astype(jnp.bfloat16)


def laplace_tile(wave, first, band):
    center = wave[:, pl.ds(first, 8), :]
    layers = center.shape[0]
    line = [center[i] for i in range(layers)]
    high, rest = split_two(center.reshape(layers * 8, 128))
    depth = jnp.dot(
        jnp.concatenate([high, rest], axis=1), band, preferred_element_type=jnp.float32
    ).reshape(layers, 8, 128)
    parts = [3.0 * CENTER / INTEGER_SCALE * line[i] + depth[i] for i in range(layers)]
    for shift in range(1, 5):
        beside = wave[:, pl.ds(first + shift, 8), :] + wave[:, pl.ds(first - shift, 8), :]
        for i in range(layers):
            sums = beside[i]
            if i + shift < layers:
                sums = sums + line[i + shift]
            if i >= shift:
                sums = sums + line[i - shift]
            parts[i] = parts[i] + INTEGER_COEFFS[shift - 1] * sums
    return center, jnp.stack(parts, axis=0)


def own_half(value, inline):
    return jnp.where(inline == 0, value[:OWN_X], value[OWN_X:])


def solve_rows(sums):
    entry = {}
    index = 0
    for k in range(TAPS):
        for l in range(k + 1):
            entry[k, l] = sums[index : index + 1]
            index += 1
    right = [sums[index + k : index + k + 1] for k in range(TAPS)]
    trace_sum = sum(entry[k, k] for k in range(TAPS))
    ridge = RIDGE_BASE + RIDGE_SHARE * trace_sum / TAPS
    for k in range(TAPS):
        entry[k, k] = entry[k, k] + ridge
    inverse = []
    for k in range(TAPS):
        inverse.append(1.0 / entry[k, k])
        factor = {i: entry[i, k] * inverse[k] for i in range(k + 1, TAPS)}
        for i in range(k + 1, TAPS):
            for l in range(k + 1, i + 1):
                entry[i, l] = entry[i, l] - factor[i] * entry[l, k]
            right[i] = right[i] - factor[i] * right[k]
        for i in range(k + 1, TAPS):
            entry[i, k] = factor[i]
    right = [right[k] * inverse[k] for k in range(TAPS)]
    for k in reversed(range(TAPS)):
        for i in range(k):
            right[i] = right[i] - entry[k, i] * right[k]
    return right


def tiles_of(step):
    first = 4 * (step + 1)
    return range(first, OWN_END + 4 * (HALF - 1 - step % HALF), 8)


def plan():
    first_half = [(s, f) for s in range(HALF) for f in tiles_of(s)]
    later = [(s, f) for s in range(HALF, STEPS) for f in tiles_of(s)]
    order, done = [], set()

    def ready(step, first, pieces, core, core_later):
        if Z_HALO - (first - 4 * (step + 1)) > 8 * pieces:
            return False
        reach = first + 8 + 4 * (step % HALF + 1)
        if reach > OWN_END and not (core if step < HALF else core_later):
            return False
        if step == 0:
            return True
        if step >= HALF and any(
            f + 8 > Z_HALO and f < OWN_END and (step - HALF, f) not in done
            for f in tiles_of(step - HALF)
        ):
            return False
        span = range(first - 4, first + 12)
        covered = {r for s, f in done if s == step - 1 for r in range(f, f + 8)}
        if step == HALF:
            return all(r in covered for r in span if r < OWN_END)
        return all(r in covered for r in span)

    def take(tiles, pieces, core, core_later):
        changed = True
        while changed:
            changed = False
            for step, first in tiles:
                if (step, first) not in done and ready(step, first, pieces, core, core_later):
                    done.add((step, first))
                    order.append(("tile", step, first))
                    changed = True

    both = first_half + later
    take(both, 0, False, False)
    order.append(("core", 0))
    take(both, 0, True, False)
    order.append(("piece", 0))
    take(first_half, 1, True, False)
    order.append(("middle",))
    take(both, 1, True, False)
    order.append(("piece", 1))
    take(both, 2, True, False)
    order.append(("core", 1))
    take(both, 2, True, True)
    order.append(("early", 0))
    order.append(("piece", 2))
    order.append(("piece", 3))
    left = [tile for tile in both if tile not in done]
    for step, first in sorted(left, key=lambda t: t[0] + 1.5 * (t[1] == 4 * (t[0] + 1)))[:-1]:
        assert ready(step, first, 4, True, True)
        done.add((step, first))
        order.append(("tile", step, first))
    take(both, 4, True, True)
    order.append(("early", 1))
    assert len(done) == len(both)
    return order


def columns_of(first):
    return [c for c, (start, stop) in enumerate(SPANS) if first < stop and first + 8 > start]


def hit_slots():
    slots = {}
    for step in range(STEPS):
        for first in tiles_of(step):
            for column in columns_of(first):
                slots.setdefault((first, column), len(slots))
    return slots


def flip(block, index):
    return jnp.stack(
        [jnp.take_along_axis(block[i], index, axis=0) for i in range(block.shape[0])], axis=0
    )


def whole_kernel(
    rec_cell, velocity, state_now, state_prev, observed, cells, gathers, update,
    rec_layer, rec_row, fields, seen, cell_row, gather_row, notes, depth_mask, local_sem, courant, wave, staged, staged_core, z_land, core_land, x_first, near_first, core_first,
    second_first, laplacians, picked, notes_all, traces, traces_all, sums_own, sums_all, turned,
    model, synthetic, products, filters, misfit, strengths, hits, places, gradient, gradient_own,
    gradient_other, start_send, start_recv, z_send, z_recv, core_send, core_recv, note_send,
    note_recv, trace_send, trace_recv, sum_send, sum_recv, pair_send, pair_recv,
):
    inline, xline, particle = (lax.axis_index(a) for a in ("inline", "xline", "particle"))
    count = lax.axis_size("xline")
    size = 2 * count
    me = inline * count + xline
    receivers = rec_cell.shape[0]
    odd = lax.rem(xline, 2)
    toward = 1 - 2 * odd
    other = 1 - inline
    near, core = xline - toward, xline + toward
    second_in, second_out = xline - 2 * toward, xline + 2 * toward
    has_near = (near >= 0) & (near < count)
    has_in = (second_in >= 0) & (second_in < count)
    has_out = (second_out >= 0) & (second_out < count)
    always = xline >= 0
    sources = [fields.at[pl.ds(kind, 1)] for kind in range(3)]
    frames = (wave.at[0], wave.at[1], courant)
    sublane = lax.broadcasted_iota(jnp.int32, (8, 128), 0)
    backward_rows = 7 - sublane
    own_rows = jnp.where(odd == 1, 7 - sublane, sublane)

    inputs = [
        pltpu.make_async_copy(source, target, local_sem.at[i])
        for i, (source, target) in enumerate(
            [
                (observed, seen),
                (cells, cell_row),
                (gathers, gather_row),
                (state_now.at[0], fields.at[0]),
                (state_prev.at[0], fields.at[1]),
                (velocity.at[0], fields.at[2]),
            ]
        )
    ]
    for copy in inputs:
        copy.start()
    barrier = pltpu.get_barrier_semaphore()

    def greet(step, carry):
        peer = lax.rem(me + step, size)
        pl.semaphore_signal(
            barrier, inc=1, device_id=(peer // count, lax.rem(peer, count), particle),
            device_id_type=MESH,
        )
        return carry

    lax.fori_loop(1, size, greet, 0)
    pl.semaphore_signal(
        barrier, inc=1, device_id=(inline, xline, 1 - particle), device_id_type=MESH
    )

    for r in range(receivers):
        line = rec_cell[r] >> 7
        layer = (line * 2731) >> 16
        row = line - layer * OWN_Y
        rec_layer[r] = layer
        rec_row[r] = Z_HALO + row + odd * (OWN_Y - 1 - 2 * row)
    for copy in inputs:
        copy.wait()
    pl.semaphore_wait(barrier, size)

    routes = [
        (always, always, (other, xline, particle), OWN),
        (always, always, (inline, core, particle), CORE),
        (always, always, (other, core, particle), CORE),
        (has_near, has_near, (inline, near, particle), NEAR),
        (has_near, has_near, (other, near, particle), NEAR),
        (has_out, has_in, (inline, second_out, particle), SECOND),
        (has_out, has_in, (other, second_out, particle), SECOND),
    ]
    origins = (other, inline, other, inline, other, inline, other)

    def remote(source, target, send, recv, device):
        return pltpu.make_async_remote_copy(
            src_ref=source, dst_ref=target, send_sem=send, recv_sem=recv, device_id=device,
            device_id_type=MESH,
        )

    def start_copy(index, kind, arriving=False):
        column = routes[index][3]
        passed_on = index in (2, 4, 6)
        origin = other if passed_on or (arriving and index == 0) else inline
        if column == OWN:
            first, extent, landing = 0, OWN_Y, x_first.at[kind]
        elif column == NEAR:
            first, extent, landing = 0, OWN_Y, near_first.at[kind, origin]
        elif column == CORE:
            first, extent, landing = 8 * (1 - odd), CORE_HALO, core_first.at[kind, origin]
        else:
            first, extent, landing = 16 * (1 - odd), 8, second_first.at[kind, origin]
        rows = pl.ds(first if isinstance(first, int) else pl.multiple_of(first, 8), extent)
        source = x_first.at[kind, :, rows, :] if passed_on else sources[kind].at[0, :, rows, :]
        target = routes[index - 1 if passed_on else index][2]
        return remote(
            source, landing, start_send.at[index, kind], start_recv.at[index, kind], target
        )

    def start_all(index, kind):
        @pl.when(routes[index][0])
        def _():
            start_copy(index, kind).start()

    def finish_first(indices):
        for index in indices:
            for kind in range(3):

                @pl.when(routes[index][0])
                def _():
                    start_copy(index, kind).wait_send()

                @pl.when(routes[index][1])
                def _():
                    start_copy(index, kind, True).wait_recv()

    for index in (0, 3, 1, 5):
        for kind in range(3):
            start_all(index, kind)

    def pair_copy(source, target, index):
        return remote(
            source, target, pair_send.at[index], pair_recv.at[index], (inline, xline, 1 - particle)
        )

    pair_copy(fields.at[2], model, 0).start()

    def share(source, table, send, recv, origin, index):
        return remote(
            source, table.at[routes[index][3], origin], send.at[index], recv.at[index],
            routes[index][2],
        )

    def share_start(source, table, send, recv):
        for index in range(7):

            @pl.when(routes[index][0])
            def _():
                share(source, table, send, recv, inline, index).start()

    def share_wait(source, table, send, recv):
        for index in range(7):

            @pl.when(routes[index][0])
            def _():
                share(source, table, send, recv, inline, index).wait_send()

            @pl.when(routes[index][1])
            def _():
                share(source, table, send, recv, origins[index], index).wait_recv()

    layers = pl.ds(inline * OWN_X, OWN_X)
    layers_other = pl.ds(other * OWN_X, OWN_X)

    def own_block(index):
        return pl.multiple_of(8 * (index + odd * (2 - 2 * index)), 8)

    for kind in range(3):
        for index in range(3):
            scale = INTEGER_SCALE if kind == 2 else 1.0
            frames[kind][layers, pl.ds(Z_HALO + 8 * index, 8), :] = scale * flip(
                fields[kind, :, pl.ds(own_block(index), 8), :], own_rows
            )

    @pl.when(jnp.logical_not(has_near))
    def _():
        for frame in frames:
            frame[:, pl.ds(8, Z_HALO - 8), :] = jnp.zeros((2 * OWN_X, Z_HALO - 8, 128), jnp.float32)
        notes_all[NEAR] = jnp.zeros(notes_all.shape[1:], jnp.float32)
        traces_all[NEAR] = jnp.zeros(traces_all.shape[1:], jnp.float32)

    @pl.when(jnp.logical_not(has_in))
    def _():
        for frame in frames:
            frame[:, pl.ds(0, 8), :] = jnp.zeros((2 * OWN_X, 8, 128), jnp.float32)
        notes_all[SECOND] = jnp.zeros(notes_all.shape[1:], jnp.float32)
        traces_all[SECOND] = jnp.zeros(traces_all.shape[1:], jnp.float32)

    lane = lax.broadcasted_iota(jnp.int32, (8, 128), 1)
    here = (lane // receivers) == inline
    cell = jnp.concatenate([cell_row[...], cell_row[...]], axis=1)
    gather = jnp.concatenate([gather_row[...], gather_row[...]], axis=1)
    line = cell >> 7
    layer = (line * 2731) >> 16
    row = line - layer * OWN_Y
    facts = [
        (inline * OWN_X + layer) * ROWS,
        row + odd * (OWN_Y - 1 - 2 * row),
        cell & 127,
        inline * KEYS + gather,
    ]
    for block in range(0, NT, 8):
        part = seen[pl.ds(block, 8), :]
        notes[pl.ds(block, 8), :] = jnp.where(here, jnp.concatenate([part, part], axis=1), 0.0)
    notes[pl.ds(NT, 8), :] = jnp.zeros((8, 128), jnp.float32)
    for i, fact in enumerate(facts):
        notes[pl.ds(NT + i, 1), :] = jnp.where(here[0:1], fact.astype(jnp.float32), 0.0)
    keys = lax.broadcasted_iota(jnp.int32, (128, 128), 0)
    depth_mask[...] = jnp.transpose((keys == (cell & 127)).astype(jnp.float32))
    notes_all[OWN, inline] = notes[...]
    picked[:, pl.ds(other * receivers, receivers), :] = jnp.zeros(
        (NT, receivers, 128), jnp.float32
    )
    first_layers = (pl.ds(0, OWN_X), pl.ds(OWN_X, OWN_X))

    def first_core():
        finish_first((1, 2))
        for kind in range(3):
            scale = INTEGER_SCALE if kind == 2 else 1.0
            for half in range(2):
                for block in range(2):
                    at = pl.multiple_of(8 * (block + odd * (1 - 2 * block)), 8)
                    frames[kind][first_layers[half], pl.ds(OWN_END + 8 * block, 8), :] = scale * flip(
                        core_first[kind, half, :, pl.ds(at, 8), :], own_rows
                    )

    def first_piece(piece):
        if piece == 0:
            finish_first((3, 4))
        if piece == 3:
            finish_first((5, 6))

        @pl.when(has_in if piece == 3 else has_near)
        def _():
            for kind in range(3):
                scale = INTEGER_SCALE if kind == 2 else 1.0
                for half in range(2):
                    if piece == 3:
                        block = second_first[kind, half]
                    else:
                        block = near_first[kind, half, :, pl.ds(own_block(2 - piece), 8), :]
                    frames[kind][first_layers[half], pl.ds(24 - 8 * piece, 8), :] = scale * flip(
                        block, own_rows
                    )

    for kind in range(3):
        start_copy(0, kind).wait_send()
        start_copy(0, kind, True).wait_recv()
        for index in (4, 2, 6):
            start_all(index, kind)
    for kind in range(3):
        for block in range(3):
            scale = INTEGER_SCALE if kind == 2 else 1.0
            frames[kind][layers_other, pl.ds(Z_HALO + 8 * block, 8), :] = scale * flip(
                x_first[kind, :, pl.ds(own_block(block), 8), :], own_rows
            )
    share_start(notes, notes_all, note_send, note_recv)

    band = band_matrix()
    ones = jnp.ones((8, 256), jnp.bfloat16)
    ordered = plan()

    def z_copies(slot):
        to_near, to_second = (inline, near, particle), (inline, second_out, particle)
        blocks = [
            (wave.at[0, :, pl.ds(Z_HALO, 8), :], 0, to_near),
            (staged.at[0], 1, to_near),
            (staged.at[2], 2, to_near),
            (staged.at[1], 3, to_near),
            (staged.at[3], 4, to_near),
            (staged.at[1], 5, to_second),
            (staged.at[4], 6, to_near),
        ]
        return [
            remote(source, z_land.at[slot, i], z_send.at[slot, i], z_recv.at[slot, i], target)
            for source, i, target in blocks
        ]

    def core_copies(slot, blocks):
        return [
            remote(
                block, core_land.at[slot, i], core_send.at[slot, i], core_recv.at[slot, i],
                (inline, core, particle),
            )
            for i, block in enumerate(blocks)
        ]

    z_valid = [has_near] * 5 + [has_out, has_near]
    z_arrives = [has_near] * 5 + [has_in, has_near]
    z_place = [(0, 24), (0, 16), (1, 20), (0, 8), (1, 12), (0, 0), (1, 4)]
    pieces = ((0,), (1, 2), (3, 4), (5, 6))
    sent = ((0,), (1, 2, 3, 4, 5, 6), (), ())
    core_place = [(0, OWN_END), (0, OWN_END + 8), (1, OWN_END + 4)]

    def start_blocks(slot, blocks):
        copies = z_copies(slot)
        for i in blocks:
            pl.when(z_valid[i])(copies[i].start)

    def send_early(slot, part):
        if part == 0:
            staged[1] = wave[0, :, pl.ds(48, 8), :]
            staged[3] = wave[1, :, pl.ds(44, 8), :]
            staged[4] = wave[1, :, pl.ds(52, 8), :]
            start_blocks(slot, (5, 6))
        else:
            staged[0] = wave[0, :, pl.ds(40, 8), :]
            staged[2] = wave[1, :, pl.ds(36, 8), :]
            start_blocks(slot, ())
            for copy in core_copies(slot, round_blocks):
                copy.start()

    def send_round(slot):
        start_blocks(slot, (0, 1, 2, 3, 4))

    round_blocks = [staged.at[1], staged.at[0], staged.at[3]]
    middle_blocks = [staged_core.at[i] for i in range(3)]

    def send_middle(slot):
        staged_core[0] = wave[0, :, pl.ds(48, 8), :]
        staged_core[1] = wave[0, :, pl.ds(40, 8), :]
        staged_core[2] = wave[1, :, pl.ds(44, 8), :]
        for copy in core_copies(slot, middle_blocks):
            copy.start()

    def take_core(slot, blocks):
        for i, copy in enumerate(core_copies(slot, blocks)):
            copy.wait()
            level, row = core_place[i]
            wave[level, :, pl.ds(row, 8), :] = flip(core_land[slot, i], backward_rows)

    def take_piece(slot, piece):
        copies = z_copies(slot)
        for i in sent[piece]:
            pl.when(z_valid[i])(copies[i].wait_send)
        for i in pieces[piece]:

            @pl.when(z_arrives[i])
            def _():
                copies[i].wait_recv()
                level, row = z_place[i]
                block = z_land[slot, i]
                if i != 5:
                    block = flip(block, backward_rows)
                wave[level, :, pl.ds(row, 8), :] = block

    rounds = NT // STEPS

    def run_round(number, sweep, tile):
        taken = sweep * (rounds - 1) + number - 1
        middle = 2 * (rounds - 1) + sweep * rounds + number
        for entry in ordered:
            if entry[0] == "tile":
                tile(entry[1], entry[2])
            elif entry[0] == "middle":
                send_middle(middle)
            elif entry[0] == "early":

                @pl.when(number < rounds - 1)
                def _():
                    send_early(taken + 1, entry[1])
            elif entry[0] == "piece":

                @pl.when(number > 0)
                def _():
                    take_piece(taken, entry[1])

                if sweep == 0:

                    @pl.when(number == 0)
                    def _():
                        first_piece(entry[1])
            elif entry[1] == 0:

                @pl.when(number > 0)
                def _():
                    take_core(taken, round_blocks)

                if sweep == 0:
                    pl.when(number == 0)(first_core)
            else:
                take_core(middle, middle_blocks)

        @pl.when(number < rounds - 1)
        def _():
            send_round(taken + 1)

    def keep_lines(time, level):
        new = wave.at[level]
        for group in range(0, receivers, 16):
            lines = [
                new[inline * OWN_X + rec_layer[r], pl.ds(rec_row[r], 1), :]
                for r in range(group, group + 16)
            ]
            for offset, line in enumerate(lines):
                picked[time, pl.ds(inline * receivers + group + offset, 1), :] = line

    def read_traces(first_time, steps):
        for step in range(steps):
            time = first_time + step
            high, rest = split_two(picked[time] * depth_mask[...])
            row = lax.dot_general(
                ones, jnp.concatenate([high, rest], axis=1), (((1,), (1,)), ((), ())),
                preferred_element_type=jnp.float32,
            )
            traces[pl.ds(time, 1), :] = row[0:1]

    own_tiles = {s: {f for f in tiles_of(s) if f + 8 > Z_HALO and f < OWN_END} for s in range(STEPS)}

    def forward_round(number, carry):
        left = [set(own_tiles[s]) for s in range(STEPS)]

        @pl.when(number > 0)
        def _():
            for step in range(HALF, STEPS):
                keep_lines((number - 1) * STEPS + step, LEVELS[step % 4][2])
            read_traces((number - 1) * STEPS + HALF, HALF)

        def tile(step, first):
            now, old, new = (wave.at[level] for level in LEVELS[step % 4])
            time = number * STEPS + step
            center, laplacian = laplace_tile(now, first, band)
            here = pl.ds(first, 8)
            new[:, here, :] = 2.0 * center - old[:, here, :] + courant[:, here, :] * laplacian
            if first in own_tiles[step]:
                laplacians[time, :, pl.ds(first - Z_HALO + 8, 8), :] = own_half(laplacian, inline)
                left[step].discard(first)
                if step < HALF and not left[step]:
                    keep_lines(time, LEVELS[step % 4][2])

        run_round(number, 0, tile)
        read_traces(number * STEPS, HALF)
        return carry

    lax.fori_loop(0, rounds, forward_round, 0)
    for step in range(HALF, STEPS):
        keep_lines(NT - STEPS + step, LEVELS[step % 4][2])
    read_traces(NT - HALF, HALF)
    traces_all[OWN, inline] = traces[...]
    share_start(traces, traces_all, trace_send, trace_recv)

    synthetic[...] = jnp.zeros(synthetic.shape, jnp.float32)
    products[...] = jnp.zeros(products.shape, jnp.float32)
    synthetic[OWN, pl.ds(8, NT), :] = traces[pl.ds(0, NT), :]
    lagged = [synthetic[OWN, pl.ds(8 - k, NT), :] for k in range(TAPS)]
    recorded = notes[pl.ds(0, NT), :]
    index = 0
    for k in range(TAPS):
        for l in range(k + 1):
            products[pl.ds(index, 1), :] = jnp.sum(lagged[k] * lagged[l], axis=0, keepdims=True)
            index += 1
    for k in range(TAPS):
        products[pl.ds(index + k, 1), :] = jnp.sum(lagged[k] * recorded, axis=0, keepdims=True)
    own_key = notes[pl.ds(NT + 3, 1), :].astype(jnp.int32) - inline * KEYS
    local = (keys[:KEYS] == own_key).astype(jnp.float32)
    partial = lax.dot_general(
        local, products[...], (((1,), (1,)), ((), ())),
        preferred_element_type=jnp.float32, precision=HIGHEST,
    )
    pair_copy(fields.at[2], model, 0).wait()
    apart = jnp.sum(jnp.square(fields[2] - model[...]), axis=0)
    apart = apart[0:8] + apart[8:16] + apart[16:24]
    partial = jnp.where(lane == 127, jnp.sum(apart, axis=1, keepdims=True), partial)
    sums_own[...] = partial
    sums_all[me] = partial

    def sum_copy(step, peer):
        sender = lax.rem(me + size - step, size)
        return remote(
            sums_own, sums_all.at[me if peer else sender], sum_send.at[step], sum_recv.at[step],
            (
                lax.rem(me + step, size) // count if peer else sender // count,
                lax.rem(me + step if peer else sender, count),
                particle,
            ),
        )

    def sum_start(step, carry):
        sum_copy(step, True).start()
        return carry

    lax.fori_loop(1, size, sum_start, 0)

    share_wait(notes, notes_all, note_send, note_recv)
    for column in range(4):
        pair = notes_all[column, 0] + notes_all[column, 1]
        place_row = pair[NT + 1 : NT + 2].astype(jnp.int32)
        frame_row = (place_row - 16, 31 - place_row, Z_HALO + place_row, OWN_END + 23 - place_row)[
            column
        ]
        depth = pair[NT + 2 : NT + 3].astype(jnp.int32)
        fits = (frame_row >= 0) & (frame_row < ROWS)
        row_id = jnp.where(fits, pair[NT : NT + 1].astype(jnp.int32) + frame_row, -1)
        place = jnp.transpose((keys == depth).astype(jnp.float32)).astype(jnp.bfloat16)
        places[column, pl.ds(0, 128), :] = place
        places[column, pl.ds(128, 128), :] = place
        for (first, found), slot in hit_slots().items():
            if found == column:
                wanted = (keys // 8) * ROWS + first + lax.rem(keys, 8)
                hit = (wanted == row_id).astype(jnp.float32).astype(jnp.bfloat16)
                hits[slot, :, pl.ds(0, 128)] = hit
                hits[slot, :, pl.ds(128, 128)] = hit
    wave[...] = jnp.zeros(wave.shape, jnp.float32)
    gradient[...] = jnp.zeros(gradient.shape, jnp.float32)
    misfit[...] = jnp.zeros(misfit.shape, jnp.float32)
    turned[...] = jnp.zeros(turned.shape, jnp.float32)

    def sum_wait(step, carry):
        sum_copy(step, True).wait_send()
        sum_copy(step, False).wait_recv()
        return carry

    lax.fori_loop(1, size, sum_wait, 0)
    total = [jnp.zeros((8, 128), jnp.float32) for i in range(2)]
    for row in range(2):
        for column in range(count):
            total[row] = total[row] + sums_all[row * count + column]
        turned[pl.ds(KEYS * row, KEYS), :] = total[row]
    sums = jnp.transpose(turned[...])
    for k, row in enumerate(solve_rows(sums[:48])):
        filters[pl.ds(k, 1), :] = row

    share_wait(traces, traces_all, trace_send, trace_recv)
    for column in range(4):
        both = traces_all[column, 0] + traces_all[column, 1]
        synthetic[column, pl.ds(8, NT), :] = both[:NT]
        pair = notes_all[column, 0] + notes_all[column, 1]
        members = (keys == pair[NT + 3 : NT + 4].astype(jnp.int32)).astype(jnp.float32)
        own = jnp.dot(
            filters[...], members, preferred_element_type=jnp.float32, precision=HIGHEST
        )
        fitted = sum(own[k : k + 1] * synthetic[column, pl.ds(8 - k, NT), :] for k in range(TAPS))
        misfit[column, pl.ds(0, NT), :] = fitted - pair[:NT]
        source = sum(own[k : k + 1] * misfit[column, pl.ds(k, NT), :] for k in range(TAPS))
        high, rest = split_two(source)
        strengths[:, pl.ds(256 * column, 128)] = high.astype(jnp.float32)
        strengths[:, pl.ds(256 * column + 128, 128)] = rest.astype(jnp.float32)

    slots = hit_slots()

    def backward_round(number, carry):
        def tile(step, first):
            now, old, new = (wave.at[level] for level in LEVELS[step % 4])
            time = NT - 1 - (number * STEPS + step)
            strength = strengths[pl.ds(time, 1), :].astype(jnp.bfloat16)
            center, laplacian = laplace_tile(now, first, band)
            here = pl.ds(first, 8)
            added = 0.0
            for column in columns_of(first):
                part = slice(256 * column, 256 * (column + 1))
                added = added + jnp.dot(
                    hits[slots[first, column]] * strength[:, part],
                    places[column],
                    preferred_element_type=jnp.float32,
                )
            following = 2.0 * center - old[:, here, :] + courant[:, here, :] * laplacian
            following = following + added.reshape(2 * OWN_X, 8, 128)
            new[:, here, :] = following
            if first in own_tiles[step]:
                kept = pl.ds(first - Z_HALO + 8, 8)
                gradient[:, kept, :] = (
                    gradient[:, kept, :]
                    + own_half(following, inline) * laplacians[time, :, kept, :]
                )

        run_round(number, 1, tile)
        return carry

    lax.fori_loop(0, rounds, backward_round, 0)
    for index in range(3):
        gradient_own[:, pl.ds(own_block(index), 8), :] = flip(
            gradient[:, pl.ds(8 + 8 * index, 8), :] * (INTEGER_SCALE / NT), own_rows
        )
    pair_copy(gradient_own, gradient_other, 1).start()
    apart = jnp.where(lane == 127, total[0] + total[1], 0.0)
    apart = jnp.sum(jnp.sum(apart, axis=0, keepdims=True), axis=1, keepdims=True)
    distance = apart / (size * OWN_X * OWN_Y * 128)
    weight = jnp.exp(jnp.broadcast_to(-distance / KERNEL_WIDTH, (8, 128)))[0:1]
    between = 2.0 * (fields[2] - model[...]) / KERNEL_WIDTH
    pair_copy(gradient_own, gradient_other, 1).wait()
    own_term = gradient_own[...] * (-1.0 / NOISE_VARIANCE)
    other_term = gradient_other[...] * (-1.0 / NOISE_VARIANCE) + between
    update[0] = (STEP_SIZE / 2) * (own_term + weight[None] * other_term)


def per_device_pair(velocity, state_now, state_prev, observed, rec_cell, rec_gather):
    count = rec_cell.shape[0]
    size = 2 * lax.axis_size("xline")
    vmem = pl.BlockSpec(memory_space=pltpu.VMEM)
    smem = pl.BlockSpec(memory_space=pltpu.SMEM)
    f32, bf16 = jnp.float32, jnp.bfloat16
    dma = pltpu.SemaphoreType.DMA
    exchanges = 2 * (NT // STEPS - 1)
    halves = exchanges + 2 * (NT // STEPS)
    return pl.pallas_call(
        whole_kernel,
        out_shape=jax.ShapeDtypeStruct(velocity.shape, f32),
        in_specs=[smem] + [pl.BlockSpec(memory_space=pltpu.HBM)] * 6,
        out_specs=vmem,
        scratch_shapes=[
            pltpu.SMEM((count,), jnp.int32),
            pltpu.SMEM((count,), jnp.int32),
            pltpu.VMEM((3, OWN_X, OWN_Y, 128), f32),
            pltpu.VMEM((NT, count), f32),
            pltpu.VMEM((1, count), jnp.int32),
            pltpu.VMEM((1, count), jnp.int32),
            pltpu.VMEM((NT + 8, 128), f32),
            pltpu.VMEM((128, 128), f32),
            dma((6,)),
            pltpu.VMEM((2 * OWN_X, ROWS, 128), f32),
            pltpu.VMEM((4, 2 * OWN_X, ROWS, 128), f32),
            pltpu.VMEM((5, 2 * OWN_X, 8, 128), f32),
            pltpu.VMEM((3, 2 * OWN_X, 8, 128), f32),
            pltpu.VMEM((exchanges, 7, 2 * OWN_X, 8, 128), f32),
            pltpu.VMEM((halves, 3, 2 * OWN_X, 8, 128), f32),
            pltpu.VMEM((3, OWN_X, OWN_Y, 128), f32),
            pltpu.VMEM((3, 2, OWN_X, OWN_Y, 128), f32),
            pltpu.VMEM((3, 2, OWN_X, CORE_HALO, 128), f32),
            pltpu.VMEM((3, 2, OWN_X, 8, 128), f32),
            pltpu.VMEM((NT, OWN_X, OWN_Y + 16, 128), f32),
            pltpu.VMEM((NT, 2 * count, 128), f32),
            pltpu.VMEM((4, 2, NT + 8, 128), f32),
            pltpu.VMEM((NT, 128), f32),
            pltpu.VMEM((4, 2, NT, 128), f32),
            pltpu.VMEM((8, 128), f32),
            pltpu.VMEM((size, 8, 128), f32),
            pltpu.VMEM((128, 128), f32),
            pltpu.VMEM((OWN_X, OWN_Y, 128), f32),
            pltpu.VMEM((4, NT + 8, 128), f32),
            pltpu.VMEM((128, 128), f32),
            pltpu.VMEM((8, 128), f32),
            pltpu.VMEM((4, NT + 8, 128), f32),
            pltpu.VMEM((NT, 1024), f32),
            pltpu.VMEM((len(hit_slots()), 128, 256), bf16),
            pltpu.VMEM((4, 256, 128), bf16),
            pltpu.VMEM((OWN_X, OWN_Y + 16, 128), f32),
            pltpu.VMEM((OWN_X, OWN_Y, 128), f32),
            pltpu.VMEM((OWN_X, OWN_Y, 128), f32),
            dma((7, 3)),
            dma((7, 3)),
            dma((exchanges, 7)),
            dma((exchanges, 7)),
            dma((halves, 3)),
            dma((halves, 3)),
            dma((7,)),
            dma((7,)),
            dma((7,)),
            dma((7,)),
            dma((size,)),
            dma((size,)),
            dma((2,)),
            dma((2,)),
        ],
        compiler_params=pltpu.CompilerParams(
            collective_id=0, has_side_effects=True, vmem_limit_bytes=58 * 1024 * 1024
        ),
        name="inversion_window",
    )(
        rec_cell, velocity, state_now, state_prev, observed.T, rec_cell.reshape(1, count),
        rec_gather.reshape(1, count),
    )


def solution(mesh):
    shape = mesh.shape
    paired = (shape["inline"], shape["particle"]) == (2, 2) and shape["xline"] in (2, 4, 6, 8)
    return jax.shard_map(
        per_device_pair if paired else per_device,
        mesh=mesh,
        in_specs=(
            P("particle", "inline", "xline", None),
            P("particle", "inline", "xline", None),
            P("particle", "inline", "xline", None),
            P(("inline", "xline"), None),
            P(("inline", "xline")),
            P(("inline", "xline"), None),
        ),
        out_specs=P("particle", "inline", "xline", None),
        check_vma=False,
    )
```

```python
import jax
import jax.numpy as jnp
from jax import lax
from jax.experimental import pallas as pl
from jax.experimental.pallas import tpu as pltpu
from jax.sharding import PartitionSpec as P

NT = 32
CAP = 16
TAPS = 8


COEFFS = (8.0 / 5.0, -1.0 / 5.0, 8.0 / 315.0, -1.0 / 560.0)
CENTER = -205.0 / 72.0
KERNEL_WIDTH = 0.004
NOISE_VARIANCE = 0.0005
STEP_SIZE = 0.01
RIDGE_BASE = 1.0
RIDGE_SHARE = 0.1
HIGHEST = lax.Precision.HIGHEST


def extended(block, sides, width):
    for axis, dim in sides:
        count = lax.axis_size(axis)
        forward = [(i, i + 1) for i in range(count - 1)]
        backward = [(target, source) for source, target in forward]
        low = lax.ppermute(
            lax.slice_in_dim(block, block.shape[dim] - width, None, axis=dim), axis, forward
        )
        high = lax.ppermute(lax.slice_in_dim(block, 0, width, axis=dim), axis, backward)
        block = jnp.concatenate([low, block, high], axis=dim)
    return block


def laplace_inner(block):
    size_x, size_y, size_z = block.shape
    inner_x = size_x - 8
    inner_y = size_y - 8
    padded = jnp.pad(block, ((0, 0), (0, 0), (4, 4)))
    total = 3.0 * CENTER * block[4 : 4 + inner_x, 4 : 4 + inner_y, :]
    for shift in range(1, 5):
        weight = COEFFS[shift - 1]
        beside = padded[4 + shift : 4 + shift + inner_x, 4 : 4 + inner_y, 4 : 4 + size_z]
        beside = beside + padded[4 - shift : 4 - shift + inner_x, 4 : 4 + inner_y, 4 : 4 + size_z]
        beside = beside + padded[4 : 4 + inner_x, 4 + shift : 4 + shift + inner_y, 4 : 4 + size_z]
        beside = beside + padded[4 : 4 + inner_x, 4 - shift : 4 - shift + inner_y, 4 : 4 + size_z]
        beside = beside + padded[4 : 4 + inner_x, 4 : 4 + inner_y, 4 + shift : 4 + shift + size_z]
        beside = beside + padded[4 : 4 + inner_x, 4 : 4 + inner_y, 4 - shift : 4 - shift + size_z]
        total = total + weight * beside
    return total


def lagged_traces(traces):
    steps = traces.shape[1]
    padded = jnp.pad(traces, ((0, 0), (TAPS - 1, 0)))
    return jnp.stack(
        [padded[:, TAPS - 1 - shift : TAPS - 1 - shift + steps] for shift in range(TAPS)], axis=1
    )


def filter_stats(lagged, observed):
    count = lagged.shape[0]
    gram = jnp.einsum("mkt,mlt->mkl", lagged, lagged, precision=HIGHEST).reshape(count, TAPS * TAPS)
    cross = jnp.einsum("mkt,mt->mk", lagged, observed, precision=HIGHEST)
    return (gram, cross)


def solve_filter(gram, cross):
    matrix = gram.reshape(-1, TAPS, TAPS)
    sums = [matrix[:, k, l] for k in range(TAPS) for l in range(k + 1)]
    sums = jnp.stack(sums + [cross[:, k] for k in range(TAPS)])
    return jnp.concatenate(solve_rows(sums), axis=0).T


def adjoint_sources(lagged, observed, filters):
    steps = observed.shape[1]
    fitted = jnp.einsum("mk,mkt->mt", filters, lagged, precision=HIGHEST)
    misfit = fitted - observed
    padded = jnp.pad(misfit, ((0, 0), (0, TAPS - 1)))
    ahead = jnp.stack([padded[:, shift : shift + steps] for shift in range(TAPS)], axis=1)
    return jnp.einsum("mk,mkt->mt", filters, ahead, precision=HIGHEST)


def per_device(velocity, state_now, state_prev, observed, rec_cell, rec_gather):
    courant = velocity[0]
    particles = lax.axis_size("particle")
    models = lax.all_gather(velocity, "particle", axis=0, tiled=True)
    partial_sums = jnp.sum(jnp.square(models - velocity), axis=(1, 2, 3))
    cells_all = courant.size * lax.axis_size("inline") * lax.axis_size("xline")
    distance = lax.psum(partial_sums, ("inline", "xline")) / cells_all
    kernel = jnp.exp(-distance / KERNEL_WIDTH)

    def advance(carry, unused):
        current, previous = carry
        padded = extended(current[None], (("inline", 1), ("xline", 2)), 4)[0]
        laplacian = laplace_inner(padded)
        following = 2.0 * current - previous + courant * laplacian
        return ((following, current), (laplacian, following.reshape(-1)[rec_cell]))

    unused, (laplacians, traces) = lax.scan(advance, (state_now[0], state_prev[0]), None, length=NT)
    synthetic = traces.T
    steps = observed.shape[1]
    xline_count = lax.axis_size("xline")
    target = rec_gather[:, 0]
    choose = (target[:, None] == jnp.arange(xline_count, dtype=jnp.int32)[None, :]).astype(
        jnp.int32
    )
    order = jnp.arange(target.shape[0], dtype=jnp.int32)
    earlier = (order[None, :] < order[:, None]).astype(jnp.float32)
    before = jnp.dot(earlier, choose.astype(jnp.float32), precision=HIGHEST).astype(jnp.int32)
    position = target * CAP + jnp.sum(before * choose, axis=1)
    outgoing = jnp.zeros((xline_count * CAP, 2 * steps), jnp.float32)
    outgoing = outgoing.at[position].set(jnp.concatenate([synthetic, observed], axis=1))
    arrived = lax.all_to_all(
        outgoing.reshape(xline_count, CAP, 2 * steps),
        "xline",
        split_axis=0,
        concat_axis=0,
        tiled=True,
    )
    slots = arrived.reshape(xline_count * CAP, 2 * steps)
    slot_lagged = lagged_traces(slots[:, :steps])
    slot_observed = slots[:, steps:]
    gram, cross = filter_stats(slot_lagged, slot_observed)
    filters_one = solve_filter(
        jnp.sum(gram, axis=0, keepdims=True), jnp.sum(cross, axis=0, keepdims=True)
    )
    filters = jnp.broadcast_to(filters_one, (slots.shape[0], TAPS))
    slot_adjoint = adjoint_sources(slot_lagged, slot_observed, filters)
    returned = lax.all_to_all(
        slot_adjoint.reshape(xline_count, CAP, steps),
        "xline",
        split_axis=0,
        concat_axis=0,
        tiled=True,
    )
    adjoint_source = returned.reshape(xline_count * CAP, steps)[position]

    def backward(carry, inputs):
        wave, wave_old, gradient = carry
        laplacian, source = inputs
        padded = extended(wave[None], (("inline", 1), ("xline", 2)), 4)[0]
        wave_new = 2.0 * wave - wave_old + courant * laplace_inner(padded)
        wave_new = wave_new.reshape(-1).at[rec_cell].add(source).reshape(wave.shape)
        return ((wave_new, wave, gradient + wave_new * laplacian), None)

    zeros_field = jnp.zeros(courant.shape, jnp.float32)
    (wave, wave_old, gradient), unused = lax.scan(
        backward,
        (zeros_field, zeros_field, zeros_field),
        (laplacians, adjoint_source.T),
        reverse=True,
    )
    gradient = gradient / NT
    gradients = lax.all_gather(gradient[None], "particle", axis=0, tiled=True)
    terms = -gradients / NOISE_VARIANCE + 2.0 * (velocity - models) / KERNEL_WIDTH
    update = (
        STEP_SIZE / particles * jnp.sum(kernel[:, None, None, None] * terms, axis=0, keepdims=True)
    )
    return update


STEPS = 8
HALF = 4
Z_HALO = 4 * STEPS
CORE_HALO = 4 * HALF
OWN_X = 8
OWN_Y = Z_HALO - 8
OWN_END = Z_HALO + OWN_Y
ROWS = OWN_END + CORE_HALO
KEYS = 8
INTEGER_COEFFS = (8064.0, -1008.0, 128.0, -9.0)
INTEGER_SCALE = 1.0 / 5040.0
LEVELS = ((0, 1, 2), (2, 0, 3), (3, 2, 1), (1, 3, 0))
MESH = pl.DeviceIdType.MESH
SECOND, NEAR, OWN, CORE = range(4)
SPANS = ((0, 8), (8, Z_HALO), (Z_HALO, OWN_END), (OWN_END, ROWS))


def split_two(value):
    high = value.astype(jnp.bfloat16)
    rest = (value - high.astype(jnp.float32)).astype(jnp.bfloat16)
    return high, rest


def band_matrix():
    row = lax.broadcasted_iota(jnp.int32, (256, 128), 0) % 128
    col = lax.broadcasted_iota(jnp.int32, (256, 128), 1)
    away = jnp.abs(row - col)
    band = jnp.zeros((256, 128), jnp.float32)
    for shift in range(1, 5):
        band = jnp.where(away == shift, INTEGER_COEFFS[shift - 1], band)
    return band.astype(jnp.bfloat16)


def laplace_tile(wave, first, band):
    center = wave[:, pl.ds(first, 8), :]
    layers = center.shape[0]
    line = [center[i] for i in range(layers)]
    high, rest = split_two(center.reshape(layers * 8, 128))
    depth = jnp.dot(
        jnp.concatenate([high, rest], axis=1), band, preferred_element_type=jnp.float32
    ).reshape(layers, 8, 128)
    parts = [3.0 * CENTER / INTEGER_SCALE * line[i] + depth[i] for i in range(layers)]
    for shift in range(1, 5):
        beside = wave[:, pl.ds(first + shift, 8), :] + wave[:, pl.ds(first - shift, 8), :]
        for i in range(layers):
            sums = beside[i]
            if i + shift < layers:
                sums = sums + line[i + shift]
            if i >= shift:
                sums = sums + line[i - shift]
            parts[i] = parts[i] + INTEGER_COEFFS[shift - 1] * sums
    return center, jnp.stack(parts, axis=0)


def own_half(value, inline):
    return jnp.where(inline == 0, value[:OWN_X], value[OWN_X:])


def solve_rows(sums):
    entry = {}
    index = 0
    for k in range(TAPS):
        for l in range(k + 1):
            entry[k, l] = sums[index : index + 1]
            index += 1
    right = [sums[index + k : index + k + 1] for k in range(TAPS)]
    trace_sum = sum(entry[k, k] for k in range(TAPS))
    ridge = RIDGE_BASE + RIDGE_SHARE * trace_sum / TAPS
    for k in range(TAPS):
        entry[k, k] = entry[k, k] + ridge
    inverse = []
    for k in range(TAPS):
        inverse.append(1.0 / entry[k, k])
        factor = {i: entry[i, k] * inverse[k] for i in range(k + 1, TAPS)}
        for i in range(k + 1, TAPS):
            for l in range(k + 1, i + 1):
                entry[i, l] = entry[i, l] - factor[i] * entry[l, k]
            right[i] = right[i] - factor[i] * right[k]
        for i in range(k + 1, TAPS):
            entry[i, k] = factor[i]
    right = [right[k] * inverse[k] for k in range(TAPS)]
    for k in reversed(range(TAPS)):
        for i in range(k):
            right[i] = right[i] - entry[k, i] * right[k]
    return right


def tiles_of(step):
    first = 4 * (step + 1)
    return range(first, OWN_END + 4 * (HALF - 1 - step % HALF), 8)


def plan():
    first_half = [(s, f) for s in range(HALF) for f in tiles_of(s)]
    later = [(s, f) for s in range(HALF, STEPS) for f in tiles_of(s)]
    order, done = [], set()

    def ready(step, first, pieces, core, core_later):
        if Z_HALO - (first - 4 * (step + 1)) > 8 * pieces:
            return False
        reach = first + 8 + 4 * (step % HALF + 1)
        if reach > OWN_END and not (core if step < HALF else core_later):
            return False
        if step == 0:
            return True
        if step >= HALF and any(
            f + 8 > Z_HALO and f < OWN_END and (step - HALF, f) not in done
            for f in tiles_of(step - HALF)
        ):
            return False
        span = range(first - 4, first + 12)
        covered = {r for s, f in done if s == step - 1 for r in range(f, f + 8)}
        if step == HALF:
            return all(r in covered for r in span if r < OWN_END)
        return all(r in covered for r in span)

    def take(tiles, pieces, core, core_later):
        changed = True
        while changed:
            changed = False
            for step, first in tiles:
                if (step, first) not in done and ready(step, first, pieces, core, core_later):
                    done.add((step, first))
                    order.append(("tile", step, first))
                    changed = True

    both = first_half + later
    take(both, 0, False, False)
    order.append(("core", 0))
    take(both, 0, True, False)
    order.append(("piece", 0))
    take(first_half, 1, True, False)
    order.append(("middle",))
    take(both, 1, True, False)
    order.append(("piece", 1))
    take(both, 2, True, False)
    order.append(("core", 1))
    take(both, 2, True, True)
    order.append(("early", 0))
    order.append(("piece", 2))
    order.append(("piece", 3))
    left = [tile for tile in both if tile not in done]
    for step, first in sorted(left, key=lambda t: t[0] + 1.5 * (t[1] == 4 * (t[0] + 1)))[:-1]:
        assert ready(step, first, 4, True, True)
        done.add((step, first))
        order.append(("tile", step, first))
    take(both, 4, True, True)
    order.append(("early", 1))
    assert len(done) == len(both)
    return order


def columns_of(first):
    return [c for c, (start, stop) in enumerate(SPANS) if first < stop and first + 8 > start]


def hit_slots():
    slots = {}
    for step in range(STEPS):
        for first in tiles_of(step):
            for column in columns_of(first):
                slots.setdefault((first, column), len(slots))
    return slots


def flip(block, index):
    return jnp.stack(
        [jnp.take_along_axis(block[i], index, axis=0) for i in range(block.shape[0])], axis=0
    )


def whole_kernel(
    rec_cell, velocity, state_now, state_prev, observed, cells, gathers, update,
    rec_layer, rec_row, fields, seen, cell_row, gather_row, notes, depth_mask, local_sem, courant, wave, staged, staged_core, z_land, core_land, x_first, near_first, core_first,
    second_first, laplacians, picked, notes_all, traces, traces_all, sums_own, sums_all, turned,
    model, synthetic, products, filters, misfit, strengths, hits, places, gradient, gradient_own,
    gradient_other, start_send, start_recv, z_send, z_recv, core_send, core_recv, note_send,
    note_recv, trace_send, trace_recv, sum_send, sum_recv, pair_send, pair_recv,
):
    inline, xline, particle = (lax.axis_index(a) for a in ("inline", "xline", "particle"))
    count = lax.axis_size("xline")
    size = 2 * count
    me = inline * count + xline
    receivers = rec_cell.shape[0]
    odd = lax.rem(xline, 2)
    toward = 1 - 2 * odd
    other = 1 - inline
    near, core = xline - toward, xline + toward
    second_in, second_out = xline - 2 * toward, xline + 2 * toward
    has_near = (near >= 0) & (near < count)
    has_in = (second_in >= 0) & (second_in < count)
    has_out = (second_out >= 0) & (second_out < count)
    always = xline >= 0
    sources = [fields.at[pl.ds(kind, 1)] for kind in range(3)]
    frames = (wave.at[0], wave.at[1], courant)
    sublane = lax.broadcasted_iota(jnp.int32, (8, 128), 0)
    backward_rows = 7 - sublane
    own_rows = jnp.where(odd == 1, 7 - sublane, sublane)

    inputs = [
        pltpu.make_async_copy(source, target, local_sem.at[i])
        for i, (source, target) in enumerate(
            [
                (observed, seen),
                (cells, cell_row),
                (gathers, gather_row),
                (state_now.at[0], fields.at[0]),
                (state_prev.at[0], fields.at[1]),
                (velocity.at[0], fields.at[2]),
            ]
        )
    ]
    for copy in inputs:
        copy.start()
    barrier = pltpu.get_barrier_semaphore()

    def greet(step, carry):
        peer = lax.rem(me + step, size)
        pl.semaphore_signal(
            barrier, inc=1, device_id=(peer // count, lax.rem(peer, count), particle),
            device_id_type=MESH,
        )
        return carry

    lax.fori_loop(1, size, greet, 0)
    pl.semaphore_signal(
        barrier, inc=1, device_id=(inline, xline, 1 - particle), device_id_type=MESH
    )

    for r in range(receivers):
        line = rec_cell[r] >> 7
        layer = (line * 2731) >> 16
        row = line - layer * OWN_Y
        rec_layer[r] = layer
        rec_row[r] = Z_HALO + row + odd * (OWN_Y - 1 - 2 * row)
    for copy in inputs:
        copy.wait()
    pl.semaphore_wait(barrier, size)

    routes = [
        (always, always, (other, xline, particle), OWN),
        (always, always, (inline, core, particle), CORE),
        (always, always, (other, core, particle), CORE),
        (has_near, has_near, (inline, near, particle), NEAR),
        (has_near, has_near, (other, near, particle), NEAR),
        (has_out, has_in, (inline, second_out, particle), SECOND),
        (has_out, has_in, (other, second_out, particle), SECOND),
    ]
    origins = (other, inline, other, inline, other, inline, other)

    def remote(source, target, send, recv, device):
        return pltpu.make_async_remote_copy(
            src_ref=source, dst_ref=target, send_sem=send, recv_sem=recv, device_id=device,
            device_id_type=MESH,
        )

    def start_copy(index, kind, arriving=False):
        column = routes[index][3]
        passed_on = index in (2, 4, 6)
        origin = other if passed_on or (arriving and index == 0) else inline
        if column == OWN:
            first, extent, landing = 0, OWN_Y, x_first.at[kind]
        elif column == NEAR:
            first, extent, landing = 0, OWN_Y, near_first.at[kind, origin]
        elif column == CORE:
            first, extent, landing = 8 * (1 - odd), CORE_HALO, core_first.at[kind, origin]
        else:
            first, extent, landing = 16 * (1 - odd), 8, second_first.at[kind, origin]
        rows = pl.ds(first if isinstance(first, int) else pl.multiple_of(first, 8), extent)
        source = x_first.at[kind, :, rows, :] if passed_on else sources[kind].at[0, :, rows, :]
        target = routes[index - 1 if passed_on else index][2]
        return remote(
            source, landing, start_send.at[index, kind], start_recv.at[index, kind], target
        )

    def start_all(index, kind):
        @pl.when(routes[index][0])
        def _():
            start_copy(index, kind).start()

    def finish_first(indices):
        for index in indices:
            for kind in range(3):

                @pl.when(routes[index][0])
                def _():
                    start_copy(index, kind).wait_send()

                @pl.when(routes[index][1])
                def _():
                    start_copy(index, kind, True).wait_recv()

    for index in (0, 3, 1, 5):
        for kind in range(3):
            start_all(index, kind)

    def pair_copy(source, target, index):
        return remote(
            source, target, pair_send.at[index], pair_recv.at[index], (inline, xline, 1 - particle)
        )

    pair_copy(fields.at[2], model, 0).start()

    def share(source, table, send, recv, origin, index):
        return remote(
            source, table.at[routes[index][3], origin], send.at[index], recv.at[index],
            routes[index][2],
        )

    def share_start(source, table, send, recv):
        for index in range(7):

            @pl.when(routes[index][0])
            def _():
                share(source, table, send, recv, inline, index).start()

    def share_wait(source, table, send, recv):
        for index in range(7):

            @pl.when(routes[index][0])
            def _():
                share(source, table, send, recv, inline, index).wait_send()

            @pl.when(routes[index][1])
            def _():
                share(source, table, send, recv, origins[index], index).wait_recv()

    layers = pl.ds(inline * OWN_X, OWN_X)
    layers_other = pl.ds(other * OWN_X, OWN_X)

    def own_block(index):
        return pl.multiple_of(8 * (index + odd * (2 - 2 * index)), 8)

    for kind in range(3):
        for index in range(3):
            scale = INTEGER_SCALE if kind == 2 else 1.0
            frames[kind][layers, pl.ds(Z_HALO + 8 * index, 8), :] = scale * flip(
                fields[kind, :, pl.ds(own_block(index), 8), :], own_rows
            )

    @pl.when(jnp.logical_not(has_near))
    def _():
        for frame in frames:
            frame[:, pl.ds(8, Z_HALO - 8), :] = jnp.zeros((2 * OWN_X, Z_HALO - 8, 128), jnp.float32)
        notes_all[NEAR] = jnp.zeros(notes_all.shape[1:], jnp.float32)
        traces_all[NEAR] = jnp.zeros(traces_all.shape[1:], jnp.float32)

    @pl.when(jnp.logical_not(has_in))
    def _():
        for frame in frames:
            frame[:, pl.ds(0, 8), :] = jnp.zeros((2 * OWN_X, 8, 128), jnp.float32)
        notes_all[SECOND] = jnp.zeros(notes_all.shape[1:], jnp.float32)
        traces_all[SECOND] = jnp.zeros(traces_all.shape[1:], jnp.float32)

    lane = lax.broadcasted_iota(jnp.int32, (8, 128), 1)
    here = (lane // receivers) == inline
    cell = jnp.concatenate([cell_row[...], cell_row[...]], axis=1)
    gather = jnp.concatenate([gather_row[...], gather_row[...]], axis=1)
    line = cell >> 7
    layer = (line * 2731) >> 16
    row = line - layer * OWN_Y
    facts = [
        (inline * OWN_X + layer) * ROWS,
        row + odd * (OWN_Y - 1 - 2 * row),
        cell & 127,
        inline * KEYS + gather,
    ]
    for block in range(0, NT, 8):
        part = seen[pl.ds(block, 8), :]
        notes[pl.ds(block, 8), :] = jnp.where(here, jnp.concatenate([part, part], axis=1), 0.0)
    notes[pl.ds(NT, 8), :] = jnp.zeros((8, 128), jnp.float32)
    for i, fact in enumerate(facts):
        notes[pl.ds(NT + i, 1), :] = jnp.where(here[0:1], fact.astype(jnp.float32), 0.0)
    keys = lax.broadcasted_iota(jnp.int32, (128, 128), 0)
    depth_mask[...] = jnp.transpose((keys == (cell & 127)).astype(jnp.float32))
    notes_all[OWN, inline] = notes[...]
    picked[:, pl.ds(other * receivers, receivers), :] = jnp.zeros(
        (NT, receivers, 128), jnp.float32
    )
    first_layers = (pl.ds(0, OWN_X), pl.ds(OWN_X, OWN_X))

    def first_core():
        finish_first((1, 2))
        for kind in range(3):
            scale = INTEGER_SCALE if kind == 2 else 1.0
            for half in range(2):
                for block in range(2):
                    at = pl.multiple_of(8 * (block + odd * (1 - 2 * block)), 8)
                    frames[kind][first_layers[half], pl.ds(OWN_END + 8 * block, 8), :] = scale * flip(
                        core_first[kind, half, :, pl.ds(at, 8), :], own_rows
                    )

    def first_piece(piece):
        if piece == 0:
            finish_first((3, 4))
        if piece == 3:
            finish_first((5, 6))

        @pl.when(has_in if piece == 3 else has_near)
        def _():
            for kind in range(3):
                scale = INTEGER_SCALE if kind == 2 else 1.0
                for half in range(2):
                    if piece == 3:
                        block = second_first[kind, half]
                    else:
                        block = near_first[kind, half, :, pl.ds(own_block(2 - piece), 8), :]
                    frames[kind][first_layers[half], pl.ds(24 - 8 * piece, 8), :] = scale * flip(
                        block, own_rows
                    )

    for kind in range(3):
        start_copy(0, kind).wait_send()
        start_copy(0, kind, True).wait_recv()
        for index in (4, 2, 6):
            start_all(index, kind)
    for kind in range(3):
        for block in range(3):
            scale = INTEGER_SCALE if kind == 2 else 1.0
            frames[kind][layers_other, pl.ds(Z_HALO + 8 * block, 8), :] = scale * flip(
                x_first[kind, :, pl.ds(own_block(block), 8), :], own_rows
            )
    share_start(notes, notes_all, note_send, note_recv)

    band = band_matrix()
    ones = jnp.ones((8, 256), jnp.bfloat16)
    ordered = plan()

    def z_copies(slot):
        to_near, to_second = (inline, near, particle), (inline, second_out, particle)
        blocks = [
            (wave.at[0, :, pl.ds(Z_HALO, 8), :], 0, to_near),
            (staged.at[0], 1, to_near),
            (staged.at[2], 2, to_near),
            (staged.at[1], 3, to_near),
            (staged.at[3], 4, to_near),
            (staged.at[1], 5, to_second),
            (staged.at[4], 6, to_near),
        ]
        return [
            remote(source, z_land.at[slot, i], z_send.at[slot, i], z_recv.at[slot, i], target)
            for source, i, target in blocks
        ]

    def core_copies(slot, blocks):
        return [
            remote(
                block, core_land.at[slot, i], core_send.at[slot, i], core_recv.at[slot, i],
                (inline, core, particle),
            )
            for i, block in enumerate(blocks)
        ]

    z_valid = [has_near] * 5 + [has_out, has_near]
    z_arrives = [has_near] * 5 + [has_in, has_near]
    z_place = [(0, 24), (0, 16), (1, 20), (0, 8), (1, 12), (0, 0), (1, 4)]
    pieces = ((0,), (1, 2), (3, 4), (5, 6))
    sent = ((0,), (1, 2, 3, 4, 5, 6), (), ())
    core_place = [(0, OWN_END), (0, OWN_END + 8), (1, OWN_END + 4)]

    def start_blocks(slot, blocks):
        copies = z_copies(slot)
        for i in blocks:
            pl.when(z_valid[i])(copies[i].start)

    def send_early(slot, part):
        if part == 0:
            staged[1] = wave[0, :, pl.ds(48, 8), :]
            staged[3] = wave[1, :, pl.ds(44, 8), :]
            staged[4] = wave[1, :, pl.ds(52, 8), :]
            start_blocks(slot, (5, 6))
        else:
            start_blocks(slot, (0,))
            staged[0] = wave[0, :, pl.ds(40, 8), :]
            staged[2] = wave[1, :, pl.ds(36, 8), :]
            start_blocks(slot, (1, 2))
            for copy in core_copies(slot, round_blocks):
                copy.start()

    def send_round(slot):
        start_blocks(slot, (3, 4))

    round_blocks = [staged.at[1], staged.at[0], staged.at[3]]
    middle_blocks = [staged_core.at[i] for i in range(3)]

    def send_middle(slot):
        staged_core[0] = wave[0, :, pl.ds(48, 8), :]
        staged_core[1] = wave[0, :, pl.ds(40, 8), :]
        staged_core[2] = wave[1, :, pl.ds(44, 8), :]
        for copy in core_copies(slot, middle_blocks):
            copy.start()

    def take_core(slot, blocks):
        for i, copy in enumerate(core_copies(slot, blocks)):
            copy.wait()
            level, row = core_place[i]
            wave[level, :, pl.ds(row, 8), :] = flip(core_land[slot, i], backward_rows)

    def take_piece(slot, piece):
        copies = z_copies(slot)
        for i in sent[piece]:
            pl.when(z_valid[i])(copies[i].wait_send)
        for i in pieces[piece]:

            @pl.when(z_arrives[i])
            def _():
                copies[i].wait_recv()
                level, row = z_place[i]
                block = z_land[slot, i]
                if i != 5:
                    block = flip(block, backward_rows)
                wave[level, :, pl.ds(row, 8), :] = block

    rounds = NT // STEPS

    def run_round(number, sweep, tile):
        taken = sweep * (rounds - 1) + number - 1
        middle = 2 * (rounds - 1) + sweep * rounds + number
        for entry in ordered:
            if entry[0] == "tile":
                tile(entry[1], entry[2])
            elif entry[0] == "middle":
                send_middle(middle)
            elif entry[0] == "early":

                @pl.when(number < rounds - 1)
                def _():
                    send_early(taken + 1, entry[1])
            elif entry[0] == "piece":

                @pl.when(number > 0)
                def _():
                    take_piece(taken, entry[1])

                if sweep == 0:

                    @pl.when(number == 0)
                    def _():
                        first_piece(entry[1])
            elif entry[1] == 0:

                @pl.when(number > 0)
                def _():
                    take_core(taken, round_blocks)

                if sweep == 0:
                    pl.when(number == 0)(first_core)
            else:
                take_core(middle, middle_blocks)

        @pl.when(number < rounds - 1)
        def _():
            send_round(taken + 1)

    def keep_lines(time, level):
        new = wave.at[level]
        for group in range(0, receivers, 16):
            lines = [
                new[inline * OWN_X + rec_layer[r], pl.ds(rec_row[r], 1), :]
                for r in range(group, group + 16)
            ]
            for offset, line in enumerate(lines):
                picked[time, pl.ds(inline * receivers + group + offset, 1), :] = line

    def read_traces(first_time, steps):
        for step in range(steps):
            time = first_time + step
            high, rest = split_two(picked[time] * depth_mask[...])
            row = lax.dot_general(
                ones, jnp.concatenate([high, rest], axis=1), (((1,), (1,)), ((), ())),
                preferred_element_type=jnp.float32,
            )
            traces[pl.ds(time, 1), :] = row[0:1]

    own_tiles = {s: {f for f in tiles_of(s) if f + 8 > Z_HALO and f < OWN_END} for s in range(STEPS)}

    def forward_round(number, carry):
        left = [set(own_tiles[s]) for s in range(STEPS)]

        @pl.when(number > 0)
        def _():
            for step in range(HALF, STEPS):
                keep_lines((number - 1) * STEPS + step, LEVELS[step % 4][2])
            read_traces((number - 1) * STEPS + HALF, HALF)

        def tile(step, first):
            now, old, new = (wave.at[level] for level in LEVELS[step % 4])
            time = number * STEPS + step
            center, laplacian = laplace_tile(now, first, band)
            here = pl.ds(first, 8)
            new[:, here, :] = 2.0 * center - old[:, here, :] + courant[:, here, :] * laplacian
            if first in own_tiles[step]:
                laplacians[time, :, pl.ds(first - Z_HALO + 8, 8), :] = own_half(laplacian, inline)
                left[step].discard(first)
                if step < HALF and not left[step]:
                    keep_lines(time, LEVELS[step % 4][2])

        run_round(number, 0, tile)
        read_traces(number * STEPS, HALF)
        return carry

    lax.fori_loop(0, rounds, forward_round, 0)
    for step in range(HALF, STEPS):
        keep_lines(NT - STEPS + step, LEVELS[step % 4][2])
    read_traces(NT - HALF, HALF)
    traces_all[OWN, inline] = traces[...]
    share_start(traces, traces_all, trace_send, trace_recv)

    synthetic[...] = jnp.zeros(synthetic.shape, jnp.float32)
    products[...] = jnp.zeros(products.shape, jnp.float32)
    synthetic[OWN, pl.ds(8, NT), :] = traces[pl.ds(0, NT), :]
    lagged = [synthetic[OWN, pl.ds(8 - k, NT), :] for k in range(TAPS)]
    recorded = notes[pl.ds(0, NT), :]
    index = 0
    for k in range(TAPS):
        for l in range(k + 1):
            products[pl.ds(index, 1), :] = jnp.sum(lagged[k] * lagged[l], axis=0, keepdims=True)
            index += 1
    for k in range(TAPS):
        products[pl.ds(index + k, 1), :] = jnp.sum(lagged[k] * recorded, axis=0, keepdims=True)
    own_key = notes[pl.ds(NT + 3, 1), :].astype(jnp.int32) - inline * KEYS
    local = (keys[:KEYS] == own_key).astype(jnp.float32)
    partial = lax.dot_general(
        local, products[...], (((1,), (1,)), ((), ())),
        preferred_element_type=jnp.float32, precision=HIGHEST,
    )
    pair_copy(fields.at[2], model, 0).wait()
    apart = jnp.sum(jnp.square(fields[2] - model[...]), axis=0)
    apart = apart[0:8] + apart[8:16] + apart[16:24]
    partial = jnp.where(lane == 127, jnp.sum(apart, axis=1, keepdims=True), partial)
    sums_own[...] = partial
    sums_all[me] = partial

    def sum_copy(step, peer):
        sender = lax.rem(me + size - step, size)
        return remote(
            sums_own, sums_all.at[me if peer else sender], sum_send.at[step], sum_recv.at[step],
            (
                lax.rem(me + step, size) // count if peer else sender // count,
                lax.rem(me + step if peer else sender, count),
                particle,
            ),
        )

    def sum_start(step, carry):
        sum_copy(step, True).start()
        return carry

    lax.fori_loop(1, size, sum_start, 0)

    share_wait(notes, notes_all, note_send, note_recv)
    for column in range(4):
        pair = notes_all[column, 0] + notes_all[column, 1]
        place_row = pair[NT + 1 : NT + 2].astype(jnp.int32)
        frame_row = (place_row - 16, 31 - place_row, Z_HALO + place_row, OWN_END + 23 - place_row)[
            column
        ]
        depth = pair[NT + 2 : NT + 3].astype(jnp.int32)
        fits = (frame_row >= 0) & (frame_row < ROWS)
        row_id = jnp.where(fits, pair[NT : NT + 1].astype(jnp.int32) + frame_row, -1)
        place = jnp.transpose((keys == depth).astype(jnp.float32)).astype(jnp.bfloat16)
        places[column, pl.ds(0, 128), :] = place
        places[column, pl.ds(128, 128), :] = place
        for (first, found), slot in hit_slots().items():
            if found == column:
                wanted = (keys // 8) * ROWS + first + lax.rem(keys, 8)
                hit = (wanted == row_id).astype(jnp.float32).astype(jnp.bfloat16)
                hits[slot, :, pl.ds(0, 128)] = hit
                hits[slot, :, pl.ds(128, 128)] = hit
    wave[...] = jnp.zeros(wave.shape, jnp.float32)
    gradient[...] = jnp.zeros(gradient.shape, jnp.float32)
    misfit[...] = jnp.zeros(misfit.shape, jnp.float32)
    turned[...] = jnp.zeros(turned.shape, jnp.float32)

    def sum_wait(step, carry):
        sum_copy(step, True).wait_send()
        sum_copy(step, False).wait_recv()
        return carry

    lax.fori_loop(1, size, sum_wait, 0)
    total = [jnp.zeros((8, 128), jnp.float32) for i in range(2)]
    for row in range(2):
        for column in range(count):
            total[row] = total[row] + sums_all[row * count + column]
        turned[pl.ds(KEYS * row, KEYS), :] = total[row]
    sums = jnp.transpose(turned[...])
    for k, row in enumerate(solve_rows(sums[:48])):
        filters[pl.ds(k, 1), :] = row

    share_wait(traces, traces_all, trace_send, trace_recv)
    for column in range(4):
        both = traces_all[column, 0] + traces_all[column, 1]
        synthetic[column, pl.ds(8, NT), :] = both[:NT]
        pair = notes_all[column, 0] + notes_all[column, 1]
        members = (keys == pair[NT + 3 : NT + 4].astype(jnp.int32)).astype(jnp.float32)
        own = jnp.dot(
            filters[...], members, preferred_element_type=jnp.float32, precision=HIGHEST
        )
        fitted = sum(own[k : k + 1] * synthetic[column, pl.ds(8 - k, NT), :] for k in range(TAPS))
        misfit[column, pl.ds(0, NT), :] = fitted - pair[:NT]
        source = sum(own[k : k + 1] * misfit[column, pl.ds(k, NT), :] for k in range(TAPS))
        high, rest = split_two(source)
        strengths[:, pl.ds(256 * column, 128)] = high.astype(jnp.float32)
        strengths[:, pl.ds(256 * column + 128, 128)] = rest.astype(jnp.float32)

    slots = hit_slots()

    def backward_round(number, carry):
        def tile(step, first):
            now, old, new = (wave.at[level] for level in LEVELS[step % 4])
            time = NT - 1 - (number * STEPS + step)
            strength = strengths[pl.ds(time, 1), :].astype(jnp.bfloat16)
            center, laplacian = laplace_tile(now, first, band)
            here = pl.ds(first, 8)
            added = 0.0
            for column in columns_of(first):
                part = slice(256 * column, 256 * (column + 1))
                added = added + jnp.dot(
                    hits[slots[first, column]] * strength[:, part],
                    places[column],
                    preferred_element_type=jnp.float32,
                )
            following = 2.0 * center - old[:, here, :] + courant[:, here, :] * laplacian
            following = following + added.reshape(2 * OWN_X, 8, 128)
            new[:, here, :] = following
            if first in own_tiles[step]:
                kept = pl.ds(first - Z_HALO + 8, 8)
                gradient[:, kept, :] = (
                    gradient[:, kept, :]
                    + own_half(following, inline) * laplacians[time, :, kept, :]
                )

        run_round(number, 1, tile)
        return carry

    lax.fori_loop(0, rounds, backward_round, 0)
    for index in range(3):
        gradient_own[:, pl.ds(own_block(index), 8), :] = flip(
            gradient[:, pl.ds(8 + 8 * index, 8), :] * (INTEGER_SCALE / NT), own_rows
        )
    pair_copy(gradient_own, gradient_other, 1).start()
    apart = jnp.where(lane == 127, total[0] + total[1], 0.0)
    apart = jnp.sum(jnp.sum(apart, axis=0, keepdims=True), axis=1, keepdims=True)
    distance = apart / (size * OWN_X * OWN_Y * 128)
    weight = jnp.exp(jnp.broadcast_to(-distance / KERNEL_WIDTH, (8, 128)))[0:1]
    between = 2.0 * (fields[2] - model[...]) / KERNEL_WIDTH
    pair_copy(gradient_own, gradient_other, 1).wait()
    own_term = gradient_own[...] * (-1.0 / NOISE_VARIANCE)
    other_term = gradient_other[...] * (-1.0 / NOISE_VARIANCE) + between
    update[0] = (STEP_SIZE / 2) * (own_term + weight[None] * other_term)


def per_device_pair(velocity, state_now, state_prev, observed, rec_cell, rec_gather):
    count = rec_cell.shape[0]
    size = 2 * lax.axis_size("xline")
    vmem = pl.BlockSpec(memory_space=pltpu.VMEM)
    smem = pl.BlockSpec(memory_space=pltpu.SMEM)
    f32, bf16 = jnp.float32, jnp.bfloat16
    dma = pltpu.SemaphoreType.DMA
    exchanges = 2 * (NT // STEPS - 1)
    halves = exchanges + 2 * (NT // STEPS)
    return pl.pallas_call(
        whole_kernel,
        out_shape=jax.ShapeDtypeStruct(velocity.shape, f32),
        in_specs=[smem] + [pl.BlockSpec(memory_space=pltpu.HBM)] * 6,
        out_specs=vmem,
        scratch_shapes=[
            pltpu.SMEM((count,), jnp.int32),
            pltpu.SMEM((count,), jnp.int32),
            pltpu.VMEM((3, OWN_X, OWN_Y, 128), f32),
            pltpu.VMEM((NT, count), f32),
            pltpu.VMEM((1, count), jnp.int32),
            pltpu.VMEM((1, count), jnp.int32),
            pltpu.VMEM((NT + 8, 128), f32),
            pltpu.VMEM((128, 128), f32),
            dma((6,)),
            pltpu.VMEM((2 * OWN_X, ROWS, 128), f32),
            pltpu.VMEM((4, 2 * OWN_X, ROWS, 128), f32),
            pltpu.VMEM((5, 2 * OWN_X, 8, 128), f32),
            pltpu.VMEM((3, 2 * OWN_X, 8, 128), f32),
            pltpu.VMEM((exchanges, 7, 2 * OWN_X, 8, 128), f32),
            pltpu.VMEM((halves, 3, 2 * OWN_X, 8, 128), f32),
            pltpu.VMEM((3, OWN_X, OWN_Y, 128), f32),
            pltpu.VMEM((3, 2, OWN_X, OWN_Y, 128), f32),
            pltpu.VMEM((3, 2, OWN_X, CORE_HALO, 128), f32),
            pltpu.VMEM((3, 2, OWN_X, 8, 128), f32),
            pltpu.VMEM((NT, OWN_X, OWN_Y + 16, 128), f32),
            pltpu.VMEM((NT, 2 * count, 128), f32),
            pltpu.VMEM((4, 2, NT + 8, 128), f32),
            pltpu.VMEM((NT, 128), f32),
            pltpu.VMEM((4, 2, NT, 128), f32),
            pltpu.VMEM((8, 128), f32),
            pltpu.VMEM((size, 8, 128), f32),
            pltpu.VMEM((128, 128), f32),
            pltpu.VMEM((OWN_X, OWN_Y, 128), f32),
            pltpu.VMEM((4, NT + 8, 128), f32),
            pltpu.VMEM((128, 128), f32),
            pltpu.VMEM((8, 128), f32),
            pltpu.VMEM((4, NT + 8, 128), f32),
            pltpu.VMEM((NT, 1024), f32),
            pltpu.VMEM((len(hit_slots()), 128, 256), bf16),
            pltpu.VMEM((4, 256, 128), bf16),
            pltpu.VMEM((OWN_X, OWN_Y + 16, 128), f32),
            pltpu.VMEM((OWN_X, OWN_Y, 128), f32),
            pltpu.VMEM((OWN_X, OWN_Y, 128), f32),
            dma((7, 3)),
            dma((7, 3)),
            dma((exchanges, 7)),
            dma((exchanges, 7)),
            dma((halves, 3)),
            dma((halves, 3)),
            dma((7,)),
            dma((7,)),
            dma((7,)),
            dma((7,)),
            dma((size,)),
            dma((size,)),
            dma((2,)),
            dma((2,)),
        ],
        compiler_params=pltpu.CompilerParams(
            collective_id=0, has_side_effects=True, vmem_limit_bytes=58 * 1024 * 1024
        ),
        name="inversion_window",
    )(
        rec_cell, velocity, state_now, state_prev, observed.T, rec_cell.reshape(1, count),
        rec_gather.reshape(1, count),
    )


def solution(mesh):
    shape = mesh.shape
    paired = (shape["inline"], shape["particle"]) == (2, 2) and shape["xline"] in (2, 4, 6, 8)
    return jax.shard_map(
        per_device_pair if paired else per_device,
        mesh=mesh,
        in_specs=(
            P("particle", "inline", "xline", None),
            P("particle", "inline", "xline", None),
            P("particle", "inline", "xline", None),
            P(("inline", "xline"), None),
            P(("inline", "xline")),
            P(("inline", "xline"), None),
        ),
        out_specs=P("particle", "inline", "xline", None),
        check_vma=False,
    )
```
